128 devices in a mesh: row: 8 (over z, y_lo), col: 4 (over x), chan: 4 (over y_hi, core).
Axes of the slice: x: 4, y: 4 (y_hi: 2, y_lo: 2; y = y_hi * 2 + y_lo), z: 4, core: 2. Of those that a mesh axis runs over, the one named last changes fastest.
Arguments:
- image_gen: float32 [3, 2048, 4096], P(None, ('row', 'chan'), 'col'), may hold values from -3 to 3
- image_ref: float32 [3, 2048, 4096], P(None, ('row', 'chan'), 'col'), may hold values from -1 to 1
- kernel_one: bfloat16 [3, 3, 48, 64], replicated, may hold values from -0.3125 to 0.3125
- bias_one: float32 [64], replicated, may hold values from -1.5 to 1.5
- kernel_two: bfloat16 [5, 5, 64, 192], replicated, may hold values from -0.15625 to 0.15625
- bias_two: float32 [192], replicated, may hold values from -1.5 to 1.5
- kernel_three: bfloat16 [3, 3, 192, 384], P(None, None, None, 'chan'), may hold values from -0.15625 to 0.15625
- bias_three: float32 [384], replicated, may hold values from -1.5 to 1.5
- lin_first: float32 [64], replicated, may hold values from 0.1 to 1
- lin_second: float32 [192], replicated, may hold values from 0.1 to 1
- lin_third: float32 [384], replicated, may hold values from 0.1 to 1
Outputs:
- image_grad: float32 [3, 2048, 4096], P(None, ('row', 'chan'), 'col')
- loss: float32 [], replicated
The draws below stay inside these ranges and needn't reach their ends.
All inputs are finite; a program needn't handle non-finite values.
Results may differ from the reference program's by a relative error of at most 0.0086.
Values may be sent and summed in bfloat16 or wider, within the bound.
A program may use at most 128 MiB of HBM per device.

```python
import math
import jax
import jax.numpy as jnp
from jax import lax

CH1 = 64
CH2 = 192
CH3 = 384
HEIGHT = 2048
WIDTH = 4096


def frame_pair(key):
    base = jax.random.fold_in(key, 7101)
    first_key, second_key = jax.random.split(base)
    shape = (3, HEIGHT, WIDTH)
    reference_frame = jax.random.uniform(first_key, shape, jnp.float32, -1.0, 1.0)
    noise = jax.random.normal(second_key, shape, jnp.float32)
    lowest = 0.25
    highest = 0.75
    position = jnp.arange(HEIGHT).astype(jnp.float32) / HEIGHT
    amplitude = lowest + (highest - lowest) * position
    generated = jnp.clip(reference_frame + amplitude[None, :, None] * noise, -3.0, 3.0)
    return (generated, reference_frame)


def draw_image_gen(key, part):
    return frame_pair(key)[0]


def draw_image_ref(key, part):
    return frame_pair(key)[1]


def shard_levels(rng, shape, cuts, least, top_value):
    loudness = 1.0
    for dim, shards_of in cuts:
        heights = jax.random.uniform(jax.random.fold_in(jax.random.fold_in(rng, 6), dim), (shards_of,), jnp.float32, least / len(cuts), top_value / len(cuts))
        loudness = loudness * jnp.repeat(jnp.exp(heights), shape[dim] // shards_of).reshape((-1,) + (1,) * (len(shape) - 1 - dim))
    return loudness


def scatter_about(rng, extent, width, reach, cuts=(), kind=jnp.bfloat16):
    values = jax.random.normal(rng, extent, jnp.float32) * width
    if len(cuts) > 0:
        values = shard_levels(rng, extent, cuts, -0.22, 0.18) * values
    return jnp.clip(values, min=-reach, max=reach).astype(kind)


def setup_inputs(seed: int = 0) -> dict:
    streams_of = jax.random.split(jax.random.key(seed), 12)
    image_gen = draw_image_gen(jax.random.fold_in(streams_of[11], 71), 0)
    image_ref = draw_image_ref(jax.random.fold_in(streams_of[11], 71), 0)
    kernel_one = scatter_about(streams_of[2], (3, 3, 48, CH1), 432 ** -0.5, 0.3125)
    bias_one = scatter_about(streams_of[3], (CH1,), 0.3, 1.5, (), jnp.float32)
    kernel_two = scatter_about(streams_of[4], (5, 5, CH1, CH2), (25 * CH1) ** -0.5, 0.15625)
    bias_two = scatter_about(streams_of[5], (CH2,), 0.3, 1.5, (), jnp.float32)
    kernel_three = scatter_about(streams_of[6], (3, 3, CH2, CH3), (9 * CH2) ** -0.5, 0.15625, ((3, 4),))
    bias_three = scatter_about(streams_of[7], (CH3,), 0.3, 1.5, (), jnp.float32)
    lin_first = jnp.clip(jnp.exp(jax.random.uniform(streams_of[8], (CH1,), jnp.float32, math.log(0.1), math.log(1.0))), 0.1, 1.0)
    lin_second = jnp.clip(jnp.exp(jax.random.uniform(streams_of[9], (CH2,), jnp.float32, math.log(0.1), math.log(1.0))), 0.1, 1.0)
    lin_third = jnp.clip(jnp.exp(jax.random.uniform(streams_of[10], (CH3,), jnp.float32, math.log(0.1), math.log(1.0))), 0.1, 1.0)
    return {"image_gen": image_gen, "image_ref": image_ref, "kernel_one": kernel_one, "bias_one": bias_one, "kernel_two": kernel_two, "bias_two": bias_two, "kernel_three": kernel_three, "bias_three": bias_three, "lin_first": lin_first, "lin_second": lin_second, "lin_third": lin_third}


OFFSETS = (-0.03, -0.088, -0.188)
SPREADS = (0.458, 0.448, 0.45)
EPSILON = 1e-06

def normed_cells(image):
    offsets = jnp.array(OFFSETS, jnp.float32)[:, None, None]
    spreads = jnp.array(SPREADS, jnp.float32)[:, None, None]
    scaled = ((image - offsets) / spreads).astype(jnp.bfloat16)
    planes, height, columns = image.shape
    blocks = scaled.reshape(planes, height // 4, 4, columns // 4, 4)
    return blocks.transpose(0, 2, 4, 1, 3).reshape(planes * 16, height // 4, columns // 4)

def from_cells(values):
    planes, height, columns = values.shape
    blocks = values.reshape(planes // 16, 4, 4, height, columns)
    return blocks.transpose(0, 3, 1, 4, 2).reshape(planes // 16, height * 4, columns * 4)

def conv_valid(padded, kernel):
    return lax.conv_general_dilated(padded, kernel, (1, 1), 'VALID', dimension_numbers=('NCHW', 'HWIO', 'NCHW'), preferred_element_type=jnp.float32)

def padded_by(values, margin):
    return jnp.pad(values, ((0, 0), (0, 0), (margin, margin), (margin, margin)))

def flipped(kernel):
    return jnp.swapaxes(kernel[::-1, ::-1], 2, 3)

def pooled(values):
    batch, planes, height, columns = values.shape
    return values.reshape(batch, planes, height // 2, 2, columns // 2, 2).mean(axis=(3, 5))

def unpooled(values):
    return 0.25 * jnp.repeat(jnp.repeat(values, 2, axis=-2), 2, axis=-1)

def activate(pre):
    return pre * jax.nn.sigmoid(pre)

def activate_slope(pre):
    sigma = jax.nn.sigmoid(pre)
    return sigma * (1.0 + pre * (1.0 - sigma))

def unit_terms(features, sums):
    scales = lax.rsqrt(sums + EPSILON)
    return (features * scales[:, None], scales)

def layer_loss(unit_vec, weights):
    differ = unit_vec[0] - unit_vec[1]
    return jnp.sum(weights[:, None, None] * differ * differ)

def slopes(unit_vec, features, weights, factor):
    slope = 2.0 * factor * weights[:, None, None] * (unit_vec[0] - unit_vec[1])
    return (slope, lax.optimization_barrier(jnp.sum(features[0] * slope, axis=0)))

def finish_grad(slope, features, scales, inners):
    first = scales[0]
    return first[None] * slope - features[0] * (first * first * first * inners)[None]

def reference(image_gen, image_ref, kernel_one, bias_one, kernel_two, bias_two, kernel_three, bias_three, lin_first, lin_second, lin_third):
    pixels = image_gen.shape[1] * image_gen.shape[2]
    stacked = jnp.stack([normed_cells(image_gen), normed_cells(image_ref)])
    pre_one = conv_valid(padded_by(stacked, 1), kernel_one) + bias_one[None, :, None, None]
    features_one = activate(pre_one)
    pool_one = pooled(features_one).astype(jnp.bfloat16)
    pre_two = conv_valid(padded_by(pool_one, 2), kernel_two) + bias_two[None, :, None, None]
    features_two = activate(pre_two)
    pool_two = pooled(features_two).astype(jnp.bfloat16)
    pre_three = conv_valid(padded_by(pool_two, 1), kernel_three) + bias_three[None, :, None, None]
    features_three = activate(pre_three)
    unit_one, scales_one = unit_terms(features_one, lax.optimization_barrier(jnp.sum(features_one * features_one, axis=1)))
    unit_two, scales_two = unit_terms(features_two, lax.optimization_barrier(jnp.sum(features_two * features_two, axis=1)))
    unit_three, scales_three = unit_terms(features_three, lax.optimization_barrier(jnp.sum(features_three * features_three, axis=1)))
    count_one = pixels // 16
    count_two = pixels // 64
    count_three = pixels // 256
    loss = layer_loss(unit_one, lin_first) / count_one + layer_loss(unit_two, lin_second) / count_two + layer_loss(unit_three, lin_third) / count_three
    slope_one, inners_one = slopes(unit_one, features_one, lin_first, 16.0)
    slope_two, inners_two = slopes(unit_two, features_two, lin_second, 64.0)
    slope_three, inners_three = slopes(unit_three, features_three, lin_third, 256.0)
    dfeat_three = finish_grad(slope_three, features_three, scales_three, inners_three)
    dpre_three = (dfeat_three * activate_slope(pre_three[0])).astype(jnp.bfloat16)
    dpool_two = conv_valid(padded_by(dpre_three[None], 1), flipped(kernel_three))[0]
    dfeat_two = finish_grad(slope_two, features_two, scales_two, inners_two) + unpooled(dpool_two)
    dpre_two = (dfeat_two * activate_slope(pre_two[0])).astype(jnp.bfloat16)
    dpool_one = conv_valid(padded_by(dpre_two[None], 2), flipped(kernel_two))[0]
    dfeat_one = finish_grad(slope_one, features_one, scales_one, inners_one) + unpooled(dpool_one)
    dpre_one = (dfeat_one * activate_slope(pre_one[0])).astype(jnp.bfloat16)
    back_cells = conv_valid(padded_by(dpre_one[None], 1), flipped(kernel_one))[0]
    spreads = jnp.array(SPREADS, jnp.float32)[:, None, None]
    image_grad = from_cells(back_cells) / spreads
    return (image_grad, loss)
```

```python
import functools

import jax
import jax.numpy as jnp
from jax import lax
from jax.experimental import pallas as pl
from jax.experimental.pallas import tpu as pltpu
from jax.sharding import PartitionSpec as P

OFFSETS = (-0.03, -0.088, -0.188)
SPREADS = (0.458, 0.448, 0.45)
EPSILON = 1e-06
BF = jnp.bfloat16
F32 = jnp.float32
DIRS = ((-1, 0), (1, 0), (0, -1), (0, 1), (-1, -1), (-1, 1), (1, -1), (1, 1))
UP, DOWN, LEFT, RIGHT, UL, UR, DL, DR = range(8)
OPP = (1, 0, 3, 2, 7, 6, 5, 4)
STAGES = 8


def roll(x, shift):
    return pltpu.roll(x, shift % 128, 1)


def dot(a, b):
    return jnp.dot(a, b, preferred_element_type=F32)


def lanes(shape):
    return lax.broadcasted_iota(jnp.int32, shape, 1)


def shifted(x, e):
    low = lanes(x.shape) < 64
    if e == 1:
        return jnp.where(low, roll(x, 64), roll(x, 63))
    if e == -1:
        return jnp.where(low, roll(x, 65), roll(x, 64))
    return roll(x, -e // 2)


def kernel(
    img0, img1, wb1, w2t, w2n, w3s, wb1b, b1, b2, b3, l1, l2, l3,
    grad, loss,
    sel, pf, ef, tmp, lw, ew, x1, f1, sl1, pool1, x2, f2, sl2, keep, pool2, x3,
    f3, sl3, d3, x3d, w3t, w3n, dp2, d2, x4, yb, xh, yh, d1, x5, bf,
    cb1, cb2, cb3, cl1, cl2, cl3, la, lsa, lsb, lsc,
    su0, sd0, se0, seu, sed, ru0, rd0, rl0, rr0, rc0,
    se1, hs1, se2, hs2, ru2, rd2, se3, hs3, ru3, rd3, se4, hs4, se5, hs5, ru5, rd5,
    send_sem, recv_sem, wsend, wrecv, lsend, lrecv,
):
    n_row, n_col, n_chan = lax.axis_size("row"), lax.axis_size("col"), lax.axis_size("chan")
    i_row, i_col, i_chan = lax.axis_index("row"), lax.axis_index("col"), lax.axis_index("chan")
    tile = i_row * n_chan + i_chan
    n_tile = n_row * n_chan

    def place(step_t, step_c):
        other = tile + step_t
        return {"row": other // n_chan, "chan": other % n_chan, "col": i_col + step_c}

    def exists(step_t, step_c):
        ok = None
        for step, at, count in ((step_t, tile, n_tile), (step_c, i_col, n_col)):
            if step < 0:
                term = at > 0
            elif step > 0:
                term = at < count - 1
            else:
                continue
            ok = term if ok is None else jnp.logical_and(ok, term)
        return ok

    peers = [("chan", i_chan, n_chan, k) for k in range(1, n_chan)]
    peers += [("col", i_col, n_col, k) for k in range(1, n_col)]
    peers += [("row", i_row, n_row, k) for k in range(1, n_row)]

    barrier = pltpu.get_barrier_semaphore()

    def greets(d):
        if d in (LEFT, RIGHT):
            return None
        ok = exists(*DIRS[d])
        if d == UP:
            ok = jnp.logical_and(ok, i_chan == 0)
        if d == DOWN:
            ok = jnp.logical_and(ok, i_chan == n_chan - 1)
        return ok

    for d in range(8):
        if greets(d) is not None:

            @pl.when(greets(d))
            def _():
                pl.semaphore_signal(barrier, inc=1, device_id=place(*DIRS[d]), device_id_type=pl.DeviceIdType.MESH)

    for axis, at, count, k in peers:
        pl.semaphore_signal(
            barrier, inc=1, device_id={axis: (at + k) % count}, device_id_type=pl.DeviceIdType.MESH
        )

    def barrier_wait():
        total = jnp.int32(len(peers))
        for d in range(8):
            if greets(d) is not None:
                total = total + greets(d).astype(jnp.int32)
        pl.semaphore_wait(barrier, total)

    def copy(stage, d, src, dst):
        return pltpu.make_async_remote_copy(
            src_ref=src,
            dst_ref=dst,
            send_sem=send_sem.at[stage, d],
            recv_sem=recv_sem.at[stage, d],
            device_id=place(*DIRS[d]),
            device_id_type=pl.DeviceIdType.MESH,
        )

    def start(stage, plan):
        for d, (src, dst) in enumerate(plan):

            @pl.when(exists(*DIRS[d]))
            def _():
                copy(stage, d, src, dst).start()

    def arrive(stage, plan):
        for d, (src, dst) in enumerate(plan):
            back = DIRS[OPP[d]]

            @pl.when(exists(*back))
            def _():
                copy(stage, d, src, dst).wait_recv()

            @pl.when(jnp.logical_not(exists(*back)))
            def _():
                dst[...] = jnp.zeros(dst.shape, dst.dtype)

    def drain(stage, plan):
        for d, (src, dst) in enumerate(plan):

            @pl.when(exists(*DIRS[d]))
            def _():
                copy(stage, d, src, dst).wait_send()

    plan0 = [
        (su0, rd0), (sd0, ru0), (se0, rr0), (se0, rl0),
        (seu, rc0.at[3]), (seu, rc0.at[2]), (sed, rc0.at[1]), (sed, rc0.at[0]),
    ]

    def side_plan(up, down, side, hs):
        return [
            up, down, (side, hs.at[1]), (side, hs.at[0]),
            (side, hs.at[5]), (side, hs.at[4]), (side, hs.at[3]), (side, hs.at[2]),
        ]

    plan1 = [
        side_plan(
            (pool1.at[f, pl.ds(2, 2)], pool1.at[f, pl.ds(10, 2)]),
            (pool1.at[f, pl.ds(8, 2)], pool1.at[f, pl.ds(0, 2)]),
            se1.at[f], hs1.at[f],
        )
        for f in range(2)
    ]
    plan2 = [
        side_plan((pool2.at[f, 0], rd2.at[f]), (pool2.at[f, 1], ru2.at[f]), se2.at[f], hs2.at[f])
        for f in range(2)
    ]
    plan3 = side_plan((d3.at[0], rd3), (d3.at[1], ru3), se3, hs3)
    plan4 = side_plan((d2.at[pl.ds(2, 2)], d2.at[pl.ds(10, 2)]), (d2.at[pl.ds(8, 2)], d2.at[pl.ds(0, 2)]), se4, hs4)
    plan5 = side_plan((d1.at[0], rd5), (d1.at[15], ru5), se5, hs5)

    for f, img in enumerate((img0, img1)):
        for c in range(3):
            v = ((img[c] - OFFSETS[c]) * (1.0 / SPREADS[c])).astype(BF)
            pf[3 * f + c, 8:72, :] = v.astype(F32)
            edge = jnp.where(
                lanes((64, 128)) < 4, v[:, :128].astype(F32), roll(v[:, 896:].astype(F32), 8)
            )
            se0[f * 192 + 64 * c : f * 192 + 64 * c + 64, :] = edge.astype(BF)
    for buf, edge, at in ((su0, seu, 8), (sd0, sed, 68)):
        tmp[...] = jnp.zeros(tmp.shape, F32)
        for f in range(2):
            for c in range(3):
                tmp[16 * f + 4 * c : 16 * f + 4 * c + 4, :] = pf[3 * f + c, at : at + 4, :]
        v = tmp[...]
        buf[...] = v.astype(BF)
        edge[...] = jnp.where(lanes((32, 128)) < 4, v[:, :128], roll(v[:, 896:], 8)).astype(BF)

    barrier_wait()
    start(0, plan0)

    def shard_copy(k):
        rows = pl.ds(i_chan * 96, 96)
        return pltpu.make_async_remote_copy(
            src_ref=w3s,
            dst_ref=w3t.at[rows],
            send_sem=wsend.at[k - 1],
            recv_sem=wrecv.at[k - 1],
            device_id={"chan": (i_chan + k) % n_chan},
            device_id_type=pl.DeviceIdType.MESH,
        )

    for k in range(1, n_chan):
        shard_copy(k).start()
    w3t[pl.ds(pl.multiple_of(i_chan * 96, 32), 96), :] = w3s[...]

    for src, dst in ((b1, cb1), (b2, cb2), (b3, cb3), (l1, cl1), (l2, cl2), (l3, cl3)):
        dst[...] = jnp.transpose(jnp.broadcast_to(src[...], (128, src.shape[1])))
    la[...] = jnp.zeros(la.shape, F32)

    for px in range(8):
        at = lax.broadcasted_iota(jnp.int32, (1024, 128), 0)
        lane = lanes((1024, 128))
        want = 8 * (2 * (lane % 64) + lane // 64) + px
        sel[:, 128 * px : 128 * px + 128] = jnp.where(at == want, 1.0, 0.0).astype(BF)

    arrive(0, plan0)
    for buf, at in ((ru0, 4), (rd0, 72)):
        tmp[...] = buf[...].astype(F32)
        for f in range(2):
            for c in range(3):
                pf[3 * f + c, at : at + 4, :] = tmp[16 * f + 4 * c : 16 * f + 4 * c + 4, :]
    for s, (mid, up, down) in enumerate(((rl0, 0, 2), (rr0, 1, 3))):
        for f in range(2):
            for c in range(3):
                ef[s, 3 * f + c, 8:72, :] = mid[f * 192 + 64 * c : f * 192 + 64 * c + 64, :].astype(F32)
        for corner, at in ((up, 4), (down, 72)):
            tmp[:, :128] = rc0[corner].astype(F32)
            for f in range(2):
                for c in range(3):
                    ef[s, 3 * f + c, at : at + 4, :] = tmp[16 * f + 4 * c : 16 * f + 4 * c + 4, :128]

    def pixels(f):
        for r in range(8):
            for c in range(3):
                rows = slice((r * 3 + c) * 16, (r * 3 + c) * 16 + 16)
                lw[rows, :] = pf[3 * f + c, 8 * r + 4 : 8 * r + 20, :].astype(BF)
                for s in range(2):
                    ew[s, rows, :] = ef[s, 3 * f + c, 8 * r + 4 : 8 * r + 20, :]
        for pp in range(4):
            both = dot(lw[...], sel[:, 256 * pp : 256 * pp + 256])
            for px in (2 * pp, 2 * pp + 1):
                x = both[:, 128 * (px % 2) : 128 * (px % 2) + 128]
                if px >= 4:
                    other = shifted(x, -1)
                    other = jnp.where(lanes(x.shape) == 0, roll(ew[0], -px), other)
                    wx = px - 4
                else:
                    other = shifted(x, 1)
                    other = jnp.where(lanes(x.shape) == 127, roll(ew[1], 127 - px), other)
                    wx = 12 + px
                for w, v in ((4 + px, x), (wx, other)):
                    v = v.astype(BF)
                    for r in range(8):
                        x1[r % 4, 48 * w : 48 * w + 48, 128 * (r // 4) : 128 * (r // 4) + 128] = v[48 * r : 48 * r + 48]

    def silu(v):
        sigma = 0.5 * jnp.tanh(0.5 * v) + 0.5
        return v * sigma, sigma

    def layer_one(f):
        def body(i, _):
            out = dot(wb1[...], x1[i])
            for h in range(2):
                acc = None
                for ph in range(4):
                    v = out[64 * ph : 64 * ph + 64, 128 * h : 128 * h + 128] + cb1[...]
                    feat, sigma = silu(v)
                    n = (i + 4 * h) * 4 + ph
                    f1[f, n] = feat
                    if f == 0:
                        sl1[n] = sigma * (1.0 + v * (1.0 - sigma))
                    acc = feat if acc is None else acc + feat
                pool1[f, 2 + i + 4 * h] = (0.25 * acc).astype(BF)
            return 0

        lax.fori_loop(0, 4, body, 0)

    def pack_columns(rows, side):
        channels = side.shape[0]
        for at in range(0, channels, 64):
            acc = jnp.zeros((64, 128), F32)
            lane = lanes((64, 128)) % 64
            for r in range(8):
                x = rows(r, at).astype(F32)
                acc = jnp.where(lane == r + 2, roll(x, r + 2), acc)
                acc = jnp.where(lane == 16 + r + 2, roll(x, 16 + r + 2 - 63), acc)
            side[at : at + 64, :] = acc.astype(BF)

    def merged(hs, at, size, step, top, bottom, base):
        lane = lanes((size, 128)) % 64
        sides = []
        for s, first in ((1, 0), (0, base)):
            mid = hs[s, at : at + size, :].astype(F32)
            up = roll(hs[2 + s, at : at + size, :].astype(F32), -step)
            down = roll(hs[4 + s, at : at + size, :].astype(F32), step)
            v = jnp.where(lane < first + top, up, jnp.where(lane < first + bottom, mid, down))
            sides.append(v)
        return jnp.where(lane < base, sides[0], sides[1])

    def layer_two_operand(f):
        lane = lanes((64, 128))
        halo = merged(hs1.at[f], 0, 64, 8, 2, 10, 16)
        for rr in range(12):
            x = pool1[f, rr].astype(F32)
            right = roll(halo, 63 - rr)
            left = roll(halo, -16 - rr)
            cols = (
                jnp.where(lane % 64 == 0, left, shifted(x, -2)),
                jnp.where(lane == 0, roll(left, 64), shifted(x, -1)),
                x,
                jnp.where(lane == 127, roll(right, 64), shifted(x, 1)),
                jnp.where(lane % 64 == 63, right, shifted(x, 2)),
            )
            for e, v in enumerate(cols):
                v = v.astype(BF)
                if rr < 8:
                    x2[320 * rr + 64 * e : 320 * rr + 64 * e + 64, :128] = v
                if rr >= 4:
                    x2[320 * (rr - 4) + 64 * e : 320 * (rr - 4) + 64 * e + 64, 128:] = v

    def layer_two(f):
        low = lanes((64, 128)) < 64
        for i in range(4):
            out = dot(w2t[...], x2[320 * i : 320 * i + 1600, :])
            for h in range(2):
                for k in range(3):
                    rows = slice(64 * k, 64 * k + 64)
                    v = out[rows, 128 * h : 128 * h + 128] + cb2[rows]
                    feat, sigma = silu(v)
                    f2[f, i + 4 * h, rows] = feat
                    if f == 0:
                        sl2[i + 4 * h, rows] = sigma * (1.0 + v * (1.0 - sigma))
                    if i % 2 == 1:
                        both = f2[f, i - 1 + 4 * h, rows] + feat
                        mean = 0.25 * (both + roll(both, 64))
                        if i == 1:
                            keep[h, rows] = mean
                        else:
                            pool2[f, h, rows] = jnp.where(low, keep[h, rows], mean).astype(BF)

    def pack_ends(tiles, side):
        channels = side.shape[0]
        for at in range(0, channels, 64):
            lane = lanes((64, 128))
            acc = jnp.zeros((64, 128), F32)
            for r in range(4):
                x = tiles[r // 2, at : at + 64, :].astype(F32)
                first = 64 * (r % 2)
                for src, dst in ((0, r + 1), (0, 64 + r), (63, 16 + r + 1), (63, 80 + r)):
                    acc = jnp.where(lane == dst, roll(x, dst - src - first), acc)
            side[at : at + 64, :] = acc.astype(BF)

    def merged_ends(hs, at):
        lane = lanes((64, 128))
        sides = []
        for s, first in ((1, 0), (0, 16)):
            mid = hs[s, at : at + 64, :].astype(F32)
            up = roll(hs[2 + s, at : at + 64, :].astype(F32), -4)
            down = roll(hs[4 + s, at : at + 64, :].astype(F32), 4)
            v = jnp.where(lane == first, up, jnp.where(lane == first + 5, down, mid))
            sides.append(jnp.where(lane == 64 + first + 4, down, v))
        return jnp.where(lane % 64 < 16, sides[0], sides[1])

    def layer_three_operand(tiles, from_up, from_down, hs, dst):
        channels = tiles.shape[1]
        for at in range(0, channels, 64):
            rows = slice(at, at + 64)
            lane = lanes((64, 128))
            low = lane < 64
            halo = merged_ends(hs, at)
            b = tiles[0, rows].astype(F32)
            d = tiles[1, rows].astype(F32)
            b_swap, d_swap = roll(b, 64), roll(d, 64)
            a = jnp.where(low, roll(from_up[rows].astype(F32), 64), b_swap)
            c = jnp.where(low, b_swap, d_swap)
            e = jnp.where(low, d_swap, roll(from_down[rows].astype(F32), 64))
            for rr, (x, spots) in enumerate(
                ((a, ((0, 0),)), (b, ((1, 0),)), (c, ((0, 1), (2, 0))), (d, ((1, 1),)), (e, ((2, 1),)))
            ):
                left = jnp.where(lane % 64 == 0, roll(halo, -16 - rr), roll(x, 1))
                right = jnp.where(lane % 64 == 63, roll(halo, 63 - rr), roll(x, 127))
                for dx, v in enumerate((left, x, right)):
                    v = v.astype(BF)
                    for dy, half in spots:
                        base = (dy * 3 + dx) * channels + at
                        dst[base : base + 64, 128 * half : 128 * half + 128] = v

    def layer_three(f):
        out = dot(w3t[...], x3[f])
        for h in range(2):
            for k in range(6):
                rows = slice(64 * k, 64 * k + 64)
                v = out[rows, 128 * h : 128 * h + 128] + cb3[rows]
                feat, sigma = silu(v)
                f3[f, h, rows] = feat
                if f == 0:
                    sl3[h, rows] = sigma * (1.0 + v * (1.0 - sigma))

    def local_terms(feats, n, weights, factor, count, finish):
        chunks = weights.shape[0] // 64
        rows = [slice(64 * k, 64 * k + 64) for k in range(chunks)]
        sums = [jnp.zeros((1, 128), F32)] * 2
        for f in range(2):
            for k in range(chunks):
                v = feats[f, n, rows[k]]
                sums[f] = sums[f] + jnp.sum(v * v, axis=0, keepdims=True)
        first, second = lax.rsqrt(sums[0] + EPSILON), lax.rsqrt(sums[1] + EPSILON)
        inner = jnp.zeros((1, 128), F32)
        total = jnp.zeros((1, 128), F32)
        for k in range(chunks):
            v = feats[0, n, rows[k]]
            differ = v * first - feats[1, n, rows[k]] * second
            slope = weights[rows[k]] * differ
            total = total + jnp.sum(slope * differ, axis=0, keepdims=True)
            inner = inner + jnp.sum(v * slope, axis=0, keepdims=True)
        la[0:1, :] = la[0:1, :] + total * (1.0 / count)
        scale = 2.0 * factor * first
        cubed = 2.0 * factor * first * first * first * inner
        for k in range(chunks):
            v = feats[0, n, rows[k]]
            slope = weights[rows[k]] * (v * first - feats[1, n, rows[k]] * second)
            finish(k, rows[k], scale * slope - v * cubed)

    for f in range(2):
        pixels(f)
        layer_one(f)
        pack_columns(lambda r, at: pool1[f, 2 + r], se1.at[f])
        start(1 + f, plan1[f])
    for f in range(2):
        arrive(1 + f, plan1[f])
        layer_two_operand(f)
        layer_two(f)
        pack_ends(pool2.at[f], se2.at[f])
        start(3 + f, plan2[f])
    for k in range(1, n_chan):
        shard_copy(k).wait_recv()
    for f in range(2):
        arrive(3 + f, plan2[f])
        layer_three_operand(pool2.at[f], ru2.at[f], rd2.at[f], hs2.at[f], x3.at[f])
        layer_three(f)

    pixel_count = 64 * n_tile * 1024 * n_col

    for h in range(2):

        def finish_three(k, rows, dfeat):
            d3[h, rows] = (dfeat * sl3[h, rows]).astype(BF)

        local_terms(f3, h, cl3, 256.0, pixel_count // 256, finish_three)
    pack_ends(d3, se3)
    start(5, plan3)

    def terms_two(n, _):
        def finish_two(k, rows, dfeat):
            f2[0, n, rows] = dfeat

        local_terms(f2, n, cl2, 64.0, pixel_count // 64, finish_two)
        return 0

    lax.fori_loop(0, 8, terms_two, 0)

    def terms_one(n, _):
        def finish_one(k, rows, dfeat):
            f1[0, n, rows] = dfeat

        local_terms(f1, n, cl1, 16.0, pixel_count // 16, finish_one)
        return 0

    lax.fori_loop(0, 32, terms_one, 0)

    def loss_copy(axis, k):
        which = ("col", "chan", "row").index(axis)
        slots = (lsa, lsb, lsc)[which]
        at, count = ((i_col, n_col), (i_chan, n_chan), (i_row, n_row))[which]
        return pltpu.make_async_remote_copy(
            src_ref=la,
            dst_ref=slots.at[k - 1],
            send_sem=lsend.at[which, k - 1],
            recv_sem=lrecv.at[which, k - 1],
            device_id={axis: (at + k) % count},
            device_id_type=pl.DeviceIdType.MESH,
        )

    def loss_start(axis, count):
        for k in range(1, count):
            loss_copy(axis, k).start()

    def loss_finish(axis, count, slots):
        for k in range(1, count):
            loss_copy(axis, k).wait()
        total = la[...]
        for k in range(1, count):
            total = total + slots[k - 1]
        la[...] = total

    loss_start("col", n_col)
    eye = jnp.where(
        lax.broadcasted_iota(jnp.int32, (128, 128), 0) == lanes((128, 128)), 1.0, 0.0
    ).astype(BF)
    for at in range(0, 1728, 128):
        size = min(128, 1728 - at)
        part = lax.dot_general(
            eye[:size, :size], w3t[:, at : at + size], (((1,), (1,)), ((), ())), preferred_element_type=F32
        )
        w3n[at : at + size, :] = part.astype(BF)

    arrive(5, plan3)
    layer_three_operand(d3, ru3, rd3, hs3, x3d)
    acc = None
    for tap in range(9):
        part = dot(w3n[192 * (8 - tap) : 192 * (8 - tap) + 192, :], x3d[384 * tap : 384 * tap + 384, :])
        acc = part if acc is None else acc + part
    dp2[...] = acc
    loss_finish("col", n_col, lsa)
    loss_start("chan", n_chan)

    for r in range(8):
        for k in range(3):
            rows = slice(64 * k, 64 * k + 64)
            t = dp2[rows, 128 * (r // 4) : 128 * (r // 4) + 128]
            low = lanes((64, 128)) < 64
            swap = roll(t, 64)
            wide = jnp.where(low, t, swap) if (r // 2) % 2 == 0 else jnp.where(low, swap, t)
            d2[2 + r, rows] = ((f2[0, r, rows] + 0.25 * wide) * sl2[r, rows]).astype(BF)
    pack_columns(lambda r, at: d2[2 + r, at : at + 64], se4)
    start(6, plan4)
    arrive(6, plan4)
    for rr in range(12):
        v = d2[rr]
        if rr < 8:
            x4[192 * rr : 192 * rr + 192, :128] = v
        if rr >= 4:
            x4[192 * (rr - 4) : 192 * (rr - 4) + 192, 128:] = v
    for at in range(0, 192, 64):
        halo = merged(hs4, at, 64, 8, 2, 10, 16)
        for dy in range(5):
            xh[192 * dy + at : 192 * dy + at + 64, :] = roll(halo, -dy).astype(BF)
    acc = None
    for dy in range(5):
        part = dot(w2n[320 * (4 - dy) : 320 * (4 - dy) + 320, :], xh[192 * dy : 192 * dy + 192, :])
        acc = part if acc is None else acc + part
    yh[...] = acc
    loss_finish("chan", n_chan, lsb)
    loss_start("row", n_row)
    lane = lanes((64, 128))
    for i in range(4):
        acc = None
        for dy in range(5):
            part = dot(
                w2n[320 * (4 - dy) : 320 * (4 - dy) + 320, :],
                x4[192 * (i + dy) : 192 * (i + dy) + 192, :],
            )
            acc = part if acc is None else acc + part
        yb[...] = acc
        for h in range(2):
            r = i + 4 * h

            def piece(e, src=None):
                if src is None:
                    return yb[64 * (2 - e) : 64 * (2 - e) + 64, 128 * h : 128 * h + 128]
                return yh[64 * (2 - e) : 64 * (2 - e) + 64, :]

            total = piece(0)
            total = total + jnp.where(lane == 127, roll(piece(1, 1), 127 - r), shifted(piece(1), 1))
            total = total + jnp.where(lane % 64 == 63, roll(piece(2, 1), 63 - r), shifted(piece(2), 2))
            total = total + jnp.where(lane == 0, roll(piece(-1, 1), -80 - r), shifted(piece(-1), -1))
            total = total + jnp.where(lane % 64 == 0, roll(piece(-2, 1), -16 - r), shifted(piece(-2), -2))
            total = 0.25 * total
            for py in range(2):
                for px in range(2):
                    n = 4 * r + 2 * py + px
                    d1[2 * r + py, 64 * px : 64 * px + 64] = ((f1[0, n] + total) * sl1[n]).astype(BF)

    acc = jnp.zeros((64, 128), F32)
    for cr in range(16):
        acc = jnp.where(lane == cr + 1, roll(d1[cr, :64].astype(F32), cr + 1), acc)
        acc = jnp.where(lane == cr + 33, roll(d1[cr, 64:].astype(F32), cr + 33 - 127), acc)
    se5[...] = acc.astype(BF)
    start(7, plan5)
    arrive(7, plan5)
    sides = []
    for s, first in ((1, 0), (0, 32)):
        mid = hs5[s].astype(F32)
        up = roll(hs5[2 + s].astype(F32), -16)
        down = roll(hs5[4 + s].astype(F32), 16)
        sides.append(jnp.where(lane == first, up, jnp.where(lane == first + 17, down, mid)))
    halo = jnp.where(lane < 32, sides[0], sides[1])
    for n in range(18):
        src = ru5 if n == 0 else rd5 if n == 17 else d1.at[n - 1]
        zero, one = src[:64], src[64:]
        before = jnp.where(lane == 0, roll(halo, -32 - n), shifted(one.astype(F32), -1)).astype(BF)
        after = jnp.where(lane == 127, roll(halo, 127 - n), shifted(zero.astype(F32), 1)).astype(BF)
        for g, v in enumerate((before, zero, one, after)):
            if n < 10:
                x5[256 * n + 64 * g : 256 * n + 64 * g + 64, :128] = v
            if n >= 8:
                x5[256 * (n - 8) + 64 * g : 256 * (n - 8) + 64 * g + 64, 128:] = v
    for i in range(4):
        out = dot(wb1b[...], x5[512 * i : 512 * i + 1024, :])
        for h in range(2):
            r = i + 4 * h
            for px in range(8):
                for c in range(3):
                    at = px * 24 + c * 8
                    bf[64 * c + 8 * r : 64 * c + 8 * r + 8, 128 * px : 128 * px + 128] = out[
                        at : at + 8, 128 * h : 128 * h + 128
                    ]
    loss_finish("row", n_row, lsc)
    loss[...] = jnp.sum(la[0:1, :], axis=1, keepdims=True)
    planes = bf[...].astype(BF)
    for part in range(4):
        cols = slice(256 * part, 256 * part + 256)
        out = lax.dot_general(planes, sel[cols, :], (((1,), (1,)), ((), ())), preferred_element_type=F32)
        for c in range(3):
            grad[c, :, cols] = out[64 * c : 64 * c + 64] * (1.0 / SPREADS[c])

    drain(0, plan0)
    for f in range(2):
        drain(1 + f, plan1[f])
        drain(3 + f, plan2[f])
    drain(5, plan3)
    drain(6, plan4)
    drain(7, plan5)
    for k in range(1, n_chan):
        shard_copy(k).wait_send()


def block_kernel(kernel_one, flip):
    base = kernel_one.reshape(3, 3, 3, 4, 4, 64)
    if flip:
        base = base[::-1, ::-1]
    rows = []
    for cy in range(2):
        rows.append(
            jnp.stack(
                [jnp.pad(base, ((cy, 1 - cy), (cx, 1 - cx)) + ((0, 0),) * 4) for cx in range(2)]
            )
        )
    return jnp.stack(rows)


def local(
    image_gen, image_ref, kernel_one, bias_one, kernel_two, bias_two, kernel_three, bias_three,
    lin_first, lin_second, lin_third,
):
    n_row, n_col, n_chan = lax.axis_size("row"), lax.axis_size("col"), lax.axis_size("chan")
    wb1 = block_kernel(kernel_one, False).transpose(0, 1, 7, 3, 6, 4, 2, 5).reshape(256, 768)
    wb1b = block_kernel(kernel_one, True).transpose(1, 6, 4, 0, 5, 2, 3, 7).reshape(192, 1024)
    w2n = kernel_two.reshape(1600, 192)
    w3s = kernel_three.reshape(1728, 96).T
    rows = [v.reshape(1, -1) for v in (bias_one, bias_two, bias_three, lin_first, lin_second, lin_third)]
    V = pltpu.VMEM
    scratch = dict(
        sel=V((1024, 1024), BF), pf=V((6, 80, 1024), F32), ef=V((2, 6, 80, 128), F32),
        tmp=V((32, 1024), F32), lw=V((384, 1024), BF), ew=V((2, 384, 128), F32),
        x1=V((4, 768, 256), BF), f1=V((2, 32, 64, 128), F32), sl1=V((32, 64, 128), F32),
        pool1=V((2, 12, 64, 128), BF), x2=V((2560, 256), BF), f2=V((2, 8, 192, 128), F32),
        sl2=V((8, 192, 128), F32), keep=V((2, 192, 128), F32), pool2=V((2, 2, 192, 128), BF),
        x3=V((2, 1728, 256), BF), f3=V((2, 2, 384, 128), F32), sl3=V((2, 384, 128), F32),
        d3=V((2, 384, 128), BF), x3d=V((3456, 256), BF), w3t=V((384, 1728), BF), w3n=V((1728, 384), BF),
        dp2=V((192, 256), F32), d2=V((12, 192, 128), BF), x4=V((1536, 256), BF), yb=V((320, 256), F32),
        xh=V((960, 128), BF), yh=V((320, 128), F32), d1=V((16, 128, 128), BF), x5=V((2560, 256), BF),
        bf=V((192, 1024), F32), cb1=V((64, 128), F32), cb2=V((192, 128), F32), cb3=V((384, 128), F32),
        cl1=V((64, 128), F32), cl2=V((192, 128), F32), cl3=V((384, 128), F32), la=V((8, 128), F32),
        lsa=V((max(n_col - 1, 1), 8, 128), F32), lsb=V((max(n_chan - 1, 1), 8, 128), F32),
        lsc=V((max(n_row - 1, 1), 8, 128), F32),
        su0=V((32, 1024), BF), sd0=V((32, 1024), BF), se0=V((384, 128), BF), seu=V((32, 128), BF),
        sed=V((32, 128), BF), ru0=V((32, 1024), BF), rd0=V((32, 1024), BF), rl0=V((384, 128), BF),
        rr0=V((384, 128), BF), rc0=V((4, 32, 128), BF),
        se1=V((2, 64, 128), BF), hs1=V((2, 6, 64, 128), BF), se2=V((2, 192, 128), BF),
        hs2=V((2, 6, 192, 128), BF), ru2=V((2, 192, 128), BF), rd2=V((2, 192, 128), BF),
        se3=V((384, 128), BF), hs3=V((6, 384, 128), BF), ru3=V((384, 128), BF), rd3=V((384, 128), BF),
        se4=V((192, 128), BF), hs4=V((6, 192, 128), BF), se5=V((64, 128), BF), hs5=V((6, 64, 128), BF),
        ru5=V((128, 128), BF), rd5=V((128, 128), BF),
        send_sem=pltpu.SemaphoreType.DMA((STAGES, 8)), recv_sem=pltpu.SemaphoreType.DMA((STAGES, 8)),
        wsend=pltpu.SemaphoreType.DMA((n_chan,)), wrecv=pltpu.SemaphoreType.DMA((n_chan,)),
        lsend=pltpu.SemaphoreType.DMA((3, 8)), lrecv=pltpu.SemaphoreType.DMA((3, 8)),
    )
    vmem = pl.BlockSpec(memory_space=pltpu.VMEM)
    grad, loss = pl.pallas_call(
        kernel,
        out_shape=(
            jax.ShapeDtypeStruct(image_gen.shape, F32),
            jax.ShapeDtypeStruct((1, 1), F32),
        ),
        in_specs=[vmem] * 13,
        out_specs=(vmem, vmem),
        scratch_shapes=list(scratch.values()),
        compiler_params=pltpu.CompilerParams(
            collective_id=0, has_side_effects=True, vmem_limit_bytes=62 * 1024 * 1024
        ),
        name="whole",
    )(image_gen, image_ref, wb1, w2n.T, w2n, w3s, wb1b, *rows)
    return (grad, loss.reshape(()))


def solution(mesh):
    rows = ("row", "chan")
    in_specs = (
        P(None, rows, "col"), P(None, rows, "col"), P(), P(), P(), P(),
        P(None, None, None, "chan"), P(), P(), P(), P(),
    )
    out_specs = (P(None, rows, "col"), P())
    return jax.shard_map(local, mesh=mesh, in_specs=in_specs, out_specs=out_specs, check_vma=False)
```

```python
import functools

import jax
import jax.numpy as jnp
from jax import lax
from jax.experimental import pallas as pl
from jax.experimental.pallas import tpu as pltpu
from jax.sharding import PartitionSpec as P

OFFSETS = (-0.03, -0.088, -0.188)
SPREADS = (0.458, 0.448, 0.45)
EPSILON = 1e-06
BF = jnp.bfloat16
F32 = jnp.float32
DIRS = ((-1, 0), (1, 0), (0, -1), (0, 1), (-1, -1), (-1, 1), (1, -1), (1, 1))
UP, DOWN, LEFT, RIGHT, UL, UR, DL, DR = range(8)
OPP = (1, 0, 3, 2, 7, 6, 5, 4)
STAGES = 8


def roll(x, shift):
    return pltpu.roll(x, shift % 128, 1)


def dot(a, b):
    return jnp.dot(a, b, preferred_element_type=F32)


def lanes(shape):
    return lax.broadcasted_iota(jnp.int32, shape, 1)


def shifted(x, e):
    low = lanes(x.shape) < 64
    if e == 1:
        return jnp.where(low, roll(x, 64), roll(x, 63))
    if e == -1:
        return jnp.where(low, roll(x, 65), roll(x, 64))
    return roll(x, -e // 2)


def kernel(
    img0_hbm, img1_hbm, k1_hbm, k2_hbm, k3_hbm, b1, b2, b3, l1, l2, l3,
    grad, loss,
    img, k1, w2n, k3, kpair, sela, wb1, wb1b, w2t,
    sel, pf, ef, tmp, lw, ew, x1, f1, sl1, pool1, x2, f2, sl2, keep, pool2, x3,
    f3, sl3, d3, x3d, w3t, w3n, dp2, d2, x4, yb, xh, yh, d1, x5, bf, hb,
    cb1, cb2, cb3, cl1, cl2, cl3, la, lsa, lsb, lsc,
    su0, sd0, se0, seu, sed, ru0, rd0, rl0, rr0, rc0,
    se1, hs1, se2, hs2, su2, sd2, ru2, rd2, se3, hs3, su3, sd3, ru3, rd3, se4, hs4, se5, hs5, ru5, rd5,
    send_sem, recv_sem, wsend, wrecv, lsend, lrecv, in_sem,
):
    n_row, n_col, n_chan = lax.axis_size("row"), lax.axis_size("col"), lax.axis_size("chan")
    i_row, i_col, i_chan = lax.axis_index("row"), lax.axis_index("col"), lax.axis_index("chan")
    tile = i_row * n_chan + i_chan
    n_tile = n_row * n_chan

    def place(step_t, step_c):
        other = tile + step_t
        return {"row": other // n_chan, "chan": other % n_chan, "col": i_col + step_c}

    def exists(step_t, step_c):
        ok = None
        for step, at, count in ((step_t, tile, n_tile), (step_c, i_col, n_col)):
            if step < 0:
                term = at > 0
            elif step > 0:
                term = at < count - 1
            else:
                continue
            ok = term if ok is None else jnp.logical_and(ok, term)
        return ok

    peers = [("chan", i_chan, n_chan, k) for k in range(1, n_chan)]
    peers += [("col", i_col, n_col, k) for k in range(1, n_col)]
    peers += [("row", i_row, n_row, k) for k in range(1, n_row)]
    far = {"row": i_row + 1 - 2 * (i_row % 2), "chan": (i_chan + 2) % n_chan}
    near = {"chan": i_chan + 1 - 2 * (i_chan % 2)}

    barrier = pltpu.get_barrier_semaphore()

    def greets(d):
        if d in (LEFT, RIGHT):
            return None
        ok = exists(*DIRS[d])
        if d == UP:
            ok = jnp.logical_and(ok, i_chan == 0)
        if d == DOWN:
            ok = jnp.logical_and(ok, i_chan == n_chan - 1)
        return ok

    for d in range(8):
        if greets(d) is not None:

            @pl.when(greets(d))
            def _():
                pl.semaphore_signal(barrier, inc=1, device_id=place(*DIRS[d]), device_id_type=pl.DeviceIdType.MESH)

    loads = [
        pltpu.make_async_copy(src, dst, in_sem.at[n])
        for n, (src, dst) in enumerate(
            (
                (img0_hbm, img.at[0]), (img1_hbm, img.at[1]), (k3_hbm, k3), (k1_hbm, k1), (k2_hbm, w2n),
            )
        )
    ]
    for load in loads:
        load.start()

    for axis, at, count, k in peers:
        pl.semaphore_signal(
            barrier, inc=1, device_id={axis: (at + k) % count}, device_id_type=pl.DeviceIdType.MESH
        )

    if n_chan > 1:
        pl.semaphore_signal(barrier, inc=1, device_id=far, device_id_type=pl.DeviceIdType.MESH)

    def barrier_wait():
        total = jnp.int32(len(peers) + (1 if n_chan > 1 else 0))
        for d in range(8):
            if greets(d) is not None:
                total = total + greets(d).astype(jnp.int32)
        pl.semaphore_wait(barrier, total)

    def copy(stage, d, src, dst):
        return pltpu.make_async_remote_copy(
            src_ref=src,
            dst_ref=dst,
            send_sem=send_sem.at[stage, d],
            recv_sem=recv_sem.at[stage, d],
            device_id=place(*DIRS[d]),
            device_id_type=pl.DeviceIdType.MESH,
        )

    def start(stage, plan):
        for d, (src, dst) in enumerate(plan):

            @pl.when(exists(*DIRS[d]))
            def _():
                copy(stage, d, src, dst).start()

    def arrive(stage, plan):
        for d, (src, dst) in enumerate(plan):
            back = DIRS[OPP[d]]

            @pl.when(exists(*back))
            def _():
                copy(stage, d, src, dst).wait_recv()

            @pl.when(jnp.logical_not(exists(*back)))
            def _():
                dst[...] = jnp.zeros(dst.shape, dst.dtype)

    def drain(stage, plan):
        for d, (src, dst) in enumerate(plan):

            @pl.when(exists(*DIRS[d]))
            def _():
                copy(stage, d, src, dst).wait_send()

    plan0 = [
        (su0, rd0), (sd0, ru0), (se0, rr0), (se0, rl0),
        (seu, rc0.at[3]), (seu, rc0.at[2]), (sed, rc0.at[1]), (sed, rc0.at[0]),
    ]

    def side_plan(up, down, side, hs):
        return [
            up, down, (side, hs.at[1]), (side, hs.at[0]),
            (side, hs.at[5]), (side, hs.at[4]), (side, hs.at[3]), (side, hs.at[2]),
        ]

    plan1 = [
        side_plan(
            (pool1.at[f, pl.ds(2, 2)], pool1.at[f, pl.ds(10, 2)]),
            (pool1.at[f, pl.ds(8, 2)], pool1.at[f, pl.ds(0, 2)]),
            se1.at[f], hs1.at[f],
        )
        for f in range(2)
    ]
    plan2 = [
        side_plan((su2.at[f], rd2.at[f]), (sd2.at[f], ru2.at[f]), se2.at[f], hs2.at[f])
        for f in range(2)
    ]
    plan3 = side_plan((su3, rd3), (sd3, ru3), se3, hs3)
    plan4 = side_plan((d2.at[pl.ds(2, 2)], d2.at[pl.ds(10, 2)]), (d2.at[pl.ds(8, 2)], d2.at[pl.ds(0, 2)]), se4, hs4)
    plan5 = side_plan((d1.at[0], rd5), (d1.at[15], ru5), se5, hs5)

    lane8 = lanes((8, 128))
    for f in range(2):
        loads[f].wait()
        for c in range(3):
            v = ((img[f, c] - OFFSETS[c]) * (1.0 / SPREADS[c])).astype(BF).astype(F32)
            pf[3 * f + c, 8:72, :] = v
    for c in range(3):
        acc = jnp.zeros((8, 128), F32)
        for f in range(2):
            for y in range(8):
                row = pf[3 * f + c, 8 + 8 * y : 16 + 8 * y, :]
                to = 64 * f + 8 * y
                acc = jnp.where((lane8 >= to) & (lane8 < to + 4), roll(row[:, :128], to), acc)
                acc = jnp.where((lane8 >= to + 4) & (lane8 < to + 8), roll(row[:, 896:], to + 8), acc)
        se0[8 * c : 8 * c + 8, :] = acc
    for buf, edge, at in ((su0, seu, 8), (sd0, sed, 68)):
        tmp[...] = jnp.zeros(tmp.shape, F32)
        for f in range(2):
            for c in range(3):
                tmp[16 * f + 4 * c : 16 * f + 4 * c + 4, :] = pf[3 * f + c, at : at + 4, :]
        v = tmp[...]
        buf[...] = v.astype(BF)
        edge[...] = jnp.where(lanes((32, 128)) < 4, v[:, :128], roll(v[:, 896:], 8)).astype(BF)

    barrier_wait()
    start(0, plan0)

    def eye(size):
        rows = lax.broadcasted_iota(jnp.int32, (size, size), 0)
        return jnp.where(rows == lanes((size, size)), 1.0, 0.0).astype(BF)

    def flip(one, block):
        return lax.dot_general(
            one, block, (((1,), (1,)), ((), ())), preferred_element_type=F32
        ).astype(BF)

    loads[2].wait()
    own = pl.ds(pl.multiple_of(i_chan * 96, 32), 96)
    one = eye(96)
    for at in range(0, 1728, 256):
        size = min(256, 1728 - at)
        w3t[own, at : at + size] = flip(one, k3[at : at + size, :])

    def shard_rows(owner, part):
        count = 96 if part is None else 16
        first = owner * 96 + (0 if part is None else 16 * part)
        return w3t.at[pl.ds(pl.multiple_of(first, 16), count)]

    def shard_copy(kind, part):
        rows = shard_rows((i_chan + 2) % n_chan if kind == 2 else i_chan, part)
        at = (0, 1, 7)[kind] + (part or 0)
        return pltpu.make_async_remote_copy(
            src_ref=rows,
            dst_ref=rows,
            send_sem=wsend.at[at],
            recv_sem=wrecv.at[at],
            device_id=far if kind == 1 else near,
            device_id_type=pl.DeviceIdType.MESH,
        )

    def shard_arrive(kind, part):
        owner = (near["chan"], i_chan + 2, near["chan"] + 2)[kind]
        rows = shard_rows(owner % n_chan, part)
        at = (0, 1, 7)[kind] + (part or 0)
        pltpu.make_async_remote_copy(
            src_ref=rows,
            dst_ref=rows,
            send_sem=wsend.at[at],
            recv_sem=wrecv.at[at],
            device_id=far if kind == 1 else near,
            device_id_type=pl.DeviceIdType.MESH,
        ).wait_recv()

    def shard_send(*parts):
        if n_chan > 1:
            for part in parts:
                shard_copy(1, part).start()

    def shard_pass(*parts):
        if n_chan > 1:
            for part in parts:
                shard_arrive(1, part)
                shard_copy(2, part).start()

    if n_chan > 1:
        shard_copy(0, None).start()

    for src, dst in ((b1, cb1), (b2, cb2), (b3, cb3), (l1, cl1), (l2, cl2), (l3, cl3)):
        dst[...] = jnp.transpose(jnp.broadcast_to(src[...], (128, src.shape[1])))
    la[...] = jnp.zeros(la.shape, F32)

    for px in range(8):
        at = lax.broadcasted_iota(jnp.int32, (1024, 128), 0)
        lane = lanes((1024, 128))
        want = 8 * (2 * (lane % 64) + lane // 64) + px
        sel[:, 128 * px : 128 * px + 128] = jnp.where(at == want, 1.0, 0.0).astype(BF)

    loads[3].wait()
    k1t = flip(eye(64), k1[...])
    cell = lax.broadcasted_iota(jnp.int32, (48, 128), 0)
    base = 48 * (cell % 4) + 16 * (cell // 16) + (cell // 4) % 4
    lane = lanes((48, 128))
    for cy in range(2):
        for cx in range(2):
            for tap in range(9):
                want = base + (192 * (tap % 3 + cx) + 4 * (tap // 3 + cy))
                for j in range(6):
                    sela[48 * tap : 48 * tap + 48, 128 * j : 128 * j + 128] = jnp.where(
                        lane + 128 * j == want, 1.0, 0.0
                    ).astype(BF)
            n = 2 * cy + cx
            wb1[64 * n : 64 * n + 64, :] = dot(k1t, sela[...]).astype(BF)

    kpair[...] = jnp.zeros(kpair.shape, BF)
    half = k1[...].astype(F32)
    both = jnp.concatenate([half, half], axis=1)
    low = lanes((432, 128)) < 64
    kpair[0:432, :] = jnp.where(low, both, 0.0).astype(BF)
    kpair[512:944, :] = jnp.where(low, 0.0, both).astype(BF)
    spot = lax.broadcasted_iota(jnp.int32, (24, 128), 0)
    lane = lanes((24, 128))
    in_low = (spot // 4) % 2 == 0
    within = 16 * (spot // 8) + 4 * (spot % 4)
    for wcy in range(4):
        for pair in range(2):
            for px in range(8):
                cx, b = px // 4, px % 4
                for side in range(2):
                    dx = 2 - (2 * pair + side) + cx
                    for j in range(4):
                        hit = jnp.zeros((24, 128), F32)
                        if 0 <= dx <= 2:
                            for cy in range(2):
                                dy = 2 - wcy + cy
                                first = (dy * 3 + dx) * 48
                                if 0 <= dy <= 2 and first < 128 * j + 128 and first + 48 > 128 * j:
                                    match = lane + (128 * j - first - b) == within
                                    keep_row = in_low if cy == 0 else jnp.logical_not(in_low)
                                    hit = jnp.where(match & keep_row, 1.0, hit)
                        bf[24 * px : 24 * px + 24, 512 * side + 128 * j : 512 * side + 128 * j + 128] = hit
            out = dot(bf[...].astype(BF), kpair[...])
            at = 256 * wcy + 128 * pair
            wb1b[:, at : at + 128] = out.astype(BF)

    loads[4].wait()
    one = eye(192)
    for at in range(0, 1600, 256):
        size = min(256, 1600 - at)
        w2t[:, at : at + size] = flip(one, w2n[at : at + size, :])

    arrive(0, plan0)
    shard_send(0, 1)
    for buf, at in ((ru0, 4), (rd0, 72)):
        tmp[...] = buf[...].astype(F32)
        for f in range(2):
            for c in range(3):
                pf[3 * f + c, at : at + 4, :] = tmp[16 * f + 4 * c : 16 * f + 4 * c + 4, :]
    for s, (mid, up, down) in enumerate(((rl0, 0, 2), (rr0, 1, 3))):
        for f in range(2):
            for c in range(3):
                v = mid[8 * c : 8 * c + 8, :]
                for y in range(8):
                    ef[s, 3 * f + c, 8 + 8 * y : 16 + 8 * y, :] = roll(v, -64 * f - 8 * y)
        for corner, at in ((up, 4), (down, 72)):
            tmp[:, :128] = rc0[corner].astype(F32)
            for f in range(2):
                for c in range(3):
                    ef[s, 3 * f + c, at : at + 4, :] = tmp[16 * f + 4 * c : 16 * f + 4 * c + 4, :128]

    def pixels(f):
        for r in range(8):
            for c in range(3):
                rows = slice((r * 3 + c) * 16, (r * 3 + c) * 16 + 16)
                lw[rows, :] = pf[3 * f + c, 8 * r + 4 : 8 * r + 20, :].astype(BF)
                for s in range(2):
                    ew[s, rows, :] = ef[s, 3 * f + c, 8 * r + 4 : 8 * r + 20, :]
        for pp in range(4):
            both = dot(lw[...], sel[:, 256 * pp : 256 * pp + 256])
            for px in (2 * pp, 2 * pp + 1):
                x = both[:, 128 * (px % 2) : 128 * (px % 2) + 128]
                if px >= 4:
                    other = shifted(x, -1)
                    other = jnp.where(lanes(x.shape) == 0, roll(ew[0], -px), other)
                    wx = px - 4
                else:
                    other = shifted(x, 1)
                    other = jnp.where(lanes(x.shape) == 127, roll(ew[1], 127 - px), other)
                    wx = 12 + px
                for w, v in ((4 + px, x), (wx, other)):
                    v = v.astype(BF)
                    for r in range(8):
                        x1[r % 4, 48 * w : 48 * w + 48, 128 * (r // 4) : 128 * (r // 4) + 128] = v[48 * r : 48 * r + 48]

    def silu(v):
        sigma = 0.5 * jnp.tanh(0.5 * v) + 0.5
        return v * sigma, sigma

    def layer_one(f):
        def body(i, _):
            out = dot(wb1[...], x1[i])
            for h in range(2):
                acc = None
                for ph in range(4):
                    v = out[64 * ph : 64 * ph + 64, 128 * h : 128 * h + 128] + cb1[...]
                    feat, sigma = silu(v)
                    n = (i + 4 * h) * 4 + ph
                    f1[f, n] = feat
                    if f == 0:
                        sl1[n] = sigma * (1.0 + v * (1.0 - sigma))
                    acc = feat if acc is None else acc + feat
                pool1[f, 2 + i + 4 * h] = (0.25 * acc).astype(BF)
            return 0

        lax.fori_loop(0, 4, body, 0)

    def pack_columns(rows, side):
        size = side.shape[0]
        acc = jnp.zeros((size, 128), F32)
        lane = lanes((size, 128)) % 64
        for g in range(4):
            for r in range(8):
                x = rows(r, slice(size * g, size * g + size)).astype(F32)
                to = 16 * g + r
                acc = jnp.where(lane == to, roll(x, to), acc)
                acc = jnp.where(lane == to + 8, roll(x, to + 8 - 63), acc)
        side[...] = acc.astype(BF)

    def merged(hs):
        size = hs.shape[1]
        lane = lanes((size, 128)) % 64
        slots = [hs[n].astype(F32) for n in range(6)]
        for g in range(4):
            v = roll(slots[1], 2 - 16 * g)
            v = jnp.where(lane < 2, roll(slots[3], -6 - 16 * g), v)
            v = jnp.where(lane >= 10, roll(slots[5], 10 - 16 * g), v)
            v = jnp.where(lane >= 18, roll(slots[0], 10 - 16 * g), v)
            v = jnp.where((lane >= 16) & (lane < 18), roll(slots[2], 2 - 16 * g), v)
            v = jnp.where(lane >= 26, roll(slots[4], 18 - 16 * g), v)
            hb[size * g : size * g + size, :] = v

    def layer_two_operand(f):
        lane = lanes((64, 128))
        merged(hs1.at[f])
        halo = hb[0:64, :]
        for rr in range(12):
            x = pool1[f, rr].astype(F32)
            right = roll(halo, 63 - rr)
            left = roll(halo, -16 - rr)
            cols = (
                jnp.where(lane % 64 == 0, left, shifted(x, -2)),
                jnp.where(lane == 0, roll(left, 64), shifted(x, -1)),
                x,
                jnp.where(lane == 127, roll(right, 64), shifted(x, 1)),
                jnp.where(lane % 64 == 63, right, shifted(x, 2)),
            )
            for e, v in enumerate(cols):
                v = v.astype(BF)
                if rr < 8:
                    x2[320 * rr + 64 * e : 320 * rr + 64 * e + 64, :128] = v
                if rr >= 4:
                    x2[320 * (rr - 4) + 64 * e : 320 * (rr - 4) + 64 * e + 64, 128:] = v

    def layer_two(f):
        low = lanes((64, 128)) < 64
        for i in range(4):
            out = dot(w2t[...], x2[320 * i : 320 * i + 1600, :])
            for h in range(2):
                for k in range(3):
                    rows = slice(64 * k, 64 * k + 64)
                    v = out[rows, 128 * h : 128 * h + 128] + cb2[rows]
                    feat, sigma = silu(v)
                    f2[f, i + 4 * h, rows] = feat
                    if f == 0:
                        sl2[i + 4 * h, rows] = sigma * (1.0 + v * (1.0 - sigma))
                    if i % 2 == 1:
                        both = f2[f, i - 1 + 4 * h, rows] + feat
                        mean = 0.25 * (both + roll(both, 64))
                        if i == 1:
                            keep[h, rows] = mean
                        else:
                            pool2[f, h, rows] = jnp.where(low, keep[h, rows], mean).astype(BF)

    def pack_ends(tiles, side, up, down):
        size = side.shape[0]
        lane = lanes((size, 128))
        acc = jnp.zeros((size, 128), F32)
        for g in range(12):
            for t in range(2):
                x = tiles[t, size * g : size * g + size, :].astype(F32)
                for r in (2 * t, 2 * t + 1):
                    first = 64 * (r % 2)
                    to = 8 * g + r
                    acc = jnp.where(lane == to, roll(x, to - first), acc)
                    acc = jnp.where(lane == to + 4, roll(x, to + 4 - 63 - first), acc)
        side[...] = acc.astype(BF)
        half = up.shape[0]
        for at in range(0, half, 96):
            rows, others = slice(at, at + 96), slice(half + at, half + at + 96)
            low = lanes((96, 128)) < 64
            up[rows] = jnp.where(
                low, tiles[0, rows].astype(F32), roll(tiles[0, others].astype(F32), 64)
            ).astype(BF)
            down[rows] = jnp.where(
                low, roll(tiles[1, rows].astype(F32), 64), tiles[1, others].astype(F32)
            ).astype(BF)

    def merged_ends(hs):
        size = hs.shape[1]
        lane = lanes((size, 128))
        slots = [hs[n].astype(F32) for n in range(6)]
        for g in range(12):
            v = None
            for first, (mid, up, down), skip in ((0, (1, 3, 5), 0), (16, (0, 2, 4), 4)):
                to = first - 8 * g - skip
                w = roll(slots[mid], to + 1)
                w = jnp.where(lane == first, roll(slots[up], to - 3), w)
                w = jnp.where(lane == first + 5, roll(slots[down], to + 5), w)
                w = jnp.where(lane >= 64, roll(slots[mid], to + 64), w)
                w = jnp.where(lane == first + 68, roll(slots[down], to + 68), w)
                v = w if v is None else jnp.where(lane % 64 < 16, v, w)
            hb[size * g : size * g + size, :] = v

    def layer_three_operand(tiles, from_up, from_down, hs, dst):
        channels = tiles.shape[1]
        half = channels // 2
        merged_ends(hs)
        for at in range(0, channels, 96):
            rows = slice(at, at + 96)
            fold = slice(at % half, at % half + 96)
            lane = lanes((96, 128))
            low = lane < 64
            halo = hb[rows, :]
            b = tiles[0, rows].astype(F32)
            d = tiles[1, rows].astype(F32)
            b_swap, d_swap = roll(b, 64), roll(d, 64)
            above, below = from_up[fold].astype(F32), from_down[fold].astype(F32)
            if at < half:
                below = roll(below, 64)
            else:
                above = roll(above, 64)
            a = jnp.where(low, above, b_swap)
            c = jnp.where(low, b_swap, d_swap)
            e = jnp.where(low, d_swap, below)
            for rr, (x, spots) in enumerate(
                ((a, ((0, 0),)), (b, ((1, 0),)), (c, ((0, 1), (2, 0))), (d, ((1, 1),)), (e, ((2, 1),)))
            ):
                left = jnp.where(lane % 64 == 0, roll(halo, -16 - rr), roll(x, 1))
                right = jnp.where(lane % 64 == 63, roll(halo, 63 - rr), roll(x, 127))
                for dx, v in enumerate((left, x, right)):
                    v = v.astype(BF)
                    for dy, spot in spots:
                        base = (dy * 3 + dx) * channels + at
                        dst[base : base + 96, 128 * spot : 128 * spot + 128] = v

    def layer_three(f):
        out = dot(w3t[...], x3[f])
        for h in range(2):
            for k in range(6):
                rows = slice(64 * k, 64 * k + 64)
                v = out[rows, 128 * h : 128 * h + 128] + cb3[rows]
                feat, sigma = silu(v)
                f3[f, h, rows] = feat
                if f == 0:
                    sl3[h, rows] = sigma * (1.0 + v * (1.0 - sigma))

    def local_terms(feats, n, weights, factor, count, finish):
        chunks = weights.shape[0] // 64
        rows = [slice(64 * k, 64 * k + 64) for k in range(chunks)]
        sums = [jnp.zeros((1, 128), F32)] * 2
        for f in range(2):
            for k in range(chunks):
                v = feats[f, n, rows[k]]
                sums[f] = sums[f] + jnp.sum(v * v, axis=0, keepdims=True)
        first, second = lax.rsqrt(sums[0] + EPSILON), lax.rsqrt(sums[1] + EPSILON)
        inner = jnp.zeros((1, 128), F32)
        total = jnp.zeros((1, 128), F32)
        for k in range(chunks):
            v = feats[0, n, rows[k]]
            differ = v * first - feats[1, n, rows[k]] * second
            slope = weights[rows[k]] * differ
            total = total + jnp.sum(slope * differ, axis=0, keepdims=True)
            inner = inner + jnp.sum(v * slope, axis=0, keepdims=True)
        la[0:1, :] = la[0:1, :] + total * (1.0 / count)
        scale = 2.0 * factor * first
        cubed = 2.0 * factor * first * first * first * inner
        for k in range(chunks):
            v = feats[0, n, rows[k]]
            slope = weights[rows[k]] * (v * first - feats[1, n, rows[k]] * second)
            finish(k, rows[k], scale * slope - v * cubed)

    for f in range(2):
        pixels(f)
        layer_one(f)
        pack_columns(lambda r, rows: pool1[f, 2 + r, rows], se1.at[f])
        start(1 + f, plan1[f])
        shard_send(2 + 2 * f, 3 + 2 * f)
    for f in range(2):
        shard_pass(2 * f, 2 * f + 1)
        arrive(1 + f, plan1[f])
        layer_two_operand(f)
        layer_two(f)
        pack_ends(pool2.at[f], se2.at[f], su2.at[f], sd2.at[f])
        start(3 + f, plan2[f])
    shard_pass(4, 5)
    if n_chan > 1:
        shard_arrive(0, None)
        for part in range(6):
            shard_arrive(2, part)
    for f in range(2):
        arrive(3 + f, plan2[f])
        layer_three_operand(pool2.at[f], ru2.at[f], rd2.at[f], hs2.at[f], x3.at[f])
        layer_three(f)

    pixel_count = 64 * n_tile * 1024 * n_col

    for h in range(2):

        def finish_three(k, rows, dfeat):
            d3[h, rows] = (dfeat * sl3[h, rows]).astype(BF)

        local_terms(f3, h, cl3, 256.0, pixel_count // 256, finish_three)
    pack_ends(d3, se3, su3, sd3)
    start(5, plan3)

    def terms_two(n, _):
        def finish_two(k, rows, dfeat):
            f2[0, n, rows] = dfeat

        local_terms(f2, n, cl2, 64.0, pixel_count // 64, finish_two)
        return 0

    lax.fori_loop(0, 8, terms_two, 0)

    def loss_copy(axis, k):
        which = ("col", "chan", "row").index(axis)
        slots = (lsa, lsb, lsc)[which]
        at, count = ((i_col, n_col), (i_chan, n_chan), (i_row, n_row))[which]
        return pltpu.make_async_remote_copy(
            src_ref=la,
            dst_ref=slots.at[k - 1],
            send_sem=lsend.at[which, k - 1],
            recv_sem=lrecv.at[which, k - 1],
            device_id={axis: (at + k) % count},
            device_id_type=pl.DeviceIdType.MESH,
        )

    def loss_start(axis, count):
        for k in range(1, count):
            loss_copy(axis, k).start()

    def loss_finish(axis, count, slots):
        for k in range(1, count):
            loss_copy(axis, k).wait()
        total = la[...]
        for k in range(1, count):
            total = total + slots[k - 1]
        la[...] = total

    one = eye(128)
    for at in range(0, 1728, 128):
        size = min(128, 1728 - at)
        w3n[at : at + size, :] = flip(one[:size, :size], w3t[:, at : at + size])

    arrive(5, plan3)
    layer_three_operand(d3, ru3, rd3, hs3, x3d)
    acc = None
    for tap in range(9):
        part = dot(w3n[192 * (8 - tap) : 192 * (8 - tap) + 192, :], x3d[384 * tap : 384 * tap + 384, :])
        acc = part if acc is None else acc + part
    dp2[...] = acc

    for r in range(8):
        for k in range(3):
            rows = slice(64 * k, 64 * k + 64)
            t = dp2[rows, 128 * (r // 4) : 128 * (r // 4) + 128]
            low = lanes((64, 128)) < 64
            swap = roll(t, 64)
            wide = jnp.where(low, t, swap) if (r // 2) % 2 == 0 else jnp.where(low, swap, t)
            d2[2 + r, rows] = ((f2[0, r, rows] + 0.25 * wide) * sl2[r, rows]).astype(BF)
    pack_columns(lambda r, rows: d2[2 + r, rows], se4)
    start(6, plan4)

    def terms_one(n, _):
        def finish_one(k, rows, dfeat):
            f1[0, n, rows] = dfeat

        local_terms(f1, n, cl1, 16.0, pixel_count // 16, finish_one)
        return 0

    lax.fori_loop(0, 32, terms_one, 0)

    loss_start("col", n_col)
    arrive(6, plan4)
    for rr in range(12):
        v = d2[rr]
        if rr < 8:
            x4[192 * rr : 192 * rr + 192, :128] = v
        if rr >= 4:
            x4[192 * (rr - 4) : 192 * (rr - 4) + 192, 128:] = v
    merged(hs4)
    for at in range(0, 192, 64):
        halo = hb[at : at + 64, :]
        for dy in range(5):
            xh[192 * dy + at : 192 * dy + at + 64, :] = roll(halo, -dy).astype(BF)
    acc = None
    for dy in range(5):
        part = dot(w2n[320 * (4 - dy) : 320 * (4 - dy) + 320, :], xh[192 * dy : 192 * dy + 192, :])
        acc = part if acc is None else acc + part
    yh[...] = acc
    loss_finish("col", n_col, lsa)
    loss_start("chan", n_chan)
    lane = lanes((64, 128))
    for i in range(4):
        acc = None
        for dy in range(5):
            part = dot(
                w2n[320 * (4 - dy) : 320 * (4 - dy) + 320, :],
                x4[192 * (i + dy) : 192 * (i + dy) + 192, :],
            )
            acc = part if acc is None else acc + part
        yb[...] = acc
        for h in range(2):
            r = i + 4 * h

            def piece(e, src=None):
                if src is None:
                    return yb[64 * (2 - e) : 64 * (2 - e) + 64, 128 * h : 128 * h + 128]
                return yh[64 * (2 - e) : 64 * (2 - e) + 64, :]

            total = piece(0)
            total = total + jnp.where(lane == 127, roll(piece(1, 1), 127 - r), shifted(piece(1), 1))
            total = total + jnp.where(lane % 64 == 63, roll(piece(2, 1), 63 - r), shifted(piece(2), 2))
            total = total + jnp.where(lane == 0, roll(piece(-1, 1), -80 - r), shifted(piece(-1), -1))
            total = total + jnp.where(lane % 64 == 0, roll(piece(-2, 1), -16 - r), shifted(piece(-2), -2))
            total = 0.25 * total
            for py in range(2):
                for px in range(2):
                    n = 4 * r + 2 * py + px
                    d1[2 * r + py, 64 * px : 64 * px + 64] = ((f1[0, n] + total) * sl1[n]).astype(BF)

    lane16 = lanes((16, 128))
    acc = jnp.zeros((16, 128), F32)
    for g in range(4):
        for cr in range(16):
            to = 32 * g + cr
            zero, one = d1[cr, 16 * g : 16 * g + 16], d1[cr, 64 + 16 * g : 80 + 16 * g]
            acc = jnp.where(lane16 == to, roll(zero.astype(F32), to), acc)
            acc = jnp.where(lane16 == to + 16, roll(one.astype(F32), to + 16 - 127), acc)
    se5[...] = acc.astype(BF)
    start(7, plan5)
    loss_finish("chan", n_chan, lsb)
    loss_start("row", n_row)
    arrive(7, plan5)
    slots = [hs5[n].astype(F32) for n in range(6)]
    for g in range(4):
        v = roll(slots[1], 1 - 32 * g)
        v = jnp.where(lane16 == 0, roll(slots[3], -15 - 32 * g), v)
        v = jnp.where(lane16 == 17, roll(slots[5], 17 - 32 * g), v)
        w = roll(slots[0], 17 - 32 * g)
        w = jnp.where(lane16 == 32, roll(slots[2], 1 - 32 * g), w)
        w = jnp.where(lane16 == 49, roll(slots[4], 33 - 32 * g), w)
        hb[16 * g : 16 * g + 16, :] = jnp.where(lane16 < 32, v, w)
    halo = hb[0:64, :]
    for n in range(18):
        src = ru5 if n == 0 else rd5 if n == 17 else d1.at[n - 1]
        zero, one = src[:64], src[64:]
        before = jnp.where(lane == 0, roll(halo, -32 - n), shifted(one.astype(F32), -1)).astype(BF)
        after = jnp.where(lane == 127, roll(halo, 127 - n), shifted(zero.astype(F32), 1)).astype(BF)
        for g, v in enumerate((before, zero, one, after)):
            if n < 10:
                x5[256 * n + 64 * g : 256 * n + 64 * g + 64, :128] = v
            if n >= 8:
                x5[256 * (n - 8) + 64 * g : 256 * (n - 8) + 64 * g + 64, 128:] = v
    for i in range(4):
        out = dot(wb1b[...], x5[512 * i : 512 * i + 1024, :])
        for h in range(2):
            r = i + 4 * h
            for px in range(8):
                for c in range(3):
                    at = px * 24 + c * 8
                    bf[64 * c + 8 * r : 64 * c + 8 * r + 8, 128 * px : 128 * px + 128] = out[
                        at : at + 8, 128 * h : 128 * h + 128
                    ]
    loss_finish("row", n_row, lsc)
    loss[...] = jnp.sum(la[0:1, :], axis=1, keepdims=True)
    planes = bf[...].astype(BF)
    for part in range(4):
        cols = slice(256 * part, 256 * part + 256)
        out = lax.dot_general(planes, sel[cols, :], (((1,), (1,)), ((), ())), preferred_element_type=F32)
        for c in range(3):
            grad[c, :, cols] = out[64 * c : 64 * c + 64].astype(BF)

    drain(0, plan0)
    for f in range(2):
        drain(1 + f, plan1[f])
        drain(3 + f, plan2[f])
    drain(5, plan3)
    drain(6, plan4)
    drain(7, plan5)
    if n_chan > 1:
        shard_copy(0, None).wait_send()
        for part in range(6):
            shard_copy(1, part).wait_send()
            shard_copy(2, part).wait_send()


def local(
    image_gen, image_ref, kernel_one, bias_one, kernel_two, bias_two, kernel_three, bias_three,
    lin_first, lin_second, lin_third,
):
    n_row, n_col, n_chan = lax.axis_size("row"), lax.axis_size("col"), lax.axis_size("chan")
    rows = [v.reshape(1, -1) for v in (bias_one, bias_two, bias_three, lin_first, lin_second, lin_third)]
    V = pltpu.VMEM
    scratch = dict(
        img=V((2, 3, 64, 1024), F32), k1=V((432, 64), BF), w2n=V((1600, 192), BF), k3=V((1728, 96), BF),
        kpair=V((1024, 128), BF), sela=V((432, 768), BF), wb1=V((256, 768), BF), wb1b=V((192, 1024), BF),
        w2t=V((192, 1600), BF),
        sel=V((1024, 1024), BF), pf=V((6, 80, 1024), F32), ef=V((2, 6, 80, 128), F32),
        tmp=V((32, 1024), F32), lw=V((384, 1024), BF), ew=V((2, 384, 128), F32),
        x1=V((4, 768, 256), BF), f1=V((2, 32, 64, 128), F32), sl1=V((32, 64, 128), F32),
        pool1=V((2, 12, 64, 128), BF), x2=V((2560, 256), BF), f2=V((2, 8, 192, 128), F32),
        sl2=V((8, 192, 128), F32), keep=V((2, 192, 128), F32), pool2=V((2, 2, 192, 128), BF),
        x3=V((2, 1728, 256), BF), f3=V((2, 2, 384, 128), F32), sl3=V((2, 384, 128), F32),
        d3=V((2, 384, 128), BF), x3d=V((3456, 256), BF), w3t=V((384, 1728), BF), w3n=V((1728, 384), BF),
        dp2=V((192, 256), F32), d2=V((12, 192, 128), BF), x4=V((1536, 256), BF), yb=V((320, 256), F32),
        xh=V((960, 128), BF), yh=V((320, 128), F32), d1=V((16, 128, 128), BF), x5=V((2560, 256), BF),
        bf=V((192, 1024), F32), hb=V((384, 128), F32), cb1=V((64, 128), F32), cb2=V((192, 128), F32), cb3=V((384, 128), F32),
        cl1=V((64, 128), F32), cl2=V((192, 128), F32), cl3=V((384, 128), F32), la=V((8, 128), F32),
        lsa=V((max(n_col - 1, 1), 8, 128), F32), lsb=V((max(n_chan - 1, 1), 8, 128), F32),
        lsc=V((max(n_row - 1, 1), 8, 128), F32),
        su0=V((32, 1024), BF), sd0=V((32, 1024), BF), se0=V((24, 128), F32), seu=V((32, 128), BF),
        sed=V((32, 128), BF), ru0=V((32, 1024), BF), rd0=V((32, 1024), BF), rl0=V((24, 128), F32),
        rr0=V((24, 128), F32), rc0=V((4, 32, 128), BF),
        se1=V((2, 16, 128), BF), hs1=V((2, 6, 16, 128), BF), se2=V((2, 16, 128), BF),
        hs2=V((2, 6, 16, 128), BF), su2=V((2, 96, 128), BF), sd2=V((2, 96, 128), BF),
        ru2=V((2, 96, 128), BF), rd2=V((2, 96, 128), BF),
        se3=V((32, 128), BF), hs3=V((6, 32, 128), BF), su3=V((192, 128), BF), sd3=V((192, 128), BF),
        ru3=V((192, 128), BF), rd3=V((192, 128), BF),
        se4=V((48, 128), BF), hs4=V((6, 48, 128), BF), se5=V((16, 128), BF), hs5=V((6, 16, 128), BF),
        ru5=V((128, 128), BF), rd5=V((128, 128), BF),
        send_sem=pltpu.SemaphoreType.DMA((STAGES, 8)), recv_sem=pltpu.SemaphoreType.DMA((STAGES, 8)),
        wsend=pltpu.SemaphoreType.DMA((13,)), wrecv=pltpu.SemaphoreType.DMA((13,)),
        lsend=pltpu.SemaphoreType.DMA((3, 8)), lrecv=pltpu.SemaphoreType.DMA((3, 8)),
        in_sem=pltpu.SemaphoreType.DMA((5,)),
    )
    vmem = pl.BlockSpec(memory_space=pltpu.VMEM)
    grad, loss = pl.pallas_call(
        kernel,
        out_shape=(
            jax.ShapeDtypeStruct(image_gen.shape, BF),
            jax.ShapeDtypeStruct((1, 1), F32),
        ),
        in_specs=[pl.BlockSpec(memory_space=pl.ANY)] * 5 + [vmem] * 6,
        out_specs=(vmem, vmem),
        scratch_shapes=list(scratch.values()),
        compiler_params=pltpu.CompilerParams(
            collective_id=0, has_side_effects=True, vmem_limit_bytes=62 * 1024 * 1024
        ),
        name="whole",
    )(
        image_gen, image_ref, kernel_one.reshape(432, 64), kernel_two.reshape(1600, 192),
        kernel_three.reshape(1728, 96), *rows,
    )
    spreads = jnp.array(SPREADS, F32)[:, None, None]
    return (grad.astype(F32) / spreads, loss.reshape(()))


def solution(mesh):
    rows = ("row", "chan")
    in_specs = (
        P(None, rows, "col"), P(None, rows, "col"), P(), P(), P(), P(),
        P(None, None, None, "chan"), P(), P(), P(), P(),
    )
    out_specs = (P(None, rows, "col"), P())
    return jax.shard_map(local, mesh=mesh, in_specs=in_specs, out_specs=out_specs, check_vma=False)
```

```python
import functools

import jax
import jax.numpy as jnp
from jax import lax
from jax.experimental import pallas as pl
from jax.experimental.pallas import tpu as pltpu
from jax.sharding import PartitionSpec as P

OFFSETS = (-0.03, -0.088, -0.188)
SPREADS = (0.458, 0.448, 0.45)
EPSILON = 1e-06
BF = jnp.bfloat16
F32 = jnp.float32
DIRS = ((-1, 0), (1, 0), (0, -1), (0, 1), (-1, -1), (-1, 1), (1, -1), (1, 1))
UP, DOWN, LEFT, RIGHT, UL, UR, DL, DR = range(8)
OPP = (1, 0, 3, 2, 7, 6, 5, 4)
STAGES = 8


def roll(x, shift):
    return pltpu.roll(x, shift % 128, 1)


def dot(a, b):
    return jnp.dot(a, b, preferred_element_type=F32)


def lanes(shape):
    return lax.broadcasted_iota(jnp.int32, shape, 1)


def shifted(x, e):
    low = lanes(x.shape) < 64
    if e == 1:
        return jnp.where(low, roll(x, 64), roll(x, 63))
    if e == -1:
        return jnp.where(low, roll(x, 65), roll(x, 64))
    return roll(x, -e // 2)


def kernel(
    img0_hbm, img1_hbm, k1_hbm, k2_hbm, k3_hbm, b1, b2, b3, l1, l2, l3,
    planes, loss,
    img, k1, w2n, k3, kpair, sela, wb1, wb1b, w2t,
    sel, pf, ef, tmp, lw, ew, x1, f1, sl1, pool1, x2, f2, sl2, keep, pool2, x3,
    f3, sl3, d3, x3d, w3t, w3n, dp2, d2, x4, yb, xh, yh, d1, x5, bf, hb, wends, dp1, xe,
    cb1, cb2, cb3, cl1, cl2, cl3, la, lsa, lsb, lsc,
    su0, sd0, se0, seu, sed, ru0, rd0, rl0, rr0, rc0,
    se1, hs1, se2, hs2, su2, sd2, ru2, rd2, se3, hs3, su3, sd3, ru3, rd3, se4, hs4, se5, hs5, ru5, rd5,
    send_sem, recv_sem, wsend, wrecv, lsend, lrecv, in_sem,
):
    n_row, n_col, n_chan = lax.axis_size("row"), lax.axis_size("col"), lax.axis_size("chan")
    i_row, i_col, i_chan = lax.axis_index("row"), lax.axis_index("col"), lax.axis_index("chan")
    tile = i_row * n_chan + i_chan
    n_tile = n_row * n_chan

    def place(step_t, step_c):
        other = tile + step_t
        return {"row": other // n_chan, "chan": other % n_chan, "col": i_col + step_c}

    def exists(step_t, step_c):
        ok = None
        for step, at, count in ((step_t, tile, n_tile), (step_c, i_col, n_col)):
            if step < 0:
                term = at > 0
            elif step > 0:
                term = at < count - 1
            else:
                continue
            ok = term if ok is None else jnp.logical_and(ok, term)
        return ok

    peers = [("chan", i_chan, n_chan, k) for k in range(1, n_chan)]
    peers += [("col", i_col, n_col, k) for k in range(1, n_col)]
    peers += [("row", i_row, n_row, k) for k in range(1, n_row)]
    far = {"row": i_row + 1 - 2 * (i_row % 2), "chan": (i_chan + 2) % n_chan}
    near = {"chan": i_chan + 1 - 2 * (i_chan % 2)}

    barrier = pltpu.get_barrier_semaphore()

    def greets(d):
        if d in (LEFT, RIGHT):
            return None
        ok = exists(*DIRS[d])
        if d == UP:
            ok = jnp.logical_and(ok, i_chan == 0)
        if d == DOWN:
            ok = jnp.logical_and(ok, i_chan == n_chan - 1)
        return ok

    for d in range(8):
        if greets(d) is not None:

            @pl.when(greets(d))
            def _():
                pl.semaphore_signal(barrier, inc=1, device_id=place(*DIRS[d]), device_id_type=pl.DeviceIdType.MESH)

    loads = [
        pltpu.make_async_copy(src, dst, in_sem.at[n])
        for n, (src, dst) in enumerate(
            (
                (img0_hbm, img.at[0]), (img1_hbm, img.at[1]), (k3_hbm, k3), (k1_hbm, k1), (k2_hbm, w2n),
            )
        )
    ]
    for load in loads:
        load.start()

    for axis, at, count, k in peers:
        pl.semaphore_signal(
            barrier, inc=1, device_id={axis: (at + k) % count}, device_id_type=pl.DeviceIdType.MESH
        )

    if n_chan > 1:
        pl.semaphore_signal(barrier, inc=1, device_id=far, device_id_type=pl.DeviceIdType.MESH)

    def barrier_wait():
        total = jnp.int32(len(peers) + (1 if n_chan > 1 else 0))
        for d in range(8):
            if greets(d) is not None:
                total = total + greets(d).astype(jnp.int32)
        pl.semaphore_wait(barrier, total)

    def copy(stage, d, src, dst):
        return pltpu.make_async_remote_copy(
            src_ref=src,
            dst_ref=dst,
            send_sem=send_sem.at[stage, d],
            recv_sem=recv_sem.at[stage, d],
            device_id=place(*DIRS[d]),
            device_id_type=pl.DeviceIdType.MESH,
        )

    def start(stage, plan):
        for d, (src, dst) in enumerate(plan):

            @pl.when(exists(*DIRS[d]))
            def _():
                copy(stage, d, src, dst).start()

    def arrive(stage, plan):
        for d, (src, dst) in enumerate(plan):
            back = DIRS[OPP[d]]

            @pl.when(exists(*back))
            def _():
                copy(stage, d, src, dst).wait_recv()

            @pl.when(jnp.logical_not(exists(*back)))
            def _():
                dst[...] = jnp.zeros(dst.shape, dst.dtype)

    def drain(stage, plan):
        for d, (src, dst) in enumerate(plan):

            @pl.when(exists(*DIRS[d]))
            def _():
                copy(stage, d, src, dst).wait_send()

    plan0 = [
        (su0, rd0), (sd0, ru0), (se0, rr0), (se0, rl0),
        (seu, rc0.at[3]), (seu, rc0.at[2]), (sed, rc0.at[1]), (sed, rc0.at[0]),
    ]

    def side_plan(up, down, side, hs):
        return [
            up, down, (side, hs.at[1]), (side, hs.at[0]),
            (side, hs.at[5]), (side, hs.at[4]), (side, hs.at[3]), (side, hs.at[2]),
        ]

    plan1 = [
        side_plan(
            (pool1.at[f, pl.ds(2, 2)], pool1.at[f, pl.ds(10, 2)]),
            (pool1.at[f, pl.ds(8, 2)], pool1.at[f, pl.ds(0, 2)]),
            se1.at[f], hs1.at[f],
        )
        for f in range(2)
    ]
    plan2 = [
        side_plan((su2.at[f], rd2.at[f]), (sd2.at[f], ru2.at[f]), se2.at[f], hs2.at[f])
        for f in range(2)
    ]
    plan3 = side_plan((su3, rd3), (sd3, ru3), se3, hs3)
    plan4 = side_plan((d2.at[pl.ds(2, 2)], d2.at[pl.ds(10, 2)]), (d2.at[pl.ds(8, 2)], d2.at[pl.ds(0, 2)]), se4, hs4)
    plan5 = side_plan((d1.at[0], rd5), (d1.at[15], ru5), se5, hs5)

    lane8 = lanes((8, 128))
    for f in range(2):
        loads[f].wait()
        for c in range(3):
            v = ((img[f, c] - OFFSETS[c]) * (1.0 / SPREADS[c])).astype(BF).astype(F32)
            pf[3 * f + c, 8:72, :] = v
    for c in range(3):
        acc = jnp.zeros((8, 128), F32)
        for f in range(2):
            for y in range(8):
                row = pf[3 * f + c, 8 + 8 * y : 16 + 8 * y, :]
                to = 64 * f + 8 * y
                acc = jnp.where((lane8 >= to) & (lane8 < to + 4), roll(row[:, :128], to), acc)
                acc = jnp.where((lane8 >= to + 4) & (lane8 < to + 8), roll(row[:, 896:], to + 8), acc)
        se0[8 * c : 8 * c + 8, :] = acc
    for buf, edge, at in ((su0, seu, 8), (sd0, sed, 68)):
        tmp[...] = jnp.zeros(tmp.shape, F32)
        for f in range(2):
            for c in range(3):
                tmp[16 * f + 4 * c : 16 * f + 4 * c + 4, :] = pf[3 * f + c, at : at + 4, :]
        v = tmp[...]
        buf[...] = v.astype(BF)
        edge[...] = jnp.where(lanes((32, 128)) < 4, v[:, :128], roll(v[:, 896:], 8)).astype(BF)

    barrier_wait()
    start(0, plan0)

    def eye(size):
        rows = lax.broadcasted_iota(jnp.int32, (size, size), 0)
        return jnp.where(rows == lanes((size, size)), 1.0, 0.0).astype(BF)

    def flip(one, block):
        return lax.dot_general(
            one, block, (((1,), (1,)), ((), ())), preferred_element_type=F32
        ).astype(BF)

    loads[2].wait()
    own = pl.ds(pl.multiple_of(i_chan * 96, 32), 96)
    one = eye(96)
    for at in range(0, 1728, 256):
        size = min(256, 1728 - at)
        w3t[own, at : at + size] = flip(one, k3[at : at + size, :])

    def shard_rows(owner, part):
        count = 96 if part is None else 16
        first = owner * 96 + (0 if part is None else 16 * part)
        return w3t.at[pl.ds(pl.multiple_of(first, 16), count)]

    def shard_copy(kind, part):
        rows = shard_rows((i_chan + 2) % n_chan if kind == 2 else i_chan, part)
        at = (0, 1, 7)[kind] + (part or 0)
        return pltpu.make_async_remote_copy(
            src_ref=rows,
            dst_ref=rows,
            send_sem=wsend.at[at],
            recv_sem=wrecv.at[at],
            device_id=far if kind == 1 else near,
            device_id_type=pl.DeviceIdType.MESH,
        )

    def shard_arrive(kind, part):
        owner = (near["chan"], i_chan + 2, near["chan"] + 2)[kind]
        rows = shard_rows(owner % n_chan, part)
        at = (0, 1, 7)[kind] + (part or 0)
        pltpu.make_async_remote_copy(
            src_ref=rows,
            dst_ref=rows,
            send_sem=wsend.at[at],
            recv_sem=wrecv.at[at],
            device_id=far if kind == 1 else near,
            device_id_type=pl.DeviceIdType.MESH,
        ).wait_recv()

    def shard_send(*parts):
        if n_chan > 1:
            for part in parts:
                shard_copy(1, part).start()

    def shard_pass(*parts):
        if n_chan > 1:
            for part in parts:
                shard_arrive(1, part)
                shard_copy(2, part).start()

    if n_chan > 1:
        shard_copy(0, None).start()

    for src, dst in ((b1, cb1), (b2, cb2), (b3, cb3), (l1, cl1), (l2, cl2), (l3, cl3)):
        dst[...] = jnp.transpose(jnp.broadcast_to(src[...].reshape(1, -1), (128, src.shape[0])))
    la[...] = jnp.zeros(la.shape, F32)

    for px in range(8):
        at = lax.broadcasted_iota(jnp.int32, (1024, 128), 0)
        lane = lanes((1024, 128))
        want = 8 * (2 * (lane % 64) + lane // 64) + px
        sel[:, 128 * px : 128 * px + 128] = jnp.where(at == want, 1.0, 0.0).astype(BF)

    loads[3].wait()
    k1t = flip(eye(64), k1[...])
    cell = lax.broadcasted_iota(jnp.int32, (48, 128), 0)
    base = 48 * (cell % 4) + 16 * (cell // 16) + (cell // 4) % 4
    lane = lanes((48, 128))
    for cy in range(2):
        for cx in range(2):
            for tap in range(9):
                want = base + (192 * (tap % 3 + cx) + 4 * (tap // 3 + cy))
                for j in range(6):
                    sela[48 * tap : 48 * tap + 48, 128 * j : 128 * j + 128] = jnp.where(
                        lane + 128 * j == want, 1.0, 0.0
                    ).astype(BF)
            n = 2 * cy + cx
            wb1[64 * n : 64 * n + 64, :] = dot(k1t, sela[...]).astype(BF)

    loads[4].wait()
    one = eye(192)
    for at in range(0, 1600, 256):
        size = min(256, 1600 - at)
        w2t[:, at : at + size] = flip(one, w2n[at : at + size, :])

    arrive(0, plan0)
    shard_send(0, 1)
    for buf, at in ((ru0, 4), (rd0, 72)):
        tmp[...] = buf[...].astype(F32)
        for f in range(2):
            for c in range(3):
                pf[3 * f + c, at : at + 4, :] = tmp[16 * f + 4 * c : 16 * f + 4 * c + 4, :]
    for s, (mid, up, down) in enumerate(((rl0, 0, 2), (rr0, 1, 3))):
        for f in range(2):
            for c in range(3):
                v = mid[8 * c : 8 * c + 8, :]
                for y in range(8):
                    ef[s, 3 * f + c, 8 + 8 * y : 16 + 8 * y, :] = roll(v, -64 * f - 8 * y)
        for corner, at in ((up, 4), (down, 72)):
            tmp[:, :128] = rc0[corner].astype(F32)
            for f in range(2):
                for c in range(3):
                    ef[s, 3 * f + c, at : at + 4, :] = tmp[16 * f + 4 * c : 16 * f + 4 * c + 4, :128]

    def pixels(f):
        for r in range(8):
            for c in range(3):
                rows = slice((r * 3 + c) * 16, (r * 3 + c) * 16 + 16)
                lw[rows, :] = pf[3 * f + c, 8 * r + 4 : 8 * r + 20, :].astype(BF)
                for s in range(2):
                    ew[s, rows, :] = ef[s, 3 * f + c, 8 * r + 4 : 8 * r + 20, :]
        for pp in range(4):
            both = dot(lw[...], sel[:, 256 * pp : 256 * pp + 256])
            for px in (2 * pp, 2 * pp + 1):
                x = both[:, 128 * (px % 2) : 128 * (px % 2) + 128]
                if px >= 4:
                    other = shifted(x, -1)
                    other = jnp.where(lanes(x.shape) == 0, roll(ew[0], -px), other)
                    wx = px - 4
                else:
                    other = shifted(x, 1)
                    other = jnp.where(lanes(x.shape) == 127, roll(ew[1], 127 - px), other)
                    wx = 12 + px
                for w, v in ((4 + px, x), (wx, other)):
                    v = v.astype(BF)
                    for r in range(8):
                        x1[r % 4, 48 * w : 48 * w + 48, 128 * (r // 4) : 128 * (r // 4) + 128] = v[48 * r : 48 * r + 48]

    def silu(v):
        sigma = 0.5 * jnp.tanh(0.5 * v) + 0.5
        return v * sigma, sigma

    def layer_one(f):
        def body(i, _):
            out = dot(wb1[...], x1[i])
            for h in range(2):
                acc = None
                for ph in range(4):
                    v = out[64 * ph : 64 * ph + 64, 128 * h : 128 * h + 128] + cb1[...]
                    feat, sigma = silu(v)
                    n = (i + 4 * h) * 4 + ph
                    f1[f, n] = feat
                    if f == 0:
                        sl1[n] = sigma * (1.0 + v * (1.0 - sigma))
                    acc = feat if acc is None else acc + feat
                pool1[f, 2 + i + 4 * h] = (0.25 * acc).astype(BF)
            return 0

        lax.fori_loop(0, 4, body, 0)

    def pack_columns(rows, side):
        size = side.shape[0]
        acc = jnp.zeros((size, 128), F32)
        lane = lanes((size, 128)) % 64
        for g in range(4):
            for r in range(8):
                x = rows(r, slice(size * g, size * g + size)).astype(F32)
                to = 16 * g + r
                acc = jnp.where(lane == to, roll(x, to), acc)
                acc = jnp.where(lane == to + 8, roll(x, to + 8 - 63), acc)
        side[...] = acc.astype(BF)

    def merged(hs):
        size = hs.shape[1]
        lane = lanes((size, 128)) % 64
        slots = [hs[n].astype(F32) for n in range(6)]
        for g in range(4):
            v = roll(slots[1], 2 - 16 * g)
            v = jnp.where(lane < 2, roll(slots[3], -6 - 16 * g), v)
            v = jnp.where(lane >= 10, roll(slots[5], 10 - 16 * g), v)
            v = jnp.where(lane >= 18, roll(slots[0], 10 - 16 * g), v)
            v = jnp.where((lane >= 16) & (lane < 18), roll(slots[2], 2 - 16 * g), v)
            v = jnp.where(lane >= 26, roll(slots[4], 18 - 16 * g), v)
            hb[size * g : size * g + size, :] = v

    def layer_two_operand(f):
        lane = lanes((64, 128))
        merged(hs1.at[f])
        halo = hb[0:64, :]
        for rr in range(12):
            x = pool1[f, rr].astype(F32)
            right = roll(halo, 63 - rr)
            left = roll(halo, -16 - rr)
            cols = (
                jnp.where(lane % 64 == 0, left, shifted(x, -2)),
                jnp.where(lane == 0, roll(left, 64), shifted(x, -1)),
                x,
                jnp.where(lane == 127, roll(right, 64), shifted(x, 1)),
                jnp.where(lane % 64 == 63, right, shifted(x, 2)),
            )
            for e, v in enumerate(cols):
                v = v.astype(BF)
                if rr < 8:
                    x2[320 * rr + 64 * e : 320 * rr + 64 * e + 64, :128] = v
                if rr >= 4:
                    x2[320 * (rr - 4) + 64 * e : 320 * (rr - 4) + 64 * e + 64, 128:] = v

    def layer_two(f):
        low = lanes((64, 128)) < 64
        for i in range(4):
            out = dot(w2t[...], x2[320 * i : 320 * i + 1600, :])
            for h in range(2):
                for k in range(3):
                    rows = slice(64 * k, 64 * k + 64)
                    v = out[rows, 128 * h : 128 * h + 128] + cb2[rows]
                    feat, sigma = silu(v)
                    f2[f, i + 4 * h, rows] = feat
                    if f == 0:
                        sl2[i + 4 * h, rows] = sigma * (1.0 + v * (1.0 - sigma))
                    if i % 2 == 1:
                        both = f2[f, i - 1 + 4 * h, rows] + feat
                        mean = 0.25 * (both + roll(both, 64))
                        if i == 1:
                            keep[h, rows] = mean
                        else:
                            pool2[f, h, rows] = jnp.where(low, keep[h, rows], mean).astype(BF)

    def pack_ends(tiles, side, up, down):
        size = side.shape[0]
        lane = lanes((size, 128))
        acc = jnp.zeros((size, 128), F32)
        for g in range(12):
            for t in range(2):
                x = tiles[t, size * g : size * g + size, :].astype(F32)
                for r in (2 * t, 2 * t + 1):
                    first = 64 * (r % 2)
                    to = 8 * g + r
                    acc = jnp.where(lane == to, roll(x, to - first), acc)
                    acc = jnp.where(lane == to + 4, roll(x, to + 4 - 63 - first), acc)
        side[...] = acc.astype(BF)
        half = up.shape[0]
        for at in range(0, half, 96):
            rows, others = slice(at, at + 96), slice(half + at, half + at + 96)
            low = lanes((96, 128)) < 64
            up[rows] = jnp.where(
                low, tiles[0, rows].astype(F32), roll(tiles[0, others].astype(F32), 64)
            ).astype(BF)
            down[rows] = jnp.where(
                low, roll(tiles[1, rows].astype(F32), 64), tiles[1, others].astype(F32)
            ).astype(BF)

    def merged_ends(hs):
        size = hs.shape[1]
        lane = lanes((size, 128))
        slots = [hs[n].astype(F32) for n in range(6)]
        for g in range(12):
            v = None
            for first, (mid, up, down), skip in ((0, (1, 3, 5), 0), (16, (0, 2, 4), 4)):
                to = first - 8 * g - skip
                w = roll(slots[mid], to + 1)
                w = jnp.where(lane == first, roll(slots[up], to - 3), w)
                w = jnp.where(lane == first + 5, roll(slots[down], to + 5), w)
                w = jnp.where(lane >= 64, roll(slots[mid], to + 64), w)
                w = jnp.where(lane == first + 68, roll(slots[down], to + 68), w)
                v = w if v is None else jnp.where(lane % 64 < 16, v, w)
            hb[size * g : size * g + size, :] = v

    def layer_three_operand(tiles, from_up, from_down, hs, dst):
        channels = tiles.shape[1]
        half = channels // 2
        merged_ends(hs)
        for at in range(0, channels, 96):
            rows = slice(at, at + 96)
            fold = slice(at % half, at % half + 96)
            lane = lanes((96, 128))
            low = lane < 64
            halo = hb[rows, :]
            b = tiles[0, rows].astype(F32)
            d = tiles[1, rows].astype(F32)
            b_swap, d_swap = roll(b, 64), roll(d, 64)
            above, below = from_up[fold].astype(F32), from_down[fold].astype(F32)
            if at < half:
                below = roll(below, 64)
            else:
                above = roll(above, 64)
            a = jnp.where(low, above, b_swap)
            c = jnp.where(low, b_swap, d_swap)
            e = jnp.where(low, d_swap, below)
            for rr, (x, spots) in enumerate(
                ((a, ((0, 0),)), (b, ((1, 0),)), (c, ((0, 1), (2, 0))), (d, ((1, 1),)), (e, ((2, 1),)))
            ):
                left = jnp.where(lane % 64 == 0, roll(halo, -16 - rr), roll(x, 1))
                right = jnp.where(lane % 64 == 63, roll(halo, 63 - rr), roll(x, 127))
                for dx, v in enumerate((left, x, right)):
                    v = v.astype(BF)
                    for dy, spot in spots:
                        base = (dy * 3 + dx) * channels + at
                        dst[base : base + 96, 128 * spot : 128 * spot + 128] = v

    def layer_three(f):
        out = dot(w3t[...], x3[f])
        for h in range(2):
            for k in range(6):
                rows = slice(64 * k, 64 * k + 64)
                v = out[rows, 128 * h : 128 * h + 128] + cb3[rows]
                feat, sigma = silu(v)
                f3[f, h, rows] = feat
                if f == 0:
                    sl3[h, rows] = sigma * (1.0 + v * (1.0 - sigma))

    def local_terms(feats, n, weights, factor, count, finish):
        chunks = weights.shape[0] // 64
        rows = [slice(64 * k, 64 * k + 64) for k in range(chunks)]
        sums = [jnp.zeros((1, 128), F32)] * 2
        for f in range(2):
            for k in range(chunks):
                v = feats[f, n, rows[k]]
                sums[f] = sums[f] + jnp.sum(v * v, axis=0, keepdims=True)
        first, second = lax.rsqrt(sums[0] + EPSILON), lax.rsqrt(sums[1] + EPSILON)
        inner = jnp.zeros((1, 128), F32)
        total = jnp.zeros((1, 128), F32)
        for k in range(chunks):
            v = feats[0, n, rows[k]]
            differ = v * first - feats[1, n, rows[k]] * second
            slope = weights[rows[k]] * differ
            total = total + jnp.sum(slope * differ, axis=0, keepdims=True)
            inner = inner + jnp.sum(v * slope, axis=0, keepdims=True)
        la[0:1, :] = la[0:1, :] + total * (1.0 / count)
        scale = 2.0 * factor * first
        cubed = 2.0 * factor * first * first * first * inner
        for k in range(chunks):
            v = feats[0, n, rows[k]]
            slope = weights[rows[k]] * (v * first - feats[1, n, rows[k]] * second)
            finish(k, rows[k], scale * slope - v * cubed)

    for f in range(2):
        pixels(f)
        layer_one(f)
        pack_columns(lambda r, rows: pool1[f, 2 + r, rows], se1.at[f])
        start(1 + f, plan1[f])
        shard_send(2 + 2 * f, 3 + 2 * f)
    kpair[...] = jnp.zeros(kpair.shape, BF)
    half = k1[...].astype(F32)
    both = jnp.concatenate([half, half], axis=1)
    low = lanes((432, 128)) < 64
    kpair[0:432, :] = jnp.where(low, both, 0.0).astype(BF)
    kpair[512:944, :] = jnp.where(low, 0.0, both).astype(BF)
    spot = lax.broadcasted_iota(jnp.int32, (24, 128), 0)
    lane = lanes((24, 128))
    in_low = (spot // 4) % 2 == 0
    within = 16 * (spot // 8) + 4 * (spot % 4)
    for wcy in range(4):
        for pair in range(2):
            for px in range(8):
                cx, b = px // 4, px % 4
                for side in range(2):
                    dx = 2 - (2 * pair + side) + cx
                    for j in range(4):
                        hit = jnp.zeros((24, 128), F32)
                        if 0 <= dx <= 2:
                            for cy in range(2):
                                dy = 2 - wcy + cy
                                first = (dy * 3 + dx) * 48
                                if 0 <= dy <= 2 and first < 128 * j + 128 and first + 48 > 128 * j:
                                    match = lane + (128 * j - first - b) == within
                                    keep_row = in_low if cy == 0 else jnp.logical_not(in_low)
                                    hit = jnp.where(match & keep_row, 1.0, hit)
                        bf[24 * px : 24 * px + 24, 512 * side + 128 * j : 512 * side + 128 * j + 128] = hit
            out = dot(bf[...].astype(BF), kpair[...])
            at = 256 * wcy + 128 * pair
            wb1b[:, at : at + 128] = out.astype(BF)

    for side in range(2):
        at = 96 * side
        wends[side] = jnp.concatenate(
            [wb1b[at : at + 96, 256 * w + 192 * side : 256 * w + 192 * side + 64].astype(F32) for w in range(4)], axis=1
        ).astype(BF)

    for f in range(2):
        shard_pass(2 * f, 2 * f + 1)
        arrive(1 + f, plan1[f])
        layer_two_operand(f)
        layer_two(f)
        pack_ends(pool2.at[f], se2.at[f], su2.at[f], sd2.at[f])
        start(3 + f, plan2[f])
    shard_pass(4, 5)
    pixel_count = 64 * n_tile * 1024 * n_col

    def terms_two(n, _):
        def finish_two(k, rows, dfeat):
            f2[0, n, rows] = dfeat

        local_terms(f2, n, cl2, 64.0, pixel_count // 64, finish_two)
        return 0

    lax.fori_loop(0, 8, terms_two, 0)

    def terms_one(n, _):
        def finish_one(k, rows, dfeat):
            f1[0, n, rows] = dfeat

        local_terms(f1, n, cl1, 16.0, pixel_count // 16, finish_one)
        return 0

    lax.fori_loop(0, 32, terms_one, 0)

    if n_chan > 1:
        shard_arrive(0, None)
        for part in range(6):
            shard_arrive(2, part)
    for f in range(2):
        arrive(3 + f, plan2[f])
        layer_three_operand(pool2.at[f], ru2.at[f], rd2.at[f], hs2.at[f], x3.at[f])
        layer_three(f)

    def loss_copy(axis, k):
        which = ("col", "chan", "row").index(axis)
        slots = (lsa, lsb, lsc)[which]
        at, count = ((i_col, n_col), (i_chan, n_chan), (i_row, n_row))[which]
        return pltpu.make_async_remote_copy(
            src_ref=la,
            dst_ref=slots.at[k - 1],
            send_sem=lsend.at[which, k - 1],
            recv_sem=lrecv.at[which, k - 1],
            device_id={axis: (at + k) % count},
            device_id_type=pl.DeviceIdType.MESH,
        )

    def loss_start(axis, count):
        for k in range(1, count):
            loss_copy(axis, k).start()

    def loss_finish(axis, count, slots):
        for k in range(1, count):
            loss_copy(axis, k).wait()
        total = la[...]
        for k in range(1, count):
            total = total + slots[k - 1]
        la[...] = total

    for h in range(2):

        def finish_three(k, rows, dfeat):
            d3[h, rows] = (dfeat * sl3[h, rows]).astype(BF)

        local_terms(f3, h, cl3, 256.0, pixel_count // 256, finish_three)
    pack_ends(d3, se3, su3, sd3)
    start(5, plan3)
    loss_start("col", n_col)


    one = eye(128)
    for at in range(0, 1728, 128):
        size = min(128, 1728 - at)
        w3n[at : at + size, :] = flip(one[:size, :size], w3t[:, at : at + size])

    arrive(5, plan3)
    loss_finish("col", n_col, lsa)
    loss_start("chan", n_chan)
    layer_three_operand(d3, ru3, rd3, hs3, x3d)
    acc = None
    for tap in range(9):
        part = dot(w3n[192 * (8 - tap) : 192 * (8 - tap) + 192, :], x3d[384 * tap : 384 * tap + 384, :])
        acc = part if acc is None else acc + part
    dp2[...] = acc

    for r in range(8):
        for k in range(3):
            rows = slice(64 * k, 64 * k + 64)
            t = dp2[rows, 128 * (r // 4) : 128 * (r // 4) + 128]
            low = lanes((64, 128)) < 64
            swap = roll(t, 64)
            wide = jnp.where(low, t, swap) if (r // 2) % 2 == 0 else jnp.where(low, swap, t)
            d2[2 + r, rows] = ((f2[0, r, rows] + 0.25 * wide) * sl2[r, rows]).astype(BF)
    pack_columns(lambda r, rows: d2[2 + r, rows], se4)
    start(6, plan4)

    zero = jnp.zeros((192, 128), BF)
    for rr in range(12):
        v = d2[rr] if 2 <= rr < 10 else zero
        if rr < 8:
            x4[192 * rr : 192 * rr + 192, :128] = v
        if rr >= 4:
            x4[192 * (rr - 4) : 192 * (rr - 4) + 192, 128:] = v
    lane = lanes((64, 128))

    def joined(pick):
        total = pick(0)
        for e, edge in ((1, lane == 127), (-1, lane == 0), (2, lane % 64 == 63), (-2, lane % 64 == 0)):
            total = total + jnp.where(edge, 0.0, shifted(pick(e), e))
        return total

    def taps(operand, pairs):
        acc = None
        for dy, block in pairs:
            part = dot(w2n[320 * (4 - dy) : 320 * (4 - dy) + 320, :], operand(block))
            acc = part if acc is None else acc + part
        return acc

    for i in range(4):
        yb[...] = taps(lambda n: x4[192 * n : 192 * n + 192, :], [(dy, i + dy) for dy in range(5)])
        for h in range(2):
            dp1[i + 4 * h] = joined(
                lambda e: yb[64 * (2 - e) : 64 * (2 - e) + 64, 128 * h : 128 * h + 128]
            )

    arrive(6, plan4)
    loss_finish("chan", n_chan, lsb)
    loss_start("row", n_row)
    merged(hs4)
    for at in range(0, 192, 64):
        halo = hb[at : at + 64, :]
        for dy in range(5):
            xh[192 * dy + at : 192 * dy + at + 64, :] = roll(halo, -dy).astype(BF)
    yh[...] = taps(lambda n: xh[192 * n : 192 * n + 192, :], [(dy, dy) for dy in range(5)])
    for n, v in enumerate((d2[0], d2[1], d2[1], zero, d2[10], d2[11], zero, d2[10])):
        xe[192 * (n // 2) : 192 * (n // 2) + 192, 128 * (n % 2) : 128 * (n % 2) + 128] = v
    for first, pairs in ((0, ((0, 0), (1, 1))), (6, ((4, 2), (3, 3)))):
        yb[...] = taps(lambda n: xe[192 * n : 192 * n + 192, :], pairs)
        for h in range(2):
            dp1[first + h] = dp1[first + h] + joined(
                lambda e: yb[64 * (2 - e) : 64 * (2 - e) + 64, 128 * h : 128 * h + 128]
            )
    for r in range(8):

        def side(e):
            return yh[64 * (2 - e) : 64 * (2 - e) + 64, :]

        total = dp1[r]
        total = total + jnp.where(lane == 127, roll(side(1), 127 - r), 0.0)
        total = total + jnp.where(lane % 64 == 63, roll(side(2), 63 - r), 0.0)
        total = total + jnp.where(lane == 0, roll(side(-1), -80 - r), 0.0)
        total = total + jnp.where(lane % 64 == 0, roll(side(-2), -16 - r), 0.0)
        total = 0.25 * total
        for py in range(2):
            for px in range(2):
                n = 4 * r + 2 * py + px
                d1[2 * r + py, 64 * px : 64 * px + 64] = ((f1[0, n] + total) * sl1[n]).astype(BF)

    lane16 = lanes((16, 128))
    acc = jnp.zeros((16, 128), F32)
    for g in range(4):
        for cr in range(16):
            to = 32 * g + cr
            zero, one = d1[cr, 16 * g : 16 * g + 16], d1[cr, 64 + 16 * g : 80 + 16 * g]
            acc = jnp.where(lane16 == to, roll(zero.astype(F32), to), acc)
            acc = jnp.where(lane16 == to + 16, roll(one.astype(F32), to + 16 - 127), acc)
    se5[...] = acc.astype(BF)
    start(7, plan5)

    def beside(src):
        zero, one = src[:64], src[64:]
        before = jnp.where(lane == 0, 0.0, shifted(one.astype(F32), -1)).astype(BF)
        after = jnp.where(lane == 127, 0.0, shifted(zero.astype(F32), 1)).astype(BF)
        return before, zero, one, after

    for n in range(18):
        if n in (0, 17):
            cols = (jnp.zeros((64, 128), BF),) * 4
        else:
            cols = beside(d1.at[n - 1])
        for g, v in enumerate(cols):
            if n < 10:
                x5[256 * n + 64 * g : 256 * n + 64 * g + 64, :128] = v
            if n >= 8:
                x5[256 * (n - 8) + 64 * g : 256 * (n - 8) + 64 * g + 64, 128:] = v

    def spots(r):
        for px in range(8):
            for c in range(3):
                yield px * 24 + c * 8, 64 * c + 8 * r, 128 * px

    for i in range(4):
        out = dot(wb1b[...], x5[512 * i : 512 * i + 1024, :])
        for h in range(2):
            for at, row, col in spots(i + 4 * h):
                bf[row : row + 8, col : col + 128] = out[at : at + 8, 128 * h : 128 * h + 128]

    arrive(7, plan5)
    slots = [hs5[n].astype(F32) for n in range(6)]
    for g in range(4):
        v = roll(slots[1], 1 - 32 * g)
        v = jnp.where(lane16 == 0, roll(slots[3], -15 - 32 * g), v)
        v = jnp.where(lane16 == 17, roll(slots[5], 17 - 32 * g), v)
        w = roll(slots[0], 17 - 32 * g)
        w = jnp.where(lane16 == 32, roll(slots[2], 1 - 32 * g), w)
        w = jnp.where(lane16 == 49, roll(slots[4], 33 - 32 * g), w)
        hb[16 * g : 16 * g + 16, :] = jnp.where(lane16 < 32, v, w)
    for r, src, at in ((0, ru5, 0), (7, rd5, 768)):
        out = dot(wb1b[:, at : at + 256], jnp.concatenate(beside(src), axis=0))
        for at, row, col in spots(r):
            bf[row : row + 8, col : col + 128] = bf[row : row + 8, col : col + 128] + out[at : at + 8]
    halo = hb[0:64, :]
    stack = jnp.concatenate([roll(halo, -w).astype(BF) for w in range(4)], axis=0)
    for side, (first, edge) in enumerate(((32, 0), (0, 127))):
        yh[0:96, :] = dot(wends[side], stack)
        for r in range(8):
            for at, row, col in spots(r):
                if at // 96 == side:
                    part = roll(yh[at - 96 * side : at - 96 * side + 8, :], edge - first - 2 * r)
                    bf[row : row + 8, col : col + 128] = bf[row : row + 8, col : col + 128] + jnp.where(
                        lane8 == edge, part, 0.0
                    )
    loss_finish("row", n_row, lsc)
    loss[...] = jnp.sum(la[0:1, :], axis=1, keepdims=True)
    planes[...] = bf[...].astype(BF)

    drain(0, plan0)
    for f in range(2):
        drain(1 + f, plan1[f])
        drain(3 + f, plan2[f])
    drain(5, plan3)
    drain(6, plan4)
    drain(7, plan5)
    if n_chan > 1:
        shard_copy(0, None).wait_send()
        for part in range(6):
            shard_copy(1, part).wait_send()
            shard_copy(2, part).wait_send()


def to_pixels(planes, grad, want):
    @pl.when(pl.program_id(0) == 0)
    def _():
        at = lax.broadcasted_iota(jnp.int32, (1024, 128), 0)
        want[...] = 8 * (2 * (at % 64) + (at // 64) % 2) + at // 128 - lanes((1024, 128))

    first = 256 * pl.program_id(0)
    spread = jnp.concatenate(
        [jnp.where(want[...] == first + 128 * j, 1.0, 0.0).astype(BF) for j in range(2)], axis=1
    )
    out = dot(planes[...], spread)
    for c in range(3):
        grad[c] = out[64 * c : 64 * c + 64] * (1.0 / SPREADS[c])


def local(
    image_gen, image_ref, kernel_one, bias_one, kernel_two, bias_two, kernel_three, bias_three,
    lin_first, lin_second, lin_third,
):
    n_row, n_col, n_chan = lax.axis_size("row"), lax.axis_size("col"), lax.axis_size("chan")
    rows = (bias_one, bias_two, bias_three, lin_first, lin_second, lin_third)
    V = pltpu.VMEM
    scratch = dict(
        img=V((2, 3, 64, 1024), F32), k1=V((432, 64), BF), w2n=V((1600, 192), BF), k3=V((1728, 96), BF),
        kpair=V((1024, 128), BF), sela=V((432, 768), BF), wb1=V((256, 768), BF), wb1b=V((192, 1024), BF),
        w2t=V((192, 1600), BF),
        sel=V((1024, 1024), BF), pf=V((6, 80, 1024), F32), ef=V((2, 6, 80, 128), F32),
        tmp=V((32, 1024), F32), lw=V((384, 1024), BF), ew=V((2, 384, 128), F32),
        x1=V((4, 768, 256), BF), f1=V((2, 32, 64, 128), F32), sl1=V((32, 64, 128), F32),
        pool1=V((2, 12, 64, 128), BF), x2=V((2560, 256), BF), f2=V((2, 8, 192, 128), F32),
        sl2=V((8, 192, 128), F32), keep=V((2, 192, 128), F32), pool2=V((2, 2, 192, 128), BF),
        x3=V((2, 1728, 256), BF), f3=V((2, 2, 384, 128), F32), sl3=V((2, 384, 128), F32),
        d3=V((2, 384, 128), BF), x3d=V((3456, 256), BF), w3t=V((384, 1728), BF), w3n=V((1728, 384), BF),
        dp2=V((192, 256), F32), d2=V((12, 192, 128), BF), x4=V((1536, 256), BF), yb=V((320, 256), F32),
        xh=V((960, 128), BF), yh=V((320, 128), F32), d1=V((16, 128, 128), BF), x5=V((2560, 256), BF),
        bf=V((192, 1024), F32), hb=V((384, 128), F32), wends=V((2, 96, 256), BF), dp1=V((8, 64, 128), F32),
        xe=V((768, 256), BF), cb1=V((64, 128), F32), cb2=V((192, 128), F32), cb3=V((384, 128), F32),
        cl1=V((64, 128), F32), cl2=V((192, 128), F32), cl3=V((384, 128), F32), la=V((8, 128), F32),
        lsa=V((max(n_col - 1, 1), 8, 128), F32), lsb=V((max(n_chan - 1, 1), 8, 128), F32),
        lsc=V((max(n_row - 1, 1), 8, 128), F32),
        su0=V((32, 1024), BF), sd0=V((32, 1024), BF), se0=V((24, 128), F32), seu=V((32, 128), BF),
        sed=V((32, 128), BF), ru0=V((32, 1024), BF), rd0=V((32, 1024), BF), rl0=V((24, 128), F32),
        rr0=V((24, 128), F32), rc0=V((4, 32, 128), BF),
        se1=V((2, 16, 128), BF), hs1=V((2, 6, 16, 128), BF), se2=V((2, 16, 128), BF),
        hs2=V((2, 6, 16, 128), BF), su2=V((2, 96, 128), BF), sd2=V((2, 96, 128), BF),
        ru2=V((2, 96, 128), BF), rd2=V((2, 96, 128), BF),
        se3=V((32, 128), BF), hs3=V((6, 32, 128), BF), su3=V((192, 128), BF), sd3=V((192, 128), BF),
        ru3=V((192, 128), BF), rd3=V((192, 128), BF),
        se4=V((48, 128), BF), hs4=V((6, 48, 128), BF), se5=V((16, 128), BF), hs5=V((6, 16, 128), BF),
        ru5=V((128, 128), BF), rd5=V((128, 128), BF),
        send_sem=pltpu.SemaphoreType.DMA((STAGES, 8)), recv_sem=pltpu.SemaphoreType.DMA((STAGES, 8)),
        wsend=pltpu.SemaphoreType.DMA((13,)), wrecv=pltpu.SemaphoreType.DMA((13,)),
        lsend=pltpu.SemaphoreType.DMA((3, 8)), lrecv=pltpu.SemaphoreType.DMA((3, 8)),
        in_sem=pltpu.SemaphoreType.DMA((5,)),
    )
    vmem = pl.BlockSpec(memory_space=pltpu.VMEM)
    planes, loss = pl.pallas_call(
        kernel,
        out_shape=(
            jax.ShapeDtypeStruct((192, 1024), BF),
            jax.ShapeDtypeStruct((1, 1), F32),
        ),
        in_specs=[pl.BlockSpec(memory_space=pl.ANY)] * 5 + [vmem] * 6,
        out_specs=(vmem, vmem),
        scratch_shapes=list(scratch.values()),
        compiler_params=pltpu.CompilerParams(
            collective_id=0, has_side_effects=True, vmem_limit_bytes=62 * 1024 * 1024
        ),
        name="whole",
    )(
        image_gen, image_ref, kernel_one.reshape(432, 64), kernel_two.reshape(1600, 192),
        kernel_three.reshape(1728, 96), *rows,
    )
    grad = pl.pallas_call(
        to_pixels,
        out_shape=jax.ShapeDtypeStruct(image_gen.shape, F32),
        grid=(4,),
        in_specs=[pl.BlockSpec((192, 1024), lambda n: (0, 0))],
        out_specs=pl.BlockSpec((3, 64, 256), lambda n: (0, 0, n)),
        scratch_shapes=[pltpu.VMEM((1024, 128), jnp.int32)],
        name="pixels",
    )(planes)
    return (grad, loss.reshape(()))


def solution(mesh):
    rows = ("row", "chan")
    in_specs = (
        P(None, rows, "col"), P(None, rows, "col"), P(), P(), P(), P(),
        P(None, None, None, "chan"), P(), P(), P(), P(),
    )
    out_specs = (P(None, rows, "col"), P())
    return jax.shard_map(local, mesh=mesh, in_specs=in_specs, out_specs=out_specs, check_vma=False)
```

```python
import functools

import jax
import jax.numpy as jnp
from jax import lax
from jax.experimental import pallas as pl
from jax.experimental.pallas import tpu as pltpu
from jax.sharding import PartitionSpec as P

OFFSETS = (-0.03, -0.088, -0.188)
SPREADS = (0.458, 0.448, 0.45)
EPSILON = 1e-06
BF = jnp.bfloat16
F32 = jnp.float32
DIRS = ((-1, 0), (1, 0), (0, -1), (0, 1), (-1, -1), (-1, 1), (1, -1), (1, 1))
UP, DOWN, LEFT, RIGHT, UL, UR, DL, DR = range(8)
OPP = (1, 0, 3, 2, 7, 6, 5, 4)
STAGES = 8


def roll(x, shift):
    return pltpu.roll(x, shift % 128, 1)


def dot(a, b):
    return jnp.dot(a, b, preferred_element_type=F32)


def lanes(shape):
    return lax.broadcasted_iota(jnp.int32, shape, 1)


def shifted(x, e):
    low = lanes(x.shape) < 64
    if e == 1:
        return jnp.where(low, roll(x, 64), roll(x, 63))
    if e == -1:
        return jnp.where(low, roll(x, 65), roll(x, 64))
    return roll(x, -e // 2)


def kernel(
    img0_hbm, img1_hbm, k1_hbm, k2_hbm, k3_hbm, b1, b2, b3, l1, l2, l3,
    planes, loss,
    img, k1, w2n, k3, kpair, sela, wb1, wb1b, w2t,
    sel, pf, ef, tmp, lw, ew, x1, f1, sl1, pool1, x2, f2, sl2, keep, pool2, x3,
    f3, sl3, d3, x3d, w3t, w3n, dp2, d2, x4, yb, xh, yh, d1, x5, bf, hb, wends, dp1, xe,
    cb1, cb2, cb3, cl1, cl2, cl3, la, lsa, lsb, lsc,
    su0, sd0, se0, seu, sed, ru0, rd0, rl0, rr0, rc0,
    se1, hs1, se2, hs2, su2, sd2, ru2, rd2, se3, hs3, su3, sd3, ru3, rd3, se4, hs4, se5, hs5, ru5, rd5,
    send_sem, recv_sem, wsend, wrecv, lsend, lrecv, in_sem,
):
    n_row, n_col, n_chan = lax.axis_size("row"), lax.axis_size("col"), lax.axis_size("chan")
    i_row, i_col, i_chan = lax.axis_index("row"), lax.axis_index("col"), lax.axis_index("chan")
    tile = i_row * n_chan + i_chan
    n_tile = n_row * n_chan

    def place(step_t, step_c):
        other = tile + step_t
        return {"row": other // n_chan, "chan": other % n_chan, "col": i_col + step_c}

    def exists(step_t, step_c):
        ok = None
        for step, at, count in ((step_t, tile, n_tile), (step_c, i_col, n_col)):
            if step < 0:
                term = at > 0
            elif step > 0:
                term = at < count - 1
            else:
                continue
            ok = term if ok is None else jnp.logical_and(ok, term)
        return ok

    peers = [("chan", i_chan, n_chan, k) for k in range(1, n_chan)]
    peers += [("col", i_col, n_col, k) for k in range(1, n_col)]
    peers += [("row", i_row, n_row, k) for k in range(1, n_row)]
    far = {"row": i_row + 1 - 2 * (i_row % 2), "chan": (i_chan + 2) % n_chan}
    near = {"chan": i_chan + 1 - 2 * (i_chan % 2)}

    barrier = pltpu.get_barrier_semaphore()

    def greets(d):
        if d in (LEFT, RIGHT):
            return None
        ok = exists(*DIRS[d])
        if d == UP:
            ok = jnp.logical_and(ok, i_chan == 0)
        if d == DOWN:
            ok = jnp.logical_and(ok, i_chan == n_chan - 1)
        return ok

    for d in range(8):
        if greets(d) is not None:

            @pl.when(greets(d))
            def _():
                pl.semaphore_signal(barrier, inc=1, device_id=place(*DIRS[d]), device_id_type=pl.DeviceIdType.MESH)

    loads = [
        pltpu.make_async_copy(src, dst, in_sem.at[n])
        for n, (src, dst) in enumerate(
            (
                (img0_hbm, img.at[0]), (img1_hbm, img.at[1]), (k3_hbm, k3), (k1_hbm, k1), (k2_hbm, w2n),
            )
        )
    ]
    for load in loads:
        load.start()

    for axis, at, count, k in peers:
        pl.semaphore_signal(
            barrier, inc=1, device_id={axis: (at + k) % count}, device_id_type=pl.DeviceIdType.MESH
        )

    if n_chan > 1:
        pl.semaphore_signal(barrier, inc=1, device_id=far, device_id_type=pl.DeviceIdType.MESH)

    def barrier_wait():
        total = jnp.int32(len(peers) + (1 if n_chan > 1 else 0))
        for d in range(8):
            if greets(d) is not None:
                total = total + greets(d).astype(jnp.int32)
        pl.semaphore_wait(barrier, total)

    def copy(stage, d, src, dst):
        return pltpu.make_async_remote_copy(
            src_ref=src,
            dst_ref=dst,
            send_sem=send_sem.at[stage, d],
            recv_sem=recv_sem.at[stage, d],
            device_id=place(*DIRS[d]),
            device_id_type=pl.DeviceIdType.MESH,
        )

    def start(stage, plan):
        for d, (src, dst) in enumerate(plan):

            @pl.when(exists(*DIRS[d]))
            def _():
                copy(stage, d, src, dst).start()

    def arrive(stage, plan):
        for d, (src, dst) in enumerate(plan):
            back = DIRS[OPP[d]]

            @pl.when(exists(*back))
            def _():
                copy(stage, d, src, dst).wait_recv()

            @pl.when(jnp.logical_not(exists(*back)))
            def _():
                dst[...] = jnp.zeros(dst.shape, dst.dtype)

    def drain(stage, plan):
        for d, (src, dst) in enumerate(plan):

            @pl.when(exists(*DIRS[d]))
            def _():
                copy(stage, d, src, dst).wait_send()

    plan0 = [
        (su0, rd0), (sd0, ru0), (se0, rr0), (se0, rl0),
        (seu, rc0.at[3]), (seu, rc0.at[2]), (sed, rc0.at[1]), (sed, rc0.at[0]),
    ]

    def side_plan(up, down, side, hs):
        return [
            up, down, (side, hs.at[1]), (side, hs.at[0]),
            (side, hs.at[5]), (side, hs.at[4]), (side, hs.at[3]), (side, hs.at[2]),
        ]

    plan1 = [
        side_plan(
            (pool1.at[f, pl.ds(2, 2)], pool1.at[f, pl.ds(10, 2)]),
            (pool1.at[f, pl.ds(8, 2)], pool1.at[f, pl.ds(0, 2)]),
            se1.at[f], hs1.at[f],
        )
        for f in range(2)
    ]
    plan2 = [
        side_plan((su2.at[f], rd2.at[f]), (sd2.at[f], ru2.at[f]), se2.at[f], hs2.at[f])
        for f in range(2)
    ]
    plan3 = side_plan((su3, rd3), (sd3, ru3), se3, hs3)
    plan4 = side_plan((d2.at[pl.ds(2, 2)], d2.at[pl.ds(10, 2)]), (d2.at[pl.ds(8, 2)], d2.at[pl.ds(0, 2)]), se4, hs4)
    plan5 = side_plan((d1.at[0], rd5), (d1.at[15], ru5), se5, hs5)

    lane8 = lanes((8, 128))
    for f in range(2):
        loads[f].wait()
        for c in range(3):
            v = ((img[f, c] - OFFSETS[c]) * (1.0 / SPREADS[c])).astype(BF).astype(F32)
            pf[3 * f + c, 8:72, :] = v
    for c in range(3):
        acc = jnp.zeros((8, 128), F32)
        for f in range(2):
            for y in range(8):
                row = pf[3 * f + c, 8 + 8 * y : 16 + 8 * y, :]
                to = 64 * f + 8 * y
                acc = jnp.where((lane8 >= to) & (lane8 < to + 4), roll(row[:, :128], to), acc)
                acc = jnp.where((lane8 >= to + 4) & (lane8 < to + 8), roll(row[:, 896:], to + 8), acc)
        se0[8 * c : 8 * c + 8, :] = acc
    for buf, edge, at in ((su0, seu, 8), (sd0, sed, 68)):
        tmp[...] = jnp.zeros(tmp.shape, F32)
        for f in range(2):
            for c in range(3):
                tmp[16 * f + 4 * c : 16 * f + 4 * c + 4, :] = pf[3 * f + c, at : at + 4, :]
        v = tmp[...]
        buf[...] = v.astype(BF)
        edge[...] = jnp.where(lanes((32, 128)) < 4, v[:, :128], roll(v[:, 896:], 8)).astype(BF)

    barrier_wait()
    start(0, plan0)

    def eye(size):
        rows = lax.broadcasted_iota(jnp.int32, (size, size), 0)
        return jnp.where(rows == lanes((size, size)), 1.0, 0.0).astype(BF)

    def flip(one, block):
        return lax.dot_general(
            one, block, (((1,), (1,)), ((), ())), preferred_element_type=F32
        ).astype(BF)

    loads[2].wait()
    own = pl.ds(pl.multiple_of(i_chan * 96, 32), 96)
    one = eye(96)
    for at in range(0, 1728, 256):
        size = min(256, 1728 - at)
        w3t[own, at : at + size] = flip(one, k3[at : at + size, :])

    def shard_rows(owner, part):
        count = 96 if part is None else 16
        first = owner * 96 + (0 if part is None else 16 * part)
        return w3t.at[pl.ds(pl.multiple_of(first, 16), count)]

    def shard_copy(kind, part):
        rows = shard_rows((i_chan + 2) % n_chan if kind == 2 else i_chan, part)
        at = (0, 1, 7)[kind] + (part or 0)
        return pltpu.make_async_remote_copy(
            src_ref=rows,
            dst_ref=rows,
            send_sem=wsend.at[at],
            recv_sem=wrecv.at[at],
            device_id=far if kind == 1 else near,
            device_id_type=pl.DeviceIdType.MESH,
        )

    def shard_arrive(kind, part):
        owner = (near["chan"], i_chan + 2, near["chan"] + 2)[kind]
        rows = shard_rows(owner % n_chan, part)
        at = (0, 1, 7)[kind] + (part or 0)
        pltpu.make_async_remote_copy(
            src_ref=rows,
            dst_ref=rows,
            send_sem=wsend.at[at],
            recv_sem=wrecv.at[at],
            device_id=far if kind == 1 else near,
            device_id_type=pl.DeviceIdType.MESH,
        ).wait_recv()

    def shard_send(*parts):
        if n_chan > 1:
            for part in parts:
                shard_copy(1, part).start()

    def shard_pass(*parts):
        if n_chan > 1:
            for part in parts:
                shard_arrive(1, part)
                shard_copy(2, part).start()

    if n_chan > 1:
        shard_copy(0, None).start()
    shard_send(0, 1, 2)

    for src, dst in ((b1, cb1), (b2, cb2), (b3, cb3), (l1, cl1), (l2, cl2), (l3, cl3)):
        dst[...] = jnp.transpose(jnp.broadcast_to(src[...].reshape(1, -1), (128, src.shape[0])))
    la[...] = jnp.zeros(la.shape, F32)

    for px in range(8):
        at = lax.broadcasted_iota(jnp.int32, (1024, 128), 0)
        lane = lanes((1024, 128))
        want = 8 * (2 * (lane % 64) + lane // 64) + px
        sel[:, 128 * px : 128 * px + 128] = jnp.where(at == want, 1.0, 0.0).astype(BF)

    loads[3].wait()
    k1t = flip(eye(64), k1[...])
    cell = lax.broadcasted_iota(jnp.int32, (48, 128), 0)
    base = 48 * (cell % 4) + 16 * (cell // 16) + (cell // 4) % 4
    lane = lanes((48, 128))
    for cy in range(2):
        for cx in range(2):
            for tap in range(9):
                want = base + (192 * (tap % 3 + cx) + 4 * (tap // 3 + cy))
                for j in range(6):
                    sela[48 * tap : 48 * tap + 48, 128 * j : 128 * j + 128] = jnp.where(
                        lane + 128 * j == want, 1.0, 0.0
                    ).astype(BF)
            n = 2 * cy + cx
            wb1[64 * n : 64 * n + 64, :] = dot(k1t, sela[...]).astype(BF)

    loads[4].wait()
    one = eye(192)
    for at in range(0, 1600, 256):
        size = min(256, 1600 - at)
        w2t[:, at : at + size] = flip(one, w2n[at : at + size, :])

    arrive(0, plan0)
    for buf, at in ((ru0, 4), (rd0, 72)):
        tmp[...] = buf[...].astype(F32)
        for f in range(2):
            for c in range(3):
                pf[3 * f + c, at : at + 4, :] = tmp[16 * f + 4 * c : 16 * f + 4 * c + 4, :]
    for s, (mid, up, down) in enumerate(((rl0, 0, 2), (rr0, 1, 3))):
        for f in range(2):
            for c in range(3):
                v = mid[8 * c : 8 * c + 8, :]
                for y in range(8):
                    ef[s, 3 * f + c, 8 + 8 * y : 16 + 8 * y, :] = roll(v, -64 * f - 8 * y)
        for corner, at in ((up, 4), (down, 72)):
            tmp[:, :128] = rc0[corner].astype(F32)
            for f in range(2):
                for c in range(3):
                    ef[s, 3 * f + c, at : at + 4, :] = tmp[16 * f + 4 * c : 16 * f + 4 * c + 4, :128]

    def pixels(f):
        for r in range(8):
            for c in range(3):
                rows = slice((r * 3 + c) * 16, (r * 3 + c) * 16 + 16)
                lw[rows, :] = pf[3 * f + c, 8 * r + 4 : 8 * r + 20, :].astype(BF)
                for s in range(2):
                    ew[s, rows, :] = ef[s, 3 * f + c, 8 * r + 4 : 8 * r + 20, :]
        for pp in range(4):
            both = dot(lw[...], sel[:, 256 * pp : 256 * pp + 256])
            for px in (2 * pp, 2 * pp + 1):
                x = both[:, 128 * (px % 2) : 128 * (px % 2) + 128]
                if px >= 4:
                    other = shifted(x, -1)
                    other = jnp.where(lanes(x.shape) == 0, roll(ew[0], -px), other)
                    wx = px - 4
                else:
                    other = shifted(x, 1)
                    other = jnp.where(lanes(x.shape) == 127, roll(ew[1], 127 - px), other)
                    wx = 12 + px
                for w, v in ((4 + px, x), (wx, other)):
                    v = v.astype(BF)
                    for r in range(8):
                        x1[r % 4, 48 * w : 48 * w + 48, 128 * (r // 4) : 128 * (r // 4) + 128] = v[48 * r : 48 * r + 48]

    def silu(v):
        sigma = 0.5 * jnp.tanh(0.5 * v) + 0.5
        return v * sigma, sigma

    def layer_one(f):
        def body(i, _):
            out = dot(wb1[...], x1[i])
            for h in range(2):
                acc = None
                for ph in range(4):
                    v = out[64 * ph : 64 * ph + 64, 128 * h : 128 * h + 128] + cb1[...]
                    feat, sigma = silu(v)
                    n = (i + 4 * h) * 4 + ph
                    f1[f, n] = feat
                    if f == 0:
                        sl1[n] = sigma * (1.0 + v * (1.0 - sigma))
                    acc = feat if acc is None else acc + feat
                pool1[f, 2 + i + 4 * h] = (0.25 * acc).astype(BF)
            return 0

        lax.fori_loop(0, 4, body, 0)

    def pack_columns(rows, side):
        size = side.shape[0]
        acc = jnp.zeros((size, 128), F32)
        lane = lanes((size, 128)) % 64
        for g in range(4):
            for r in range(8):
                x = rows(r, slice(size * g, size * g + size)).astype(F32)
                to = 16 * g + r
                acc = jnp.where(lane == to, roll(x, to), acc)
                acc = jnp.where(lane == to + 8, roll(x, to + 8 - 63), acc)
        side[...] = acc.astype(BF)

    def merged(hs):
        size = hs.shape[1]
        lane = lanes((size, 128)) % 64
        slots = [hs[n].astype(F32) for n in range(6)]
        for g in range(4):
            v = roll(slots[1], 2 - 16 * g)
            v = jnp.where(lane < 2, roll(slots[3], -6 - 16 * g), v)
            v = jnp.where(lane >= 10, roll(slots[5], 10 - 16 * g), v)
            v = jnp.where(lane >= 18, roll(slots[0], 10 - 16 * g), v)
            v = jnp.where((lane >= 16) & (lane < 18), roll(slots[2], 2 - 16 * g), v)
            v = jnp.where(lane >= 26, roll(slots[4], 18 - 16 * g), v)
            hb[size * g : size * g + size, :] = v

    def layer_two_operand(f):
        lane = lanes((64, 128))
        merged(hs1.at[f])
        halo = hb[0:64, :]
        for rr in range(12):
            x = pool1[f, rr].astype(F32)
            right = roll(halo, 63 - rr)
            left = roll(halo, -16 - rr)
            cols = (
                jnp.where(lane % 64 == 0, left, shifted(x, -2)),
                jnp.where(lane == 0, roll(left, 64), shifted(x, -1)),
                x,
                jnp.where(lane == 127, roll(right, 64), shifted(x, 1)),
                jnp.where(lane % 64 == 63, right, shifted(x, 2)),
            )
            for e, v in enumerate(cols):
                v = v.astype(BF)
                if rr < 8:
                    x2[320 * rr + 64 * e : 320 * rr + 64 * e + 64, :128] = v
                if rr >= 4:
                    x2[320 * (rr - 4) + 64 * e : 320 * (rr - 4) + 64 * e + 64, 128:] = v

    def layer_two(f):
        low = lanes((64, 128)) < 64
        for i in range(4):
            out = dot(w2t[...], x2[320 * i : 320 * i + 1600, :])
            for h in range(2):
                for k in range(3):
                    rows = slice(64 * k, 64 * k + 64)
                    v = out[rows, 128 * h : 128 * h + 128] + cb2[rows]
                    feat, sigma = silu(v)
                    f2[f, i + 4 * h, rows] = feat
                    if f == 0:
                        sl2[i + 4 * h, rows] = sigma * (1.0 + v * (1.0 - sigma))
                    if i % 2 == 1:
                        both = f2[f, i - 1 + 4 * h, rows] + feat
                        mean = 0.25 * (both + roll(both, 64))
                        if i == 1:
                            keep[h, rows] = mean
                        else:
                            pool2[f, h, rows] = jnp.where(low, keep[h, rows], mean).astype(BF)

    def pack_ends(tiles, side, up, down):
        size = side.shape[0]
        lane = lanes((size, 128))
        acc = jnp.zeros((size, 128), F32)
        for g in range(12):
            for t in range(2):
                x = tiles[t, size * g : size * g + size, :].astype(F32)
                for r in (2 * t, 2 * t + 1):
                    first = 64 * (r % 2)
                    to = 8 * g + r
                    acc = jnp.where(lane == to, roll(x, to - first), acc)
                    acc = jnp.where(lane == to + 4, roll(x, to + 4 - 63 - first), acc)
        side[...] = acc.astype(BF)
        half = up.shape[0]
        for at in range(0, half, 96):
            rows, others = slice(at, at + 96), slice(half + at, half + at + 96)
            low = lanes((96, 128)) < 64
            up[rows] = jnp.where(
                low, tiles[0, rows].astype(F32), roll(tiles[0, others].astype(F32), 64)
            ).astype(BF)
            down[rows] = jnp.where(
                low, roll(tiles[1, rows].astype(F32), 64), tiles[1, others].astype(F32)
            ).astype(BF)

    def merged_ends(hs):
        size = hs.shape[1]
        lane = lanes((size, 128))
        slots = [hs[n].astype(F32) for n in range(6)]
        for g in range(12):
            v = None
            for first, (mid, up, down), skip in ((0, (1, 3, 5), 0), (16, (0, 2, 4), 4)):
                to = first - 8 * g - skip
                w = roll(slots[mid], to + 1)
                w = jnp.where(lane == first, roll(slots[up], to - 3), w)
                w = jnp.where(lane == first + 5, roll(slots[down], to + 5), w)
                w = jnp.where(lane >= 64, roll(slots[mid], to + 64), w)
                w = jnp.where(lane == first + 68, roll(slots[down], to + 68), w)
                v = w if v is None else jnp.where(lane % 64 < 16, v, w)
            hb[size * g : size * g + size, :] = v

    def layer_three_operand(tiles, from_up, from_down, hs, dst):
        channels = tiles.shape[1]
        half = channels // 2
        merged_ends(hs)
        for at in range(0, channels, 96):
            rows = slice(at, at + 96)
            fold = slice(at % half, at % half + 96)
            lane = lanes((96, 128))
            low = lane < 64
            halo = hb[rows, :]
            b = tiles[0, rows].astype(F32)
            d = tiles[1, rows].astype(F32)
            b_swap, d_swap = roll(b, 64), roll(d, 64)
            above, below = from_up[fold].astype(F32), from_down[fold].astype(F32)
            if at < half:
                below = roll(below, 64)
            else:
                above = roll(above, 64)
            a = jnp.where(low, above, b_swap)
            c = jnp.where(low, b_swap, d_swap)
            e = jnp.where(low, d_swap, below)
            for rr, (x, spots) in enumerate(
                ((a, ((0, 0),)), (b, ((1, 0),)), (c, ((0, 1), (2, 0))), (d, ((1, 1),)), (e, ((2, 1),)))
            ):
                left = jnp.where(lane % 64 == 0, roll(halo, -16 - rr), roll(x, 1))
                right = jnp.where(lane % 64 == 63, roll(halo, 63 - rr), roll(x, 127))
                for dx, v in enumerate((left, x, right)):
                    v = v.astype(BF)
                    for dy, spot in spots:
                        base = (dy * 3 + dx) * channels + at
                        dst[base : base + 96, 128 * spot : 128 * spot + 128] = v

    def layer_three(f):
        out = dot(w3t[...], x3[f])
        for h in range(2):
            for k in range(6):
                rows = slice(64 * k, 64 * k + 64)
                v = out[rows, 128 * h : 128 * h + 128] + cb3[rows]
                feat, sigma = silu(v)
                f3[f, h, rows] = feat
                if f == 0:
                    sl3[h, rows] = sigma * (1.0 + v * (1.0 - sigma))

    def local_terms(feats, n, weights, factor, count, finish):
        chunks = weights.shape[0] // 64
        rows = [slice(64 * k, 64 * k + 64) for k in range(chunks)]
        sums = [jnp.zeros((1, 128), F32)] * 2
        for f in range(2):
            for k in range(chunks):
                v = feats[f, n, rows[k]]
                sums[f] = sums[f] + jnp.sum(v * v, axis=0, keepdims=True)
        first, second = lax.rsqrt(sums[0] + EPSILON), lax.rsqrt(sums[1] + EPSILON)
        inner = jnp.zeros((1, 128), F32)
        total = jnp.zeros((1, 128), F32)
        for k in range(chunks):
            v = feats[0, n, rows[k]]
            differ = v * first - feats[1, n, rows[k]] * second
            slope = weights[rows[k]] * differ
            total = total + jnp.sum(slope * differ, axis=0, keepdims=True)
            inner = inner + jnp.sum(v * slope, axis=0, keepdims=True)
        la[0:1, :] = la[0:1, :] + total * (1.0 / count)
        scale = 2.0 * factor * first
        cubed = 2.0 * factor * first * first * first * inner
        for k in range(chunks):
            v = feats[0, n, rows[k]]
            slope = weights[rows[k]] * (v * first - feats[1, n, rows[k]] * second)
            finish(k, rows[k], scale * slope - v * cubed)

    for f in range(2):
        pixels(f)
        layer_one(f)
        pack_columns(lambda r, rows: pool1[f, 2 + r, rows], se1.at[f])
        start(1 + f, plan1[f])
        shard_send(*((3, 4), (5,))[f])
    kpair[...] = jnp.zeros(kpair.shape, BF)
    half = k1[...].astype(F32)
    both = jnp.concatenate([half, half], axis=1)
    low = lanes((432, 128)) < 64
    kpair[0:432, :] = jnp.where(low, both, 0.0).astype(BF)
    kpair[512:944, :] = jnp.where(low, 0.0, both).astype(BF)
    spot = lax.broadcasted_iota(jnp.int32, (24, 128), 0)
    lane = lanes((24, 128))
    in_low = (spot // 4) % 2 == 0
    within = 16 * (spot // 8) + 4 * (spot % 4)
    for wcy in range(4):
        for pair in range(2):
            for px in range(8):
                cx, b = px // 4, px % 4
                for side in range(2):
                    dx = 2 - (2 * pair + side) + cx
                    for j in range(4):
                        hit = jnp.zeros((24, 128), F32)
                        if 0 <= dx <= 2:
                            for cy in range(2):
                                dy = 2 - wcy + cy
                                first = (dy * 3 + dx) * 48
                                if 0 <= dy <= 2 and first < 128 * j + 128 and first + 48 > 128 * j:
                                    match = lane + (128 * j - first - b) == within
                                    keep_row = in_low if cy == 0 else jnp.logical_not(in_low)
                                    hit = jnp.where(match & keep_row, 1.0, hit)
                        bf[24 * px : 24 * px + 24, 512 * side + 128 * j : 512 * side + 128 * j + 128] = hit
            out = dot(bf[...].astype(BF), kpair[...])
            at = 256 * wcy + 128 * pair
            wb1b[:, at : at + 128] = out.astype(BF)

    for side in range(2):
        at = 96 * side
        wends[side] = jnp.concatenate(
            [wb1b[at : at + 96, 256 * w + 192 * side : 256 * w + 192 * side + 64].astype(F32) for w in range(4)], axis=1
        ).astype(BF)

    for f in range(2):
        shard_pass(2 * f, 2 * f + 1)
        arrive(1 + f, plan1[f])
        layer_two_operand(f)
        layer_two(f)
        pack_ends(pool2.at[f], se2.at[f], su2.at[f], sd2.at[f])
        start(3 + f, plan2[f])
    shard_pass(4, 5)
    pixel_count = 64 * n_tile * 1024 * n_col

    def terms_two(n, _):
        def finish_two(k, rows, dfeat):
            f2[0, n, rows] = dfeat

        local_terms(f2, n, cl2, 64.0, pixel_count // 64, finish_two)
        return 0

    lax.fori_loop(0, 8, terms_two, 0)

    def terms_one(n, _):
        def finish_one(k, rows, dfeat):
            f1[0, n, rows] = dfeat

        local_terms(f1, n, cl1, 16.0, pixel_count // 16, finish_one)
        return 0

    lax.fori_loop(0, 32, terms_one, 0)

    if n_chan > 1:
        shard_arrive(0, None)
        for part in range(6):
            shard_arrive(2, part)
    for f in range(2):
        arrive(3 + f, plan2[f])
        layer_three_operand(pool2.at[f], ru2.at[f], rd2.at[f], hs2.at[f], x3.at[f])
        layer_three(f)

    def loss_copy(axis, k):
        which = ("col", "chan", "row").index(axis)
        slots = (lsa, lsb, lsc)[which]
        at, count = ((i_col, n_col), (i_chan, n_chan), (i_row, n_row))[which]
        return pltpu.make_async_remote_copy(
            src_ref=la,
            dst_ref=slots.at[k - 1],
            send_sem=lsend.at[which, k - 1],
            recv_sem=lrecv.at[which, k - 1],
            device_id={axis: (at + k) % count},
            device_id_type=pl.DeviceIdType.MESH,
        )

    def loss_start(axis, count):
        for k in range(1, count):
            loss_copy(axis, k).start()

    def loss_finish(axis, count, slots):
        for k in range(1, count):
            loss_copy(axis, k).wait()
        total = la[...]
        for k in range(1, count):
            total = total + slots[k - 1]
        la[...] = total

    for h in range(2):

        def finish_three(k, rows, dfeat):
            d3[h, rows] = (dfeat * sl3[h, rows]).astype(BF)

        local_terms(f3, h, cl3, 256.0, pixel_count // 256, finish_three)
    pack_ends(d3, se3, su3, sd3)
    start(5, plan3)
    loss_start("col", n_col)


    one = eye(128)
    for at in range(0, 1728, 128):
        size = min(128, 1728 - at)
        w3n[at : at + size, :] = flip(one[:size, :size], w3t[:, at : at + size])

    drain(0, plan0)
    for f in range(2):
        drain(1 + f, plan1[f])
        drain(3 + f, plan2[f])
    if n_chan > 1:
        shard_copy(0, None).wait_send()
        for part in range(6):
            shard_copy(1, part).wait_send()
            shard_copy(2, part).wait_send()
    arrive(5, plan3)
    loss_finish("col", n_col, lsa)
    loss_start("chan", n_chan)
    layer_three_operand(d3, ru3, rd3, hs3, x3d)
    acc = None
    for tap in range(9):
        part = dot(w3n[192 * (8 - tap) : 192 * (8 - tap) + 192, :], x3d[384 * tap : 384 * tap + 384, :])
        acc = part if acc is None else acc + part
    dp2[...] = acc

    for r in range(8):
        for k in range(3):
            rows = slice(64 * k, 64 * k + 64)
            t = dp2[rows, 128 * (r // 4) : 128 * (r // 4) + 128]
            low = lanes((64, 128)) < 64
            swap = roll(t, 64)
            wide = jnp.where(low, t, swap) if (r // 2) % 2 == 0 else jnp.where(low, swap, t)
            d2[2 + r, rows] = ((f2[0, r, rows] + 0.25 * wide) * sl2[r, rows]).astype(BF)
    pack_columns(lambda r, rows: d2[2 + r, rows], se4)
    start(6, plan4)

    zero = jnp.zeros((192, 128), BF)
    for rr in range(12):
        v = d2[rr] if 2 <= rr < 10 else zero
        if rr < 8:
            x4[192 * rr : 192 * rr + 192, :128] = v
        if rr >= 4:
            x4[192 * (rr - 4) : 192 * (rr - 4) + 192, 128:] = v
    lane = lanes((64, 128))

    def joined(pick):
        total = pick(0)
        for e, edge in ((1, lane == 127), (-1, lane == 0), (2, lane % 64 == 63), (-2, lane % 64 == 0)):
            total = total + jnp.where(edge, 0.0, shifted(pick(e), e))
        return total

    def taps(operand, pairs):
        acc = None
        for dy, block in pairs:
            part = dot(w2n[320 * (4 - dy) : 320 * (4 - dy) + 320, :], operand(block))
            acc = part if acc is None else acc + part
        return acc

    for i in range(4):
        yb[...] = taps(lambda n: x4[192 * n : 192 * n + 192, :], [(dy, i + dy) for dy in range(5)])
        for h in range(2):
            dp1[i + 4 * h] = joined(
                lambda e: yb[64 * (2 - e) : 64 * (2 - e) + 64, 128 * h : 128 * h + 128]
            )

    drain(5, plan3)
    arrive(6, plan4)
    loss_finish("chan", n_chan, lsb)
    loss_start("row", n_row)
    merged(hs4)
    for at in range(0, 192, 64):
        halo = hb[at : at + 64, :]
        for dy in range(5):
            xh[192 * dy + at : 192 * dy + at + 64, :] = roll(halo, -dy).astype(BF)
    yh[...] = taps(lambda n: xh[192 * n : 192 * n + 192, :], [(dy, dy) for dy in range(5)])
    for n, v in enumerate((d2[0], d2[1], d2[1], zero, d2[10], d2[11], zero, d2[10])):
        xe[192 * (n // 2) : 192 * (n // 2) + 192, 128 * (n % 2) : 128 * (n % 2) + 128] = v
    for first, pairs in ((0, ((0, 0), (1, 1))), (6, ((4, 2), (3, 3)))):
        yb[...] = taps(lambda n: xe[192 * n : 192 * n + 192, :], pairs)
        for h in range(2):
            dp1[first + h] = dp1[first + h] + joined(
                lambda e: yb[64 * (2 - e) : 64 * (2 - e) + 64, 128 * h : 128 * h + 128]
            )
    for r in range(8):

        def side(e):
            return yh[64 * (2 - e) : 64 * (2 - e) + 64, :]

        total = dp1[r]
        total = total + jnp.where(lane == 127, roll(side(1), 127 - r), 0.0)
        total = total + jnp.where(lane % 64 == 63, roll(side(2), 63 - r), 0.0)
        total = total + jnp.where(lane == 0, roll(side(-1), -80 - r), 0.0)
        total = total + jnp.where(lane % 64 == 0, roll(side(-2), -16 - r), 0.0)
        total = 0.25 * total
        for py in range(2):
            for px in range(2):
                n = 4 * r + 2 * py + px
                d1[2 * r + py, 64 * px : 64 * px + 64] = ((f1[0, n] + total) * sl1[n]).astype(BF)

    lane16 = lanes((16, 128))
    acc = jnp.zeros((16, 128), F32)
    for g in range(4):
        for cr in range(16):
            to = 32 * g + cr
            zero, one = d1[cr, 16 * g : 16 * g + 16], d1[cr, 64 + 16 * g : 80 + 16 * g]
            acc = jnp.where(lane16 == to, roll(zero.astype(F32), to), acc)
            acc = jnp.where(lane16 == to + 16, roll(one.astype(F32), to + 16 - 127), acc)
    se5[...] = acc.astype(BF)
    start(7, plan5)

    def beside(src):
        zero, one = src[:64], src[64:]
        before = jnp.where(lane == 0, 0.0, shifted(one.astype(F32), -1)).astype(BF)
        after = jnp.where(lane == 127, 0.0, shifted(zero.astype(F32), 1)).astype(BF)
        return before, zero, one, after

    for n in range(18):
        if n in (0, 17):
            cols = (jnp.zeros((64, 128), BF),) * 4
        else:
            cols = beside(d1.at[n - 1])
        for g, v in enumerate(cols):
            if n < 10:
                x5[256 * n + 64 * g : 256 * n + 64 * g + 64, :128] = v
            if n >= 8:
                x5[256 * (n - 8) + 64 * g : 256 * (n - 8) + 64 * g + 64, 128:] = v

    def spots(r):
        for px in range(8):
            for c in range(3):
                yield px * 24 + c * 8, 64 * c + 8 * r, 128 * px

    for i in range(4):
        out = dot(wb1b[...], x5[512 * i : 512 * i + 1024, :])
        for h in range(2):
            for at, row, col in spots(i + 4 * h):
                bf[row : row + 8, col : col + 128] = out[at : at + 8, 128 * h : 128 * h + 128]

    drain(6, plan4)
    arrive(7, plan5)
    slots = [hs5[n].astype(F32) for n in range(6)]
    for g in range(4):
        v = roll(slots[1], 1 - 32 * g)
        v = jnp.where(lane16 == 0, roll(slots[3], -15 - 32 * g), v)
        v = jnp.where(lane16 == 17, roll(slots[5], 17 - 32 * g), v)
        w = roll(slots[0], 17 - 32 * g)
        w = jnp.where(lane16 == 32, roll(slots[2], 1 - 32 * g), w)
        w = jnp.where(lane16 == 49, roll(slots[4], 33 - 32 * g), w)
        hb[16 * g : 16 * g + 16, :] = jnp.where(lane16 < 32, v, w)
    for r, src, at in ((0, ru5, 0), (7, rd5, 768)):
        out = dot(wb1b[:, at : at + 256], jnp.concatenate(beside(src), axis=0))
        for at, row, col in spots(r):
            bf[row : row + 8, col : col + 128] = bf[row : row + 8, col : col + 128] + out[at : at + 8]
    halo = hb[0:64, :]
    stack = jnp.concatenate([roll(halo, -w).astype(BF) for w in range(4)], axis=0)
    for side, (first, edge) in enumerate(((32, 0), (0, 127))):
        yh[0:96, :] = dot(wends[side], stack)
        for r in range(8):
            for at, row, col in spots(r):
                if at // 96 == side:
                    part = roll(yh[at - 96 * side : at - 96 * side + 8, :], edge - first - 2 * r)
                    bf[row : row + 8, col : col + 128] = bf[row : row + 8, col : col + 128] + jnp.where(
                        lane8 == edge, part, 0.0
                    )
    loss_finish("row", n_row, lsc)
    loss[...] = jnp.sum(la[0:1, :], axis=1, keepdims=True)
    planes[...] = bf[...].astype(BF)

    drain(7, plan5)


def to_pixels(planes, grad, want):
    @pl.when(pl.program_id(0) == 0)
    def _():
        at = lax.broadcasted_iota(jnp.int32, (1024, 128), 0)
        want[...] = 8 * (2 * (at % 64) + (at // 64) % 2) + at // 128 - lanes((1024, 128))

    first = 256 * pl.program_id(0)
    spread = jnp.concatenate(
        [jnp.where(want[...] == first + 128 * j, 1.0, 0.0).astype(BF) for j in range(2)], axis=1
    )
    out = dot(planes[...], spread)
    for c in range(3):
        grad[c] = out[64 * c : 64 * c + 64] * (1.0 / SPREADS[c])


def local(
    image_gen, image_ref, kernel_one, bias_one, kernel_two, bias_two, kernel_three, bias_three,
    lin_first, lin_second, lin_third,
):
    n_row, n_col, n_chan = lax.axis_size("row"), lax.axis_size("col"), lax.axis_size("chan")
    rows = (bias_one, bias_two, bias_three, lin_first, lin_second, lin_third)
    V = pltpu.VMEM
    scratch = dict(
        img=V((2, 3, 64, 1024), F32), k1=V((432, 64), BF), w2n=V((1600, 192), BF), k3=V((1728, 96), BF),
        kpair=V((1024, 128), BF), sela=V((432, 768), BF), wb1=V((256, 768), BF), wb1b=V((192, 1024), BF),
        w2t=V((192, 1600), BF),
        sel=V((1024, 1024), BF), pf=V((6, 80, 1024), F32), ef=V((2, 6, 80, 128), F32),
        tmp=V((32, 1024), F32), lw=V((384, 1024), BF), ew=V((2, 384, 128), F32),
        x1=V((4, 768, 256), BF), f1=V((2, 32, 64, 128), F32), sl1=V((32, 64, 128), F32),
        pool1=V((2, 12, 64, 128), BF), x2=V((2560, 256), BF), f2=V((2, 8, 192, 128), F32),
        sl2=V((8, 192, 128), F32), keep=V((2, 192, 128), F32), pool2=V((2, 2, 192, 128), BF),
        x3=V((2, 1728, 256), BF), f3=V((2, 2, 384, 128), F32), sl3=V((2, 384, 128), F32),
        d3=V((2, 384, 128), BF), x3d=V((3456, 256), BF), w3t=V((384, 1728), BF), w3n=V((1728, 384), BF),
        dp2=V((192, 256), F32), d2=V((12, 192, 128), BF), x4=V((1536, 256), BF), yb=V((320, 256), F32),
        xh=V((960, 128), BF), yh=V((320, 128), F32), d1=V((16, 128, 128), BF), x5=V((2560, 256), BF),
        bf=V((192, 1024), F32), hb=V((384, 128), F32), wends=V((2, 96, 256), BF), dp1=V((8, 64, 128), F32),
        xe=V((768, 256), BF), cb1=V((64, 128), F32), cb2=V((192, 128), F32), cb3=V((384, 128), F32),
        cl1=V((64, 128), F32), cl2=V((192, 128), F32), cl3=V((384, 128), F32), la=V((8, 128), F32),
        lsa=V((max(n_col - 1, 1), 8, 128), F32), lsb=V((max(n_chan - 1, 1), 8, 128), F32),
        lsc=V((max(n_row - 1, 1), 8, 128), F32),
        su0=V((32, 1024), BF), sd0=V((32, 1024), BF), se0=V((24, 128), F32), seu=V((32, 128), BF),
        sed=V((32, 128), BF), ru0=V((32, 1024), BF), rd0=V((32, 1024), BF), rl0=V((24, 128), F32),
        rr0=V((24, 128), F32), rc0=V((4, 32, 128), BF),
        se1=V((2, 16, 128), BF), hs1=V((2, 6, 16, 128), BF), se2=V((2, 16, 128), BF),
        hs2=V((2, 6, 16, 128), BF), su2=V((2, 96, 128), BF), sd2=V((2, 96, 128), BF),
        ru2=V((2, 96, 128), BF), rd2=V((2, 96, 128), BF),
        se3=V((32, 128), BF), hs3=V((6, 32, 128), BF), su3=V((192, 128), BF), sd3=V((192, 128), BF),
        ru3=V((192, 128), BF), rd3=V((192, 128), BF),
        se4=V((48, 128), BF), hs4=V((6, 48, 128), BF), se5=V((16, 128), BF), hs5=V((6, 16, 128), BF),
        ru5=V((128, 128), BF), rd5=V((128, 128), BF),
        send_sem=pltpu.SemaphoreType.DMA((STAGES, 8)), recv_sem=pltpu.SemaphoreType.DMA((STAGES, 8)),
        wsend=pltpu.SemaphoreType.DMA((13,)), wrecv=pltpu.SemaphoreType.DMA((13,)),
        lsend=pltpu.SemaphoreType.DMA((3, 8)), lrecv=pltpu.SemaphoreType.DMA((3, 8)),
        in_sem=pltpu.SemaphoreType.DMA((5,)),
    )
    vmem = pl.BlockSpec(memory_space=pltpu.VMEM)
    planes, loss = pl.pallas_call(
        kernel,
        out_shape=(
            jax.ShapeDtypeStruct((192, 1024), BF),
            jax.ShapeDtypeStruct((1, 1), F32),
        ),
        in_specs=[pl.BlockSpec(memory_space=pl.ANY)] * 5 + [vmem] * 6,
        out_specs=(vmem, vmem),
        scratch_shapes=list(scratch.values()),
        compiler_params=pltpu.CompilerParams(
            collective_id=0, has_side_effects=True, vmem_limit_bytes=62 * 1024 * 1024
        ),
        name="whole",
    )(
        image_gen, image_ref, kernel_one.reshape(432, 64), kernel_two.reshape(1600, 192),
        kernel_three.reshape(1728, 96), *rows,
    )
    grad = pl.pallas_call(
        to_pixels,
        out_shape=jax.ShapeDtypeStruct(image_gen.shape, F32),
        grid=(4,),
        in_specs=[pl.BlockSpec((192, 1024), lambda n: (0, 0))],
        out_specs=pl.BlockSpec((3, 64, 256), lambda n: (0, 0, n)),
        scratch_shapes=[pltpu.VMEM((1024, 128), jnp.int32)],
        name="pixels",
    )(planes)
    return (grad, loss.reshape(()))


def solution(mesh):
    rows = ("row", "chan")
    in_specs = (
        P(None, rows, "col"), P(None, rows, "col"), P(), P(), P(), P(),
        P(None, None, None, "chan"), P(), P(), P(), P(),
    )
    out_specs = (P(None, rows, "col"), P())
    return jax.shard_map(local, mesh=mesh, in_specs=in_specs, out_specs=out_specs, check_vma=False)
```

```python
import functools

import jax
import jax.numpy as jnp
from jax import lax
from jax.experimental import pallas as pl
from jax.experimental.pallas import tpu as pltpu
from jax.sharding import PartitionSpec as P

OFFSETS = (-0.03, -0.088, -0.188)
SPREADS = (0.458, 0.448, 0.45)
EPSILON = 1e-06
BF = jnp.bfloat16
F32 = jnp.float32
DIRS = ((-1, 0), (1, 0), (0, -1), (0, 1), (-1, -1), (-1, 1), (1, -1), (1, 1))
UP, DOWN, LEFT, RIGHT, UL, UR, DL, DR = range(8)
OPP = (1, 0, 3, 2, 7, 6, 5, 4)
STAGES = 8


def roll(x, shift):
    return pltpu.roll(x, shift % 128, 1)


def dot(a, b):
    return jnp.dot(a, b, preferred_element_type=F32)


def lanes(shape):
    return lax.broadcasted_iota(jnp.int32, shape, 1)


def shifted(x, e):
    low = lanes(x.shape) < 64
    if e == 1:
        return jnp.where(low, roll(x, 64), roll(x, 63))
    if e == -1:
        return jnp.where(low, roll(x, 65), roll(x, 64))
    return roll(x, -e // 2)


def kernel(
    img0_hbm, img1_hbm, k1_hbm, k2_hbm, k3_hbm, b1, b2, b3, l1, l2, l3,
    planes, loss,
    img, k1, w2n, k3, kpair, sela, wb1, wb1b, w2t,
    sel, pf, ef, tmp, lw, ew, x1, f1, sl1, pool1, x2, f2, sl2, keep, pool2, x3,
    f3, sl3, d3, x3d, w3t, w3n, dp2, d2, x4, yb, xh, yh, d1, x5, bf, hb, wends, dp1, xe,
    cb1, cb2, cb3, cl1, cl2, cl3, la, lsa, lsb, lsc,
    su0, sd0, se0, seu, sed, ru0, rd0, rl0, rr0, rc0,
    se1, hs1, se2, hs2, su2, sd2, ru2, rd2, se3, hs3, su3, sd3, ru3, rd3, se4, hs4, se5, hs5, ru5, rd5,
    send_sem, recv_sem, wsend, wrecv, lsend, lrecv, in_sem,
):
    n_row, n_col, n_chan = lax.axis_size("row"), lax.axis_size("col"), lax.axis_size("chan")
    i_row, i_col, i_chan = lax.axis_index("row"), lax.axis_index("col"), lax.axis_index("chan")
    tile = i_row * n_chan + i_chan
    n_tile = n_row * n_chan

    def place(step_t, step_c):
        other = tile + step_t
        return {"row": other // n_chan, "chan": other % n_chan, "col": i_col + step_c}

    def exists(step_t, step_c):
        ok = None
        for step, at, count in ((step_t, tile, n_tile), (step_c, i_col, n_col)):
            if step < 0:
                term = at > 0
            elif step > 0:
                term = at < count - 1
            else:
                continue
            ok = term if ok is None else jnp.logical_and(ok, term)
        return ok

    peers = [("chan", i_chan, n_chan, k) for k in range(1, n_chan)]
    peers += [("col", i_col, n_col, k) for k in range(1, n_col)]
    peers += [("row", i_row, n_row, k) for k in range(1, n_row)]
    far = {"row": i_row + 1 - 2 * (i_row % 2), "chan": (i_chan + 2) % n_chan}
    near = {"chan": i_chan + 1 - 2 * (i_chan % 2)}

    barrier = pltpu.get_barrier_semaphore()

    def greets(d):
        if d in (LEFT, RIGHT):
            return None
        ok = exists(*DIRS[d])
        if d == UP:
            ok = jnp.logical_and(ok, i_chan == 0)
        if d == DOWN:
            ok = jnp.logical_and(ok, i_chan == n_chan - 1)
        return ok

    for d in range(8):
        if greets(d) is not None:

            @pl.when(greets(d))
            def _():
                pl.semaphore_signal(barrier, inc=1, device_id=place(*DIRS[d]), device_id_type=pl.DeviceIdType.MESH)

    loads = [
        pltpu.make_async_copy(src, dst, in_sem.at[n])
        for n, (src, dst) in enumerate(
            (
                (img0_hbm, img.at[0]), (img1_hbm, img.at[1]), (k3_hbm, k3), (k1_hbm, k1), (k2_hbm, w2n),
            )
        )
    ]
    for load in loads:
        load.start()

    for axis, at, count, k in peers:
        pl.semaphore_signal(
            barrier, inc=1, device_id={axis: (at + k) % count}, device_id_type=pl.DeviceIdType.MESH
        )

    if n_chan > 1:
        pl.semaphore_signal(barrier, inc=1, device_id=far, device_id_type=pl.DeviceIdType.MESH)

    def barrier_wait():
        total = jnp.int32(len(peers) + (1 if n_chan > 1 else 0))
        for d in range(8):
            if greets(d) is not None:
                total = total + greets(d).astype(jnp.int32)
        pl.semaphore_wait(barrier, total)

    def copy(stage, d, src, dst):
        return pltpu.make_async_remote_copy(
            src_ref=src,
            dst_ref=dst,
            send_sem=send_sem.at[stage, d],
            recv_sem=recv_sem.at[stage, d],
            device_id=place(*DIRS[d]),
            device_id_type=pl.DeviceIdType.MESH,
        )

    def start(stage, plan):
        for d, (src, dst) in enumerate(plan):

            @pl.when(exists(*DIRS[d]))
            def _():
                copy(stage, d, src, dst).start()

    def arrive(stage, plan):
        for d, (src, dst) in enumerate(plan):
            back = DIRS[OPP[d]]

            @pl.when(exists(*back))
            def _():
                copy(stage, d, src, dst).wait_recv()

    def drain(stage, plan):
        for d, (src, dst) in enumerate(plan):

            @pl.when(exists(*DIRS[d]))
            def _():
                copy(stage, d, src, dst).wait_send()

    plan0 = [
        (su0, rd0), (sd0, ru0), (se0, rr0), (se0, rl0),
        (seu, rc0.at[3]), (seu, rc0.at[2]), (sed, rc0.at[1]), (sed, rc0.at[0]),
    ]

    def side_plan(up, down, side, hs):
        return [
            up, down, (side, hs.at[1]), (side, hs.at[0]),
            (side, hs.at[5]), (side, hs.at[4]), (side, hs.at[3]), (side, hs.at[2]),
        ]

    plan1 = [
        side_plan(
            (pool1.at[f, pl.ds(2, 2)], pool1.at[f, pl.ds(10, 2)]),
            (pool1.at[f, pl.ds(8, 2)], pool1.at[f, pl.ds(0, 2)]),
            se1.at[f], hs1.at[f],
        )
        for f in range(2)
    ]
    plan2 = [
        side_plan((su2.at[f], rd2.at[f]), (sd2.at[f], ru2.at[f]), se2.at[f], hs2.at[f])
        for f in range(2)
    ]
    plan3 = side_plan((su3, rd3), (sd3, ru3), se3, hs3)
    plan4 = side_plan((d2.at[pl.ds(2, 2)], d2.at[pl.ds(10, 2)]), (d2.at[pl.ds(8, 2)], d2.at[pl.ds(0, 2)]), se4, hs4)
    plan5 = side_plan((d1.at[0], rd5), (d1.at[15], ru5), se5, hs5)

    def blank(plans):
        for d in range(8):

            @pl.when(jnp.logical_not(exists(*DIRS[OPP[d]])))
            def _():
                for plan in plans:
                    dst = plan[d][1]
                    dst[...] = jnp.zeros(dst.shape, dst.dtype)

    lane8 = lanes((8, 128))
    for f in range(2):
        loads[f].wait()
        for c in range(3):
            v = ((img[f, c] - OFFSETS[c]) * (1.0 / SPREADS[c])).astype(BF).astype(F32)
            pf[3 * f + c, 8:72, :] = v
    for c in range(3):
        acc = jnp.zeros((8, 128), F32)
        for f in range(2):
            for y in range(8):
                row = pf[3 * f + c, 8 + 8 * y : 16 + 8 * y, :]
                to = 64 * f + 8 * y
                acc = jnp.where((lane8 >= to) & (lane8 < to + 4), roll(row[:, :128], to), acc)
                acc = jnp.where((lane8 >= to + 4) & (lane8 < to + 8), roll(row[:, 896:], to + 8), acc)
        se0[8 * c : 8 * c + 8, :] = acc
    for buf, edge, at in ((su0, seu, 8), (sd0, sed, 68)):
        tmp[...] = jnp.zeros(tmp.shape, F32)
        for f in range(2):
            for c in range(3):
                tmp[16 * f + 4 * c : 16 * f + 4 * c + 4, :] = pf[3 * f + c, at : at + 4, :]
        v = tmp[...]
        buf[...] = v.astype(BF)
        edge[...] = jnp.where(lanes((32, 128)) < 4, v[:, :128], roll(v[:, 896:], 8)).astype(BF)

    barrier_wait()
    start(0, plan0)

    def eye(size):
        rows = lax.broadcasted_iota(jnp.int32, (size, size), 0)
        return jnp.where(rows == lanes((size, size)), 1.0, 0.0).astype(BF)

    def flip(one, block):
        return lax.dot_general(
            one, block, (((1,), (1,)), ((), ())), preferred_element_type=F32
        ).astype(BF)

    loads[2].wait()
    own = pl.ds(pl.multiple_of(i_chan * 96, 32), 96)
    one = eye(96)
    for at in range(0, 1728, 256):
        size = min(256, 1728 - at)
        w3t[own, at : at + size] = flip(one, k3[at : at + size, :])

    def shard_rows(owner, part):
        count = 96 if part is None else 16
        first = owner * 96 + (0 if part is None else 16 * part)
        return w3t.at[pl.ds(pl.multiple_of(first, 16), count)]

    def shard_copy(kind, part):
        rows = shard_rows((i_chan + 2) % n_chan if kind == 2 else i_chan, part)
        at = (0, 1, 7)[kind] + (part or 0)
        return pltpu.make_async_remote_copy(
            src_ref=rows,
            dst_ref=rows,
            send_sem=wsend.at[at],
            recv_sem=wrecv.at[at],
            device_id=far if kind == 1 else near,
            device_id_type=pl.DeviceIdType.MESH,
        )

    def shard_arrive(kind, part):
        owner = (near["chan"], i_chan + 2, near["chan"] + 2)[kind]
        rows = shard_rows(owner % n_chan, part)
        at = (0, 1, 7)[kind] + (part or 0)
        pltpu.make_async_remote_copy(
            src_ref=rows,
            dst_ref=rows,
            send_sem=wsend.at[at],
            recv_sem=wrecv.at[at],
            device_id=far if kind == 1 else near,
            device_id_type=pl.DeviceIdType.MESH,
        ).wait_recv()

    def shard_send(*parts):
        if n_chan > 1:
            for part in parts:
                shard_copy(1, part).start()

    def shard_pass(*parts):
        if n_chan > 1:
            for part in parts:
                shard_arrive(1, part)
                shard_copy(2, part).start()

    if n_chan > 1:
        shard_copy(0, None).start()
    shard_send(0, 1, 2)

    for src, dst in ((b1, cb1), (b2, cb2), (b3, cb3), (l1, cl1), (l2, cl2), (l3, cl3)):
        dst[...] = jnp.transpose(jnp.broadcast_to(src[...].reshape(1, -1), (128, src.shape[0])))
    la[...] = jnp.zeros(la.shape, F32)

    for px in range(8):
        at = lax.broadcasted_iota(jnp.int32, (1024, 128), 0)
        lane = lanes((1024, 128))
        want = 8 * (2 * (lane % 64) + lane // 64) + px
        sel[:, 128 * px : 128 * px + 128] = jnp.where(at == want, 1.0, 0.0).astype(BF)

    loads[3].wait()
    k1t = flip(eye(64), k1[...])
    cell = lax.broadcasted_iota(jnp.int32, (48, 128), 0)
    base = 48 * (cell % 4) + 16 * (cell // 16) + (cell // 4) % 4
    lane = lanes((48, 128))
    for cy in range(2):
        for cx in range(2):
            for tap in range(9):
                want = base + (192 * (tap % 3 + cx) + 4 * (tap // 3 + cy))
                for j in range(6):
                    sela[48 * tap : 48 * tap + 48, 128 * j : 128 * j + 128] = jnp.where(
                        lane + 128 * j == want, 1.0, 0.0
                    ).astype(BF)
            n = 2 * cy + cx
            wb1[64 * n : 64 * n + 64, :] = dot(k1t, sela[...]).astype(BF)

    loads[4].wait()
    one = eye(192)
    for at in range(0, 1600, 256):
        size = min(256, 1600 - at)
        w2t[:, at : at + size] = flip(one, w2n[at : at + size, :])

    blank([plan0, *plan1, *plan2, plan3, plan4, plan5])
    arrive(0, plan0)
    for buf, at in ((ru0, 4), (rd0, 72)):
        tmp[...] = buf[...].astype(F32)
        for f in range(2):
            for c in range(3):
                pf[3 * f + c, at : at + 4, :] = tmp[16 * f + 4 * c : 16 * f + 4 * c + 4, :]
    for s, (mid, up, down) in enumerate(((rl0, 0, 2), (rr0, 1, 3))):
        for f in range(2):
            for c in range(3):
                v = mid[8 * c : 8 * c + 8, :]
                for y in range(8):
                    ef[s, 3 * f + c, 8 + 8 * y : 16 + 8 * y, :] = roll(v, -64 * f - 8 * y)
        for corner, at in ((up, 4), (down, 72)):
            tmp[:, :128] = rc0[corner].astype(F32)
            for f in range(2):
                for c in range(3):
                    ef[s, 3 * f + c, at : at + 4, :] = tmp[16 * f + 4 * c : 16 * f + 4 * c + 4, :128]

    def pixels(f):
        for r in range(8):
            for c in range(3):
                rows = slice((r * 3 + c) * 16, (r * 3 + c) * 16 + 16)
                lw[rows, :] = pf[3 * f + c, 8 * r + 4 : 8 * r + 20, :].astype(BF)
                for s in range(2):
                    ew[s, rows, :] = ef[s, 3 * f + c, 8 * r + 4 : 8 * r + 20, :]
        for pp in range(4):
            both = dot(lw[...], sel[:, 256 * pp : 256 * pp + 256])
            for px in (2 * pp, 2 * pp + 1):
                x = both[:, 128 * (px % 2) : 128 * (px % 2) + 128]
                if px >= 4:
                    other = shifted(x, -1)
                    other = jnp.where(lanes(x.shape) == 0, roll(ew[0], -px), other)
                    wx = px - 4
                else:
                    other = shifted(x, 1)
                    other = jnp.where(lanes(x.shape) == 127, roll(ew[1], 127 - px), other)
                    wx = 12 + px
                for w, v in ((4 + px, x), (wx, other)):
                    v = v.astype(BF)
                    for r in range(8):
                        x1[r % 4, 48 * w : 48 * w + 48, 128 * (r // 4) : 128 * (r // 4) + 128] = v[48 * r : 48 * r + 48]

    def silu(v):
        sigma = 0.5 * jnp.tanh(0.5 * v) + 0.5
        return v * sigma, sigma

    def layer_one(f):
        def body(i, _):
            out = dot(wb1[...], x1[i])
            for h in range(2):
                acc = None
                for ph in range(4):
                    v = out[64 * ph : 64 * ph + 64, 128 * h : 128 * h + 128] + cb1[...]
                    feat, sigma = silu(v)
                    n = (i + 4 * h) * 4 + ph
                    f1[f, n] = feat
                    if f == 0:
                        sl1[n] = sigma * (1.0 + v * (1.0 - sigma))
                    acc = feat if acc is None else acc + feat
                pool1[f, 2 + i + 4 * h] = (0.25 * acc).astype(BF)
            return 0

        lax.fori_loop(0, 4, body, 0)

    def pack_columns(rows, side):
        size = side.shape[0]
        acc = jnp.zeros((size, 128), F32)
        lane = lanes((size, 128)) % 64
        for g in range(4):
            for r in range(8):
                x = rows(r, slice(size * g, size * g + size)).astype(F32)
                to = 16 * g + r
                acc = jnp.where(lane == to, roll(x, to), acc)
                acc = jnp.where(lane == to + 8, roll(x, to + 8 - 63), acc)
        side[...] = acc.astype(BF)

    def merged(hs):
        size = hs.shape[1]
        lane = lanes((size, 128)) % 64
        slots = [hs[n].astype(F32) for n in range(6)]
        for g in range(4):
            v = roll(slots[1], 2 - 16 * g)
            v = jnp.where(lane < 2, roll(slots[3], -6 - 16 * g), v)
            v = jnp.where(lane >= 10, roll(slots[5], 10 - 16 * g), v)
            v = jnp.where(lane >= 18, roll(slots[0], 10 - 16 * g), v)
            v = jnp.where((lane >= 16) & (lane < 18), roll(slots[2], 2 - 16 * g), v)
            v = jnp.where(lane >= 26, roll(slots[4], 18 - 16 * g), v)
            hb[size * g : size * g + size, :] = v

    def layer_two_operand(f):
        lane = lanes((64, 128))
        merged(hs1.at[f])
        halo = hb[0:64, :]
        for rr in range(12):
            x = pool1[f, rr].astype(F32)
            right = roll(halo, 63 - rr)
            left = roll(halo, -16 - rr)
            cols = (
                jnp.where(lane % 64 == 0, left, shifted(x, -2)),
                jnp.where(lane == 0, roll(left, 64), shifted(x, -1)),
                x,
                jnp.where(lane == 127, roll(right, 64), shifted(x, 1)),
                jnp.where(lane % 64 == 63, right, shifted(x, 2)),
            )
            for e, v in enumerate(cols):
                v = v.astype(BF)
                if rr < 8:
                    x2[320 * rr + 64 * e : 320 * rr + 64 * e + 64, :128] = v
                if rr >= 4:
                    x2[320 * (rr - 4) + 64 * e : 320 * (rr - 4) + 64 * e + 64, 128:] = v

    def layer_two(f):
        low = lanes((64, 128)) < 64
        for i in range(4):
            out = dot(w2t[...], x2[320 * i : 320 * i + 1600, :])
            for h in range(2):
                for k in range(3):
                    rows = slice(64 * k, 64 * k + 64)
                    v = out[rows, 128 * h : 128 * h + 128] + cb2[rows]
                    feat, sigma = silu(v)
                    f2[f, i + 4 * h, rows] = feat
                    if f == 0:
                        sl2[i + 4 * h, rows] = sigma * (1.0 + v * (1.0 - sigma))
                    if i % 2 == 1:
                        both = f2[f, i - 1 + 4 * h, rows] + feat
                        mean = 0.25 * (both + roll(both, 64))
                        if i == 1:
                            keep[h, rows] = mean
                        else:
                            pool2[f, h, rows] = jnp.where(low, keep[h, rows], mean).astype(BF)

    def pack_ends(tiles, side, up, down):
        size = side.shape[0]
        lane = lanes((size, 128))
        acc = jnp.zeros((size, 128), F32)
        for g in range(12):
            for t in range(2):
                x = tiles[t, size * g : size * g + size, :].astype(F32)
                for r in (2 * t, 2 * t + 1):
                    first = 64 * (r % 2)
                    to = 8 * g + r
                    acc = jnp.where(lane == to, roll(x, to - first), acc)
                    acc = jnp.where(lane == to + 4, roll(x, to + 4 - 63 - first), acc)
        side[...] = acc.astype(BF)
        half = up.shape[0]
        for at in range(0, half, 96):
            rows, others = slice(at, at + 96), slice(half + at, half + at + 96)
            low = lanes((96, 128)) < 64
            up[rows] = jnp.where(
                low, tiles[0, rows].astype(F32), roll(tiles[0, others].astype(F32), 64)
            ).astype(BF)
            down[rows] = jnp.where(
                low, roll(tiles[1, rows].astype(F32), 64), tiles[1, others].astype(F32)
            ).astype(BF)

    def merged_ends(hs):
        size = hs.shape[1]
        lane = lanes((size, 128))
        slots = [hs[n].astype(F32) for n in range(6)]
        for g in range(12):
            v = None
            for first, (mid, up, down), skip in ((0, (1, 3, 5), 0), (16, (0, 2, 4), 4)):
                to = first - 8 * g - skip
                w = roll(slots[mid], to + 1)
                w = jnp.where(lane == first, roll(slots[up], to - 3), w)
                w = jnp.where(lane == first + 5, roll(slots[down], to + 5), w)
                w = jnp.where(lane >= 64, roll(slots[mid], to + 64), w)
                w = jnp.where(lane == first + 68, roll(slots[down], to + 68), w)
                v = w if v is None else jnp.where(lane % 64 < 16, v, w)
            hb[size * g : size * g + size, :] = v

    def layer_three_operand(tiles, from_up, from_down, hs, dst):
        channels = tiles.shape[1]
        half = channels // 2
        merged_ends(hs)
        for at in range(0, channels, 96):
            rows = slice(at, at + 96)
            fold = slice(at % half, at % half + 96)
            lane = lanes((96, 128))
            low = lane < 64
            halo = hb[rows, :]
            b = tiles[0, rows].astype(F32)
            d = tiles[1, rows].astype(F32)
            b_swap, d_swap = roll(b, 64), roll(d, 64)
            above, below = from_up[fold].astype(F32), from_down[fold].astype(F32)
            if at < half:
                below = roll(below, 64)
            else:
                above = roll(above, 64)
            a = jnp.where(low, above, b_swap)
            c = jnp.where(low, b_swap, d_swap)
            e = jnp.where(low, d_swap, below)
            for rr, (x, spots) in enumerate(
                ((a, ((0, 0),)), (b, ((1, 0),)), (c, ((0, 1), (2, 0))), (d, ((1, 1),)), (e, ((2, 1),)))
            ):
                left = jnp.where(lane % 64 == 0, roll(halo, -16 - rr), roll(x, 1))
                right = jnp.where(lane % 64 == 63, roll(halo, 63 - rr), roll(x, 127))
                for dx, v in enumerate((left, x, right)):
                    v = v.astype(BF)
                    for dy, spot in spots:
                        base = (dy * 3 + dx) * channels + at
                        dst[base : base + 96, 128 * spot : 128 * spot + 128] = v

    def layer_three(f):
        out = dot(w3t[...], x3[f])
        for h in range(2):
            for k in range(6):
                rows = slice(64 * k, 64 * k + 64)
                v = out[rows, 128 * h : 128 * h + 128] + cb3[rows]
                feat, sigma = silu(v)
                f3[f, h, rows] = feat
                if f == 0:
                    sl3[h, rows] = sigma * (1.0 + v * (1.0 - sigma))

    def local_terms(feats, n, weights, factor, count, finish):
        chunks = weights.shape[0] // 64
        rows = [slice(64 * k, 64 * k + 64) for k in range(chunks)]
        sums = [jnp.zeros((1, 128), F32)] * 2
        for f in range(2):
            for k in range(chunks):
                v = feats[f, n, rows[k]]
                sums[f] = sums[f] + jnp.sum(v * v, axis=0, keepdims=True)
        first, second = lax.rsqrt(sums[0] + EPSILON), lax.rsqrt(sums[1] + EPSILON)
        inner = jnp.zeros((1, 128), F32)
        total = jnp.zeros((1, 128), F32)
        for k in range(chunks):
            v = feats[0, n, rows[k]]
            differ = v * first - feats[1, n, rows[k]] * second
            slope = weights[rows[k]] * differ
            total = total + jnp.sum(slope * differ, axis=0, keepdims=True)
            inner = inner + jnp.sum(v * slope, axis=0, keepdims=True)
        la[0:1, :] = la[0:1, :] + total * (1.0 / count)
        scale = 2.0 * factor * first
        cubed = 2.0 * factor * first * first * first * inner
        for k in range(chunks):
            v = feats[0, n, rows[k]]
            slope = weights[rows[k]] * (v * first - feats[1, n, rows[k]] * second)
            finish(k, rows[k], scale * slope - v * cubed)

    for f in range(2):
        pixels(f)
        layer_one(f)
        pack_columns(lambda r, rows: pool1[f, 2 + r, rows], se1.at[f])
        start(1 + f, plan1[f])
        shard_send(*((3, 4), (5,))[f])
    kpair[...] = jnp.zeros(kpair.shape, BF)
    half = k1[...].astype(F32)
    both = jnp.concatenate([half, half], axis=1)
    low = lanes((432, 128)) < 64
    kpair[0:432, :] = jnp.where(low, both, 0.0).astype(BF)
    kpair[512:944, :] = jnp.where(low, 0.0, both).astype(BF)
    spot = lax.broadcasted_iota(jnp.int32, (24, 128), 0)
    lane = lanes((24, 128))
    in_low = (spot // 4) % 2 == 0
    within = 16 * (spot // 8) + 4 * (spot % 4)
    for wcy in range(4):
        for pair in range(2):
            for px in range(8):
                cx, b = px // 4, px % 4
                for side in range(2):
                    dx = 2 - (2 * pair + side) + cx
                    for j in range(4):
                        hit = jnp.zeros((24, 128), F32)
                        if 0 <= dx <= 2:
                            for cy in range(2):
                                dy = 2 - wcy + cy
                                first = (dy * 3 + dx) * 48
                                if 0 <= dy <= 2 and first < 128 * j + 128 and first + 48 > 128 * j:
                                    match = lane + (128 * j - first - b) == within
                                    keep_row = in_low if cy == 0 else jnp.logical_not(in_low)
                                    hit = jnp.where(match & keep_row, 1.0, hit)
                        bf[24 * px : 24 * px + 24, 512 * side + 128 * j : 512 * side + 128 * j + 128] = hit
            out = dot(bf[...].astype(BF), kpair[...])
            at = 256 * wcy + 128 * pair
            wb1b[:, at : at + 128] = out.astype(BF)

    for side in range(2):
        at = 96 * side
        wends[side] = jnp.concatenate(
            [wb1b[at : at + 96, 256 * w + 192 * side : 256 * w + 192 * side + 64].astype(F32) for w in range(4)], axis=1
        ).astype(BF)

    for f in range(2):
        shard_pass(2 * f, 2 * f + 1)
        arrive(1 + f, plan1[f])
        layer_two_operand(f)
        layer_two(f)
        pack_ends(pool2.at[f], se2.at[f], su2.at[f], sd2.at[f])
        start(3 + f, plan2[f])
    shard_pass(4, 5)
    pixel_count = 64 * n_tile * 1024 * n_col

    def terms_two(n, _):
        def finish_two(k, rows, dfeat):
            f2[0, n, rows] = dfeat

        local_terms(f2, n, cl2, 64.0, pixel_count // 64, finish_two)
        return 0

    lax.fori_loop(0, 8, terms_two, 0)

    def terms_one(n, _):
        def finish_one(k, rows, dfeat):
            f1[0, n, rows] = dfeat

        local_terms(f1, n, cl1, 16.0, pixel_count // 16, finish_one)
        return 0

    lax.fori_loop(0, 32, terms_one, 0)

    if n_chan > 1:
        shard_arrive(0, None)
        for part in range(6):
            shard_arrive(2, part)
    for f in range(2):
        arrive(3 + f, plan2[f])
        layer_three_operand(pool2.at[f], ru2.at[f], rd2.at[f], hs2.at[f], x3.at[f])
        layer_three(f)

    def loss_copy(axis, k):
        which = ("col", "chan", "row").index(axis)
        slots = (lsa, lsb, lsc)[which]
        at, count = ((i_col, n_col), (i_chan, n_chan), (i_row, n_row))[which]
        return pltpu.make_async_remote_copy(
            src_ref=la,
            dst_ref=slots.at[k - 1],
            send_sem=lsend.at[which, k - 1],
            recv_sem=lrecv.at[which, k - 1],
            device_id={axis: (at + k) % count},
            device_id_type=pl.DeviceIdType.MESH,
        )

    def loss_start(axis, count):
        for k in range(1, count):
            loss_copy(axis, k).start()

    def loss_finish(axis, count, slots):
        for k in range(1, count):
            loss_copy(axis, k).wait()
        total = la[...]
        for k in range(1, count):
            total = total + slots[k - 1]
        la[...] = total

    for h in range(2):

        def finish_three(k, rows, dfeat):
            d3[h, rows] = (dfeat * sl3[h, rows]).astype(BF)

        local_terms(f3, h, cl3, 256.0, pixel_count // 256, finish_three)
    pack_ends(d3, se3, su3, sd3)
    start(5, plan3)
    loss_start("col", n_col)


    one = eye(128)
    for at in range(0, 1728, 128):
        size = min(128, 1728 - at)
        w3n[at : at + size, :] = flip(one[:size, :size], w3t[:, at : at + size])

    drain(0, plan0)
    for f in range(2):
        drain(1 + f, plan1[f])
        drain(3 + f, plan2[f])
    if n_chan > 1:
        shard_copy(0, None).wait_send()
        for part in range(6):
            shard_copy(1, part).wait_send()
            shard_copy(2, part).wait_send()
    arrive(5, plan3)
    loss_finish("col", n_col, lsa)
    loss_start("chan", n_chan)
    layer_three_operand(d3, ru3, rd3, hs3, x3d)
    acc = None
    for tap in range(9):
        part = dot(w3n[192 * (8 - tap) : 192 * (8 - tap) + 192, :], x3d[384 * tap : 384 * tap + 384, :])
        acc = part if acc is None else acc + part
    dp2[...] = acc

    for r in range(8):
        for k in range(3):
            rows = slice(64 * k, 64 * k + 64)
            t = dp2[rows, 128 * (r // 4) : 128 * (r // 4) + 128]
            low = lanes((64, 128)) < 64
            swap = roll(t, 64)
            wide = jnp.where(low, t, swap) if (r // 2) % 2 == 0 else jnp.where(low, swap, t)
            d2[2 + r, rows] = ((f2[0, r, rows] + 0.25 * wide) * sl2[r, rows]).astype(BF)
    pack_columns(lambda r, rows: d2[2 + r, rows], se4)
    start(6, plan4)

    zero = jnp.zeros((192, 128), BF)
    for rr in range(12):
        v = d2[rr] if 2 <= rr < 10 else zero
        if rr < 8:
            x4[192 * rr : 192 * rr + 192, :128] = v
        if rr >= 4:
            x4[192 * (rr - 4) : 192 * (rr - 4) + 192, 128:] = v
    lane = lanes((64, 128))

    def joined(pick):
        total = pick(0)
        for e, edge in ((1, lane == 127), (-1, lane == 0), (2, lane % 64 == 63), (-2, lane % 64 == 0)):
            total = total + jnp.where(edge, 0.0, shifted(pick(e), e))
        return total

    def taps(operand, pairs):
        acc = None
        for dy, block in pairs:
            part = dot(w2n[320 * (4 - dy) : 320 * (4 - dy) + 320, :], operand(block))
            acc = part if acc is None else acc + part
        return acc

    for i in range(4):
        yb[...] = taps(lambda n: x4[192 * n : 192 * n + 192, :], [(dy, i + dy) for dy in range(5)])
        for h in range(2):
            dp1[i + 4 * h] = joined(
                lambda e: yb[64 * (2 - e) : 64 * (2 - e) + 64, 128 * h : 128 * h + 128]
            )

    drain(5, plan3)
    arrive(6, plan4)
    loss_finish("chan", n_chan, lsb)
    loss_start("row", n_row)
    merged(hs4)
    for at in range(0, 192, 64):
        halo = hb[at : at + 64, :]
        for dy in range(5):
            xh[192 * dy + at : 192 * dy + at + 64, :] = roll(halo, -dy).astype(BF)
    yh[...] = taps(lambda n: xh[192 * n : 192 * n + 192, :], [(dy, dy) for dy in range(5)])
    for n, v in enumerate((d2[0], d2[1], d2[1], zero, d2[10], d2[11], zero, d2[10])):
        xe[192 * (n // 2) : 192 * (n // 2) + 192, 128 * (n % 2) : 128 * (n % 2) + 128] = v
    for first, pairs in ((0, ((0, 0), (1, 1))), (6, ((4, 2), (3, 3)))):
        yb[...] = taps(lambda n: xe[192 * n : 192 * n + 192, :], pairs)
        for h in range(2):
            dp1[first + h] = dp1[first + h] + joined(
                lambda e: yb[64 * (2 - e) : 64 * (2 - e) + 64, 128 * h : 128 * h + 128]
            )
    for r in range(8):

        def side(e):
            return yh[64 * (2 - e) : 64 * (2 - e) + 64, :]

        total = dp1[r]
        total = total + jnp.where(lane == 127, roll(side(1), 127 - r), 0.0)
        total = total + jnp.where(lane % 64 == 63, roll(side(2), 63 - r), 0.0)
        total = total + jnp.where(lane == 0, roll(side(-1), -80 - r), 0.0)
        total = total + jnp.where(lane % 64 == 0, roll(side(-2), -16 - r), 0.0)
        total = 0.25 * total
        for py in range(2):
            for px in range(2):
                n = 4 * r + 2 * py + px
                d1[2 * r + py, 64 * px : 64 * px + 64] = ((f1[0, n] + total) * sl1[n]).astype(BF)

    lane16 = lanes((16, 128))
    acc = jnp.zeros((16, 128), F32)
    for g in range(4):
        for cr in range(16):
            to = 32 * g + cr
            zero, one = d1[cr, 16 * g : 16 * g + 16], d1[cr, 64 + 16 * g : 80 + 16 * g]
            acc = jnp.where(lane16 == to, roll(zero.astype(F32), to), acc)
            acc = jnp.where(lane16 == to + 16, roll(one.astype(F32), to + 16 - 127), acc)
    se5[...] = acc.astype(BF)
    start(7, plan5)

    def beside(src):
        zero, one = src[:64], src[64:]
        before = jnp.where(lane == 0, 0.0, shifted(one.astype(F32), -1)).astype(BF)
        after = jnp.where(lane == 127, 0.0, shifted(zero.astype(F32), 1)).astype(BF)
        return before, zero, one, after

    for n in range(18):
        if n in (0, 17):
            cols = (jnp.zeros((64, 128), BF),) * 4
        else:
            cols = beside(d1.at[n - 1])
        for g, v in enumerate(cols):
            if n < 10:
                x5[256 * n + 64 * g : 256 * n + 64 * g + 64, :128] = v
            if n >= 8:
                x5[256 * (n - 8) + 64 * g : 256 * (n - 8) + 64 * g + 64, 128:] = v

    def spots(r):
        for px in range(8):
            for c in range(3):
                yield px * 24 + c * 8, 64 * c + 8 * r, 128 * px

    for i in range(4):
        out = dot(wb1b[...], x5[512 * i : 512 * i + 1024, :])
        for h in range(2):
            for at, row, col in spots(i + 4 * h):
                bf[row : row + 8, col : col + 128] = out[at : at + 8, 128 * h : 128 * h + 128]

    drain(6, plan4)
    arrive(7, plan5)
    slots = [hs5[n].astype(F32) for n in range(6)]
    for g in range(4):
        v = roll(slots[1], 1 - 32 * g)
        v = jnp.where(lane16 == 0, roll(slots[3], -15 - 32 * g), v)
        v = jnp.where(lane16 == 17, roll(slots[5], 17 - 32 * g), v)
        w = roll(slots[0], 17 - 32 * g)
        w = jnp.where(lane16 == 32, roll(slots[2], 1 - 32 * g), w)
        w = jnp.where(lane16 == 49, roll(slots[4], 33 - 32 * g), w)
        hb[16 * g : 16 * g + 16, :] = jnp.where(lane16 < 32, v, w)
    for r, src, at in ((0, ru5, 0), (7, rd5, 768)):
        out = dot(wb1b[:, at : at + 256], jnp.concatenate(beside(src), axis=0))
        for at, row, col in spots(r):
            bf[row : row + 8, col : col + 128] = bf[row : row + 8, col : col + 128] + out[at : at + 8]
    halo = hb[0:64, :]
    stack = jnp.concatenate([roll(halo, -w).astype(BF) for w in range(4)], axis=0)
    for side, (first, edge) in enumerate(((32, 0), (0, 127))):
        yh[0:96, :] = dot(wends[side], stack)
        for r in range(8):
            for at, row, col in spots(r):
                if at // 96 == side:
                    part = roll(yh[at - 96 * side : at - 96 * side + 8, :], edge - first - 2 * r)
                    bf[row : row + 8, col : col + 128] = bf[row : row + 8, col : col + 128] + jnp.where(
                        lane8 == edge, part, 0.0
                    )
    loss_finish("row", n_row, lsc)
    loss[...] = jnp.sum(la[0:1, :], axis=1, keepdims=True)
    planes[...] = bf[...].astype(BF)

    drain(7, plan5)


def to_pixels(planes, grad):
    at = lax.broadcasted_iota(jnp.int32, (128, 1024), 0)
    want = 8 * (2 * (at % 64) + at // 64) - lanes((128, 1024))
    out = None
    for k in range(4):
        spread = jnp.concatenate(
            [jnp.where(want == -(2 * k + j), 1.0, 0.0).astype(BF) for j in range(2)], axis=0
        )
        part = dot(planes[:, 256 * k : 256 * k + 256], spread)
        out = part if out is None else out + part
    for c in range(3):
        grad[c] = out[64 * c : 64 * c + 64] * (1.0 / SPREADS[c])


def local(
    image_gen, image_ref, kernel_one, bias_one, kernel_two, bias_two, kernel_three, bias_three,
    lin_first, lin_second, lin_third,
):
    n_row, n_col, n_chan = lax.axis_size("row"), lax.axis_size("col"), lax.axis_size("chan")
    rows = (bias_one, bias_two, bias_three, lin_first, lin_second, lin_third)
    V = pltpu.VMEM
    scratch = dict(
        img=V((2, 3, 64, 1024), F32), k1=V((432, 64), BF), w2n=V((1600, 192), BF), k3=V((1728, 96), BF),
        kpair=V((1024, 128), BF), sela=V((432, 768), BF), wb1=V((256, 768), BF), wb1b=V((192, 1024), BF),
        w2t=V((192, 1600), BF),
        sel=V((1024, 1024), BF), pf=V((6, 80, 1024), F32), ef=V((2, 6, 80, 128), F32),
        tmp=V((32, 1024), F32), lw=V((384, 1024), BF), ew=V((2, 384, 128), F32),
        x1=V((4, 768, 256), BF), f1=V((2, 32, 64, 128), F32), sl1=V((32, 64, 128), F32),
        pool1=V((2, 12, 64, 128), BF), x2=V((2560, 256), BF), f2=V((2, 8, 192, 128), F32),
        sl2=V((8, 192, 128), F32), keep=V((2, 192, 128), F32), pool2=V((2, 2, 192, 128), BF),
        x3=V((2, 1728, 256), BF), f3=V((2, 2, 384, 128), F32), sl3=V((2, 384, 128), F32),
        d3=V((2, 384, 128), BF), x3d=V((3456, 256), BF), w3t=V((384, 1728), BF), w3n=V((1728, 384), BF),
        dp2=V((192, 256), F32), d2=V((12, 192, 128), BF), x4=V((1536, 256), BF), yb=V((320, 256), F32),
        xh=V((960, 128), BF), yh=V((320, 128), F32), d1=V((16, 128, 128), BF), x5=V((2560, 256), BF),
        bf=V((192, 1024), F32), hb=V((384, 128), F32), wends=V((2, 96, 256), BF), dp1=V((8, 64, 128), F32),
        xe=V((768, 256), BF), cb1=V((64, 128), F32), cb2=V((192, 128), F32), cb3=V((384, 128), F32),
        cl1=V((64, 128), F32), cl2=V((192, 128), F32), cl3=V((384, 128), F32), la=V((8, 128), F32),
        lsa=V((max(n_col - 1, 1), 8, 128), F32), lsb=V((max(n_chan - 1, 1), 8, 128), F32),
        lsc=V((max(n_row - 1, 1), 8, 128), F32),
        su0=V((32, 1024), BF), sd0=V((32, 1024), BF), se0=V((24, 128), F32), seu=V((32, 128), BF),
        sed=V((32, 128), BF), ru0=V((32, 1024), BF), rd0=V((32, 1024), BF), rl0=V((24, 128), F32),
        rr0=V((24, 128), F32), rc0=V((4, 32, 128), BF),
        se1=V((2, 16, 128), BF), hs1=V((2, 6, 16, 128), BF), se2=V((2, 16, 128), BF),
        hs2=V((2, 6, 16, 128), BF), su2=V((2, 96, 128), BF), sd2=V((2, 96, 128), BF),
        ru2=V((2, 96, 128), BF), rd2=V((2, 96, 128), BF),
        se3=V((32, 128), BF), hs3=V((6, 32, 128), BF), su3=V((192, 128), BF), sd3=V((192, 128), BF),
        ru3=V((192, 128), BF), rd3=V((192, 128), BF),
        se4=V((48, 128), BF), hs4=V((6, 48, 128), BF), se5=V((16, 128), BF), hs5=V((6, 16, 128), BF),
        ru5=V((128, 128), BF), rd5=V((128, 128), BF),
        send_sem=pltpu.SemaphoreType.DMA((STAGES, 8)), recv_sem=pltpu.SemaphoreType.DMA((STAGES, 8)),
        wsend=pltpu.SemaphoreType.DMA((13,)), wrecv=pltpu.SemaphoreType.DMA((13,)),
        lsend=pltpu.SemaphoreType.DMA((3, 8)), lrecv=pltpu.SemaphoreType.DMA((3, 8)),
        in_sem=pltpu.SemaphoreType.DMA((5,)),
    )
    vmem = pl.BlockSpec(memory_space=pltpu.VMEM)
    planes, loss = pl.pallas_call(
        kernel,
        out_shape=(
            jax.ShapeDtypeStruct((192, 1024), BF),
            jax.ShapeDtypeStruct((1, 1), F32),
        ),
        in_specs=[pl.BlockSpec(memory_space=pl.ANY)] * 5 + [vmem] * 6,
        out_specs=(vmem, vmem),
        scratch_shapes=list(scratch.values()),
        compiler_params=pltpu.CompilerParams(
            collective_id=0, has_side_effects=True, vmem_limit_bytes=62 * 1024 * 1024
        ),
        name="whole",
    )(
        image_gen, image_ref, kernel_one.reshape(432, 64), kernel_two.reshape(1600, 192),
        kernel_three.reshape(1728, 96), *rows,
    )
    grad = pl.pallas_call(
        to_pixels,
        out_shape=jax.ShapeDtypeStruct(image_gen.shape, F32),
        in_specs=[vmem],
        out_specs=vmem,
        name="pixels",
    )(planes)
    return (grad, loss.reshape(()))


def solution(mesh):
    rows = ("row", "chan")
    in_specs = (
        P(None, rows, "col"), P(None, rows, "col"), P(), P(), P(), P(),
        P(None, None, None, "chan"), P(), P(), P(), P(),
    )
    out_specs = (P(None, rows, "col"), P())
    return jax.shard_map(local, mesh=mesh, in_specs=in_specs, out_specs=out_specs, check_vma=False)
```

```python
import functools

import jax
import jax.numpy as jnp
from jax import lax
from jax.experimental import pallas as pl
from jax.experimental.pallas import tpu as pltpu
from jax.sharding import PartitionSpec as P

OFFSETS = (-0.03, -0.088, -0.188)
SPREADS = (0.458, 0.448, 0.45)
EPSILON = 1e-06
BF = jnp.bfloat16
F32 = jnp.float32
DIRS = ((-1, 0), (1, 0), (0, -1), (0, 1), (-1, -1), (-1, 1), (1, -1), (1, 1))
UP, DOWN, LEFT, RIGHT, UL, UR, DL, DR = range(8)
OPP = (1, 0, 3, 2, 7, 6, 5, 4)
STAGES = 8


def roll(x, shift):
    return pltpu.roll(x, shift % 128, 1)


def dot(a, b):
    return jnp.dot(a, b, preferred_element_type=F32)


def lanes(shape):
    return lax.broadcasted_iota(jnp.int32, shape, 1)


def shifted(x, e):
    low = lanes(x.shape) < 64
    if e == 1:
        return jnp.where(low, roll(x, 64), roll(x, 63))
    if e == -1:
        return jnp.where(low, roll(x, 65), roll(x, 64))
    return roll(x, -e // 2)


def kernel(
    img0_hbm, img1_hbm, k1_hbm, k2_hbm, k3_hbm, b1, b2, b3, l1, l2, l3,
    planes, loss,
    img, k1, w2n, k3, kpair, sela, wb1, wb1b, w2t,
    sel, pf, ef, tmp, lw, ew, x1, f1, sl1, pool1, x2, f2, sl2, keep, pool2, x3,
    f3, sl3, d3, x3d, w3t, w3n, dp2, d2, x4, yb, xh, yh, d1, x5, bf, hb, wends, dp1, xe,
    cb1, cb2, cb3, cl1, cl2, cl3, la, lsa, lsb, lsc,
    su0, sd0, se0, seu, sed, ru0, rd0, rl0, rr0, rc0,
    se1, hs1, se2, hs2, su2, sd2, ru2, rd2, se3, hs3, su3, sd3, ru3, rd3, se4, hs4, se5, hs5, ru5, rd5,
    send_sem, recv_sem, wsend, wrecv, lsend, lrecv, in_sem,
):
    n_row, n_col, n_chan = lax.axis_size("row"), lax.axis_size("col"), lax.axis_size("chan")
    i_row, i_col, i_chan = lax.axis_index("row"), lax.axis_index("col"), lax.axis_index("chan")
    tile = i_row * n_chan + i_chan
    n_tile = n_row * n_chan

    def place(step_t, step_c):
        other = tile + step_t
        return {"row": other // n_chan, "chan": other % n_chan, "col": i_col + step_c}

    def exists(step_t, step_c):
        ok = None
        for step, at, count in ((step_t, tile, n_tile), (step_c, i_col, n_col)):
            if step < 0:
                term = at > 0
            elif step > 0:
                term = at < count - 1
            else:
                continue
            ok = term if ok is None else jnp.logical_and(ok, term)
        return ok

    peers = [("chan", i_chan, n_chan, k) for k in range(1, n_chan)]
    peers += [("col", i_col, n_col, k) for k in range(1, n_col)]
    peers += [("row", i_row, n_row, k) for k in range(1, n_row)]
    far = {"row": i_row + 1 - 2 * (i_row % 2), "chan": (i_chan + 2) % n_chan}
    near = {"chan": i_chan + 1 - 2 * (i_chan % 2)}

    barrier = pltpu.get_barrier_semaphore()

    def greets(d):
        if d in (LEFT, RIGHT):
            return None
        ok = exists(*DIRS[d])
        if d == UP:
            ok = jnp.logical_and(ok, i_chan == 0)
        if d == DOWN:
            ok = jnp.logical_and(ok, i_chan == n_chan - 1)
        return ok

    for d in range(8):
        if greets(d) is not None:

            @pl.when(greets(d))
            def _():
                pl.semaphore_signal(barrier, inc=1, device_id=place(*DIRS[d]), device_id_type=pl.DeviceIdType.MESH)

    loads = [
        pltpu.make_async_copy(src, dst, in_sem.at[n])
        for n, (src, dst) in enumerate(
            (
                (img0_hbm, img.at[0]), (img1_hbm, img.at[1]), (k3_hbm, k3), (k1_hbm, k1), (k2_hbm, w2n),
            )
        )
    ]
    for load in loads:
        load.start()

    for axis, at, count, k in peers:
        pl.semaphore_signal(
            barrier, inc=1, device_id={axis: (at + k) % count}, device_id_type=pl.DeviceIdType.MESH
        )

    if n_chan > 1:
        pl.semaphore_signal(barrier, inc=1, device_id=far, device_id_type=pl.DeviceIdType.MESH)

    def barrier_wait():
        total = jnp.int32(len(peers) + (1 if n_chan > 1 else 0))
        for d in range(8):
            if greets(d) is not None:
                total = total + greets(d).astype(jnp.int32)
        pl.semaphore_wait(barrier, total)

    def copy(stage, d, src, dst):
        return pltpu.make_async_remote_copy(
            src_ref=src,
            dst_ref=dst,
            send_sem=send_sem.at[stage, d],
            recv_sem=recv_sem.at[stage, d],
            device_id=place(*DIRS[d]),
            device_id_type=pl.DeviceIdType.MESH,
        )

    def start(stage, plan):
        for d in (UL, UR, DL, DR, LEFT, RIGHT, UP, DOWN):
            src, dst = plan[d]

            @pl.when(exists(*DIRS[d]))
            def _():
                copy(stage, d, src, dst).start()

    def arrive(stage, plan):
        for d, (src, dst) in enumerate(plan):
            back = DIRS[OPP[d]]

            @pl.when(exists(*back))
            def _():
                copy(stage, d, src, dst).wait_recv()

    def drain(stage, plan):
        for d, (src, dst) in enumerate(plan):

            @pl.when(exists(*DIRS[d]))
            def _():
                copy(stage, d, src, dst).wait_send()

    plan0 = [
        (su0, rd0), (sd0, ru0), (se0, rr0), (se0, rl0),
        (seu, rc0.at[3]), (seu, rc0.at[2]), (sed, rc0.at[1]), (sed, rc0.at[0]),
    ]

    def side_plan(up, down, side, hs):
        return [
            up, down, (side, hs.at[1]), (side, hs.at[0]),
            (side, hs.at[5]), (side, hs.at[4]), (side, hs.at[3]), (side, hs.at[2]),
        ]

    plan1 = [
        side_plan(
            (pool1.at[f, pl.ds(2, 2)], pool1.at[f, pl.ds(10, 2)]),
            (pool1.at[f, pl.ds(8, 2)], pool1.at[f, pl.ds(0, 2)]),
            se1.at[f], hs1.at[f],
        )
        for f in range(2)
    ]
    plan2 = [
        side_plan((su2.at[f], rd2.at[f]), (sd2.at[f], ru2.at[f]), se2.at[f], hs2.at[f])
        for f in range(2)
    ]
    plan3 = side_plan((su3, rd3), (sd3, ru3), se3, hs3)
    plan4 = side_plan((d2.at[pl.ds(2, 2)], d2.at[pl.ds(10, 2)]), (d2.at[pl.ds(8, 2)], d2.at[pl.ds(0, 2)]), se4, hs4)
    plan5 = side_plan((d1.at[0], rd5), (d1.at[15], ru5), se5, hs5)

    def blank(plans):
        for d in range(8):

            @pl.when(jnp.logical_not(exists(*DIRS[OPP[d]])))
            def _():
                for plan in plans:
                    dst = plan[d][1]
                    dst[...] = jnp.zeros(dst.shape, dst.dtype)

    lane8 = lanes((8, 128))
    for f in range(2):
        loads[f].wait()
        for c in range(3):
            v = ((img[f, c] - OFFSETS[c]) * (1.0 / SPREADS[c])).astype(BF).astype(F32)
            pf[3 * f + c, 8:72, :] = v
    for c in range(3):
        acc = jnp.zeros((8, 128), F32)
        for f in range(2):
            for y in range(8):
                row = pf[3 * f + c, 8 + 8 * y : 16 + 8 * y, :]
                to = 64 * f + 8 * y
                acc = jnp.where((lane8 >= to) & (lane8 < to + 4), roll(row[:, :128], to), acc)
                acc = jnp.where((lane8 >= to + 4) & (lane8 < to + 8), roll(row[:, 896:], to + 8), acc)
        se0[8 * c : 8 * c + 8, :] = acc
    for buf, edge, at in ((su0, seu, 8), (sd0, sed, 68)):
        tmp[...] = jnp.zeros(tmp.shape, F32)
        for f in range(2):
            for c in range(3):
                tmp[16 * f + 4 * c : 16 * f + 4 * c + 4, :] = pf[3 * f + c, at : at + 4, :]
        v = tmp[...]
        buf[...] = v.astype(BF)
        edge[...] = jnp.where(lanes((32, 128)) < 4, v[:, :128], roll(v[:, 896:], 8)).astype(BF)

    barrier_wait()
    start(0, plan0)

    def eye(size):
        rows = lax.broadcasted_iota(jnp.int32, (size, size), 0)
        return jnp.where(rows == lanes((size, size)), 1.0, 0.0).astype(BF)

    def flip(one, block):
        return lax.dot_general(
            one, block, (((1,), (1,)), ((), ())), preferred_element_type=F32
        ).astype(BF)

    loads[2].wait()
    own = pl.ds(pl.multiple_of(i_chan * 96, 32), 96)
    one = eye(96)
    for at in range(0, 1728, 256):
        size = min(256, 1728 - at)
        w3t[own, at : at + size] = flip(one, k3[at : at + size, :])

    def shard_rows(owner, part):
        count = 96 if part is None else 16
        first = owner * 96 + (0 if part is None else 16 * part)
        return w3t.at[pl.ds(pl.multiple_of(first, 16), count)]

    def shard_copy(kind, part):
        rows = shard_rows((i_chan + 2) % n_chan if kind == 2 else i_chan, part)
        at = (0, 1, 7)[kind] + (part or 0)
        return pltpu.make_async_remote_copy(
            src_ref=rows,
            dst_ref=rows,
            send_sem=wsend.at[at],
            recv_sem=wrecv.at[at],
            device_id=far if kind == 1 else near,
            device_id_type=pl.DeviceIdType.MESH,
        )

    def shard_arrive(kind, part):
        owner = (near["chan"], i_chan + 2, near["chan"] + 2)[kind]
        rows = shard_rows(owner % n_chan, part)
        at = (0, 1, 7)[kind] + (part or 0)
        pltpu.make_async_remote_copy(
            src_ref=rows,
            dst_ref=rows,
            send_sem=wsend.at[at],
            recv_sem=wrecv.at[at],
            device_id=far if kind == 1 else near,
            device_id_type=pl.DeviceIdType.MESH,
        ).wait_recv()

    def shard_send(*parts):
        if n_chan > 1:
            for part in parts:
                shard_copy(1, part).start()

    def shard_pass(*parts):
        if n_chan > 1:
            for part in parts:
                shard_arrive(1, part)
                shard_copy(2, part).start()

    if n_chan > 1:
        shard_copy(0, None).start()
    shard_send(0, 1, 2)

    for src, dst in ((b1, cb1), (b2, cb2), (b3, cb3), (l1, cl1), (l2, cl2), (l3, cl3)):
        dst[...] = jnp.transpose(jnp.broadcast_to(src[...].reshape(1, -1), (128, src.shape[0])))
    la[...] = jnp.zeros(la.shape, F32)

    for px in range(8):
        at = lax.broadcasted_iota(jnp.int32, (1024, 128), 0)
        lane = lanes((1024, 128))
        want = 8 * (2 * (lane % 64) + lane // 64) + px
        sel[:, 128 * px : 128 * px + 128] = jnp.where(at == want, 1.0, 0.0).astype(BF)

    loads[3].wait()
    k1t = flip(eye(64), k1[...])
    cell = lax.broadcasted_iota(jnp.int32, (48, 128), 0)
    base = 48 * (cell % 4) + 16 * (cell // 16) + (cell // 4) % 4
    lane = lanes((48, 128))
    for cy in range(2):
        for cx in range(2):
            for tap in range(9):
                want = base + (192 * (tap % 3 + cx) + 4 * (tap // 3 + cy))
                for j in range(6):
                    sela[48 * tap : 48 * tap + 48, 128 * j : 128 * j + 128] = jnp.where(
                        lane + 128 * j == want, 1.0, 0.0
                    ).astype(BF)
            n = 2 * cy + cx
            wb1[64 * n : 64 * n + 64, :] = dot(k1t, sela[...]).astype(BF)

    loads[4].wait()
    one = eye(192)
    for at in range(0, 1600, 256):
        size = min(256, 1600 - at)
        w2t[:, at : at + size] = flip(one, w2n[at : at + size, :])

    blank([plan0, *plan1, *plan2, plan3, plan4, plan5])
    arrive(0, plan0)
    for buf, at in ((ru0, 4), (rd0, 72)):
        tmp[...] = buf[...].astype(F32)
        for f in range(2):
            for c in range(3):
                pf[3 * f + c, at : at + 4, :] = tmp[16 * f + 4 * c : 16 * f + 4 * c + 4, :]
    for s, (mid, up, down) in enumerate(((rl0, 0, 2), (rr0, 1, 3))):
        for f in range(2):
            for c in range(3):
                v = mid[8 * c : 8 * c + 8, :]
                for y in range(8):
                    ef[s, 3 * f + c, 8 + 8 * y : 16 + 8 * y, :] = roll(v, -64 * f - 8 * y)
        for corner, at in ((up, 4), (down, 72)):
            tmp[:, :128] = rc0[corner].astype(F32)
            for f in range(2):
                for c in range(3):
                    ef[s, 3 * f + c, at : at + 4, :] = tmp[16 * f + 4 * c : 16 * f + 4 * c + 4, :128]

    def pixels(f):
        for r in range(8):
            for c in range(3):
                rows = slice((r * 3 + c) * 16, (r * 3 + c) * 16 + 16)
                lw[rows, :] = pf[3 * f + c, 8 * r + 4 : 8 * r + 20, :].astype(BF)
                for s in range(2):
                    ew[s, rows, :] = ef[s, 3 * f + c, 8 * r + 4 : 8 * r + 20, :]
        for pp in range(4):
            both = dot(lw[...], sel[:, 256 * pp : 256 * pp + 256])
            for px in (2 * pp, 2 * pp + 1):
                x = both[:, 128 * (px % 2) : 128 * (px % 2) + 128]
                if px >= 4:
                    other = shifted(x, -1)
                    other = jnp.where(lanes(x.shape) == 0, roll(ew[0], -px), other)
                    wx = px - 4
                else:
                    other = shifted(x, 1)
                    other = jnp.where(lanes(x.shape) == 127, roll(ew[1], 127 - px), other)
                    wx = 12 + px
                for w, v in ((4 + px, x), (wx, other)):
                    v = v.astype(BF)
                    for r in range(8):
                        x1[r % 4, 48 * w : 48 * w + 48, 128 * (r // 4) : 128 * (r // 4) + 128] = v[48 * r : 48 * r + 48]

    def silu(v):
        sigma = 0.5 * jnp.tanh(0.5 * v) + 0.5
        return v * sigma, sigma

    def layer_one(f):
        def body(i, _):
            out = dot(wb1[...], x1[i])
            for h in range(2):
                acc = None
                for ph in range(4):
                    v = out[64 * ph : 64 * ph + 64, 128 * h : 128 * h + 128] + cb1[...]
                    feat, sigma = silu(v)
                    n = (i + 4 * h) * 4 + ph
                    f1[f, n] = feat
                    if f == 0:
                        sl1[n] = sigma * (1.0 + v * (1.0 - sigma))
                    acc = feat if acc is None else acc + feat
                pool1[f, 2 + i + 4 * h] = (0.25 * acc).astype(BF)
            return 0

        lax.fori_loop(0, 4, body, 0)

    def pack_columns(rows, side):
        size = side.shape[0]
        acc = jnp.zeros((size, 128), F32)
        lane = lanes((size, 128)) % 64
        for g in range(4):
            for r in range(8):
                x = rows(r, slice(size * g, size * g + size)).astype(F32)
                to = 16 * g + r
                acc = jnp.where(lane == to, roll(x, to), acc)
                acc = jnp.where(lane == to + 8, roll(x, to + 8 - 63), acc)
        side[...] = acc.astype(BF)

    def merged(hs):
        size = hs.shape[1]
        lane = lanes((size, 128)) % 64
        slots = [hs[n].astype(F32) for n in range(6)]
        for g in range(4):
            v = roll(slots[1], 2 - 16 * g)
            v = jnp.where(lane < 2, roll(slots[3], -6 - 16 * g), v)
            v = jnp.where(lane >= 10, roll(slots[5], 10 - 16 * g), v)
            v = jnp.where(lane >= 18, roll(slots[0], 10 - 16 * g), v)
            v = jnp.where((lane >= 16) & (lane < 18), roll(slots[2], 2 - 16 * g), v)
            v = jnp.where(lane >= 26, roll(slots[4], 18 - 16 * g), v)
            hb[size * g : size * g + size, :] = v

    def layer_two_operand(f):
        lane = lanes((64, 128))
        merged(hs1.at[f])
        halo = hb[0:64, :]
        for rr in range(12):
            x = pool1[f, rr].astype(F32)
            right = roll(halo, 63 - rr)
            left = roll(halo, -16 - rr)
            cols = (
                jnp.where(lane % 64 == 0, left, shifted(x, -2)),
                jnp.where(lane == 0, roll(left, 64), shifted(x, -1)),
                x,
                jnp.where(lane == 127, roll(right, 64), shifted(x, 1)),
                jnp.where(lane % 64 == 63, right, shifted(x, 2)),
            )
            for e, v in enumerate(cols):
                v = v.astype(BF)
                if rr < 8:
                    x2[320 * rr + 64 * e : 320 * rr + 64 * e + 64, :128] = v
                if rr >= 4:
                    x2[320 * (rr - 4) + 64 * e : 320 * (rr - 4) + 64 * e + 64, 128:] = v

    def layer_two(f):
        low = lanes((64, 128)) < 64
        for i in range(4):
            out = dot(w2t[...], x2[320 * i : 320 * i + 1600, :])
            for h in range(2):
                for k in range(3):
                    rows = slice(64 * k, 64 * k + 64)
                    v = out[rows, 128 * h : 128 * h + 128] + cb2[rows]
                    feat, sigma = silu(v)
                    f2[f, i + 4 * h, rows] = feat
                    if f == 0:
                        sl2[i + 4 * h, rows] = sigma * (1.0 + v * (1.0 - sigma))
                    if i % 2 == 1:
                        both = f2[f, i - 1 + 4 * h, rows] + feat
                        mean = 0.25 * (both + roll(both, 64))
                        if i == 1:
                            keep[h, rows] = mean
                        else:
                            pool2[f, h, rows] = jnp.where(low, keep[h, rows], mean).astype(BF)

    def pack_ends(tiles, side, up, down):
        size = side.shape[0]
        lane = lanes((size, 128))
        acc = jnp.zeros((size, 128), F32)
        for g in range(12):
            for t in range(2):
                x = tiles[t, size * g : size * g + size, :].astype(F32)
                for r in (2 * t, 2 * t + 1):
                    first = 64 * (r % 2)
                    to = 8 * g + r
                    acc = jnp.where(lane == to, roll(x, to - first), acc)
                    acc = jnp.where(lane == to + 4, roll(x, to + 4 - 63 - first), acc)
        side[...] = acc.astype(BF)
        half = up.shape[0]
        for at in range(0, half, 96):
            rows, others = slice(at, at + 96), slice(half + at, half + at + 96)
            low = lanes((96, 128)) < 64
            up[rows] = jnp.where(
                low, tiles[0, rows].astype(F32), roll(tiles[0, others].astype(F32), 64)
            ).astype(BF)
            down[rows] = jnp.where(
                low, roll(tiles[1, rows].astype(F32), 64), tiles[1, others].astype(F32)
            ).astype(BF)

    def merged_ends(hs):
        size = hs.shape[1]
        lane = lanes((size, 128))
        slots = [hs[n].astype(F32) for n in range(6)]
        for g in range(12):
            v = None
            for first, (mid, up, down), skip in ((0, (1, 3, 5), 0), (16, (0, 2, 4), 4)):
                to = first - 8 * g - skip
                w = roll(slots[mid], to + 1)
                w = jnp.where(lane == first, roll(slots[up], to - 3), w)
                w = jnp.where(lane == first + 5, roll(slots[down], to + 5), w)
                w = jnp.where(lane >= 64, roll(slots[mid], to + 64), w)
                w = jnp.where(lane == first + 68, roll(slots[down], to + 68), w)
                v = w if v is None else jnp.where(lane % 64 < 16, v, w)
            hb[size * g : size * g + size, :] = v

    def layer_three_operand(tiles, from_up, from_down, hs, dst):
        channels = tiles.shape[1]
        half = channels // 2
        merged_ends(hs)
        for at in range(0, channels, 96):
            rows = slice(at, at + 96)
            fold = slice(at % half, at % half + 96)
            lane = lanes((96, 128))
            low = lane < 64
            halo = hb[rows, :]
            b = tiles[0, rows].astype(F32)
            d = tiles[1, rows].astype(F32)
            b_swap, d_swap = roll(b, 64), roll(d, 64)
            above, below = from_up[fold].astype(F32), from_down[fold].astype(F32)
            if at < half:
                below = roll(below, 64)
            else:
                above = roll(above, 64)
            a = jnp.where(low, above, b_swap)
            c = jnp.where(low, b_swap, d_swap)
            e = jnp.where(low, d_swap, below)
            for rr, (x, spots) in enumerate(
                ((a, ((0, 0),)), (b, ((1, 0),)), (c, ((0, 1), (2, 0))), (d, ((1, 1),)), (e, ((2, 1),)))
            ):
                left = jnp.where(lane % 64 == 0, roll(halo, -16 - rr), roll(x, 1))
                right = jnp.where(lane % 64 == 63, roll(halo, 63 - rr), roll(x, 127))
                for dx, v in enumerate((left, x, right)):
                    v = v.astype(BF)
                    for dy, spot in spots:
                        base = (dy * 3 + dx) * channels + at
                        dst[base : base + 96, 128 * spot : 128 * spot + 128] = v

    def layer_three(f):
        out = dot(w3t[...], x3[f])
        for h in range(2):
            for k in range(6):
                rows = slice(64 * k, 64 * k + 64)
                v = out[rows, 128 * h : 128 * h + 128] + cb3[rows]
                feat, sigma = silu(v)
                f3[f, h, rows] = feat
                if f == 0:
                    sl3[h, rows] = sigma * (1.0 + v * (1.0 - sigma))

    def local_terms(feats, n, weights, factor, count, finish):
        chunks = weights.shape[0] // 64
        rows = [slice(64 * k, 64 * k + 64) for k in range(chunks)]
        sums = [jnp.zeros((1, 128), F32)] * 2
        for f in range(2):
            for k in range(chunks):
                v = feats[f, n, rows[k]]
                sums[f] = sums[f] + jnp.sum(v * v, axis=0, keepdims=True)
        first, second = lax.rsqrt(sums[0] + EPSILON), lax.rsqrt(sums[1] + EPSILON)
        inner = jnp.zeros((1, 128), F32)
        total = jnp.zeros((1, 128), F32)
        for k in range(chunks):
            v = feats[0, n, rows[k]]
            differ = v * first - feats[1, n, rows[k]] * second
            slope = weights[rows[k]] * differ
            total = total + jnp.sum(slope * differ, axis=0, keepdims=True)
            inner = inner + jnp.sum(v * slope, axis=0, keepdims=True)
        la[0:1, :] = la[0:1, :] + total * (1.0 / count)
        scale = 2.0 * factor * first
        cubed = 2.0 * factor * first * first * first * inner
        for k in range(chunks):
            v = feats[0, n, rows[k]]
            slope = weights[rows[k]] * (v * first - feats[1, n, rows[k]] * second)
            finish(k, rows[k], scale * slope - v * cubed)

    for f in range(2):
        pixels(f)
        layer_one(f)
        pack_columns(lambda r, rows: pool1[f, 2 + r, rows], se1.at[f])
        start(1 + f, plan1[f])
        shard_send(*((3, 4), (5,))[f])
    kpair[...] = jnp.zeros(kpair.shape, BF)
    half = k1[...].astype(F32)
    both = jnp.concatenate([half, half], axis=1)
    low = lanes((432, 128)) < 64
    kpair[0:432, :] = jnp.where(low, both, 0.0).astype(BF)
    kpair[512:944, :] = jnp.where(low, 0.0, both).astype(BF)
    spot = lax.broadcasted_iota(jnp.int32, (24, 128), 0)
    lane = lanes((24, 128))
    in_low = (spot // 4) % 2 == 0
    within = 16 * (spot // 8) + 4 * (spot % 4)
    for wcy in range(4):
        for pair in range(2):
            for px in range(8):
                cx, b = px // 4, px % 4
                for side in range(2):
                    dx = 2 - (2 * pair + side) + cx
                    for j in range(4):
                        hit = jnp.zeros((24, 128), F32)
                        if 0 <= dx <= 2:
                            for cy in range(2):
                                dy = 2 - wcy + cy
                                first = (dy * 3 + dx) * 48
                                if 0 <= dy <= 2 and first < 128 * j + 128 and first + 48 > 128 * j:
                                    match = lane + (128 * j - first - b) == within
                                    keep_row = in_low if cy == 0 else jnp.logical_not(in_low)
                                    hit = jnp.where(match & keep_row, 1.0, hit)
                        bf[24 * px : 24 * px + 24, 512 * side + 128 * j : 512 * side + 128 * j + 128] = hit
            out = dot(bf[...].astype(BF), kpair[...])
            at = 256 * wcy + 128 * pair
            wb1b[:, at : at + 128] = out.astype(BF)

    for side in range(2):
        at = 96 * side
        wends[side] = jnp.concatenate(
            [wb1b[at : at + 96, 256 * w + 192 * side : 256 * w + 192 * side + 64].astype(F32) for w in range(4)], axis=1
        ).astype(BF)

    for f in range(2):
        shard_pass(2 * f, 2 * f + 1)
        arrive(1 + f, plan1[f])
        layer_two_operand(f)
        layer_two(f)
        pack_ends(pool2.at[f], se2.at[f], su2.at[f], sd2.at[f])
        start(3 + f, plan2[f])
    shard_pass(4, 5)
    pixel_count = 64 * n_tile * 1024 * n_col

    def terms_two(n, _):
        def finish_two(k, rows, dfeat):
            f2[0, n, rows] = dfeat

        local_terms(f2, n, cl2, 64.0, pixel_count // 64, finish_two)
        return 0

    lax.fori_loop(0, 8, terms_two, 0)

    def terms_one(n, _):
        def finish_one(k, rows, dfeat):
            f1[0, n, rows] = dfeat

        local_terms(f1, n, cl1, 16.0, pixel_count // 16, finish_one)
        return 0

    lax.fori_loop(0, 32, terms_one, 0)

    if n_chan > 1:
        shard_arrive(0, None)
        for part in range(6):
            shard_arrive(2, part)
    for f in range(2):
        arrive(3 + f, plan2[f])
        layer_three_operand(pool2.at[f], ru2.at[f], rd2.at[f], hs2.at[f], x3.at[f])
        layer_three(f)

    def loss_copy(axis, k):
        which = ("col", "chan", "row").index(axis)
        slots = (lsa, lsb, lsc)[which]
        at, count = ((i_col, n_col), (i_chan, n_chan), (i_row, n_row))[which]
        return pltpu.make_async_remote_copy(
            src_ref=la,
            dst_ref=slots.at[k - 1],
            send_sem=lsend.at[which, k - 1],
            recv_sem=lrecv.at[which, k - 1],
            device_id={axis: (at + k) % count},
            device_id_type=pl.DeviceIdType.MESH,
        )

    def loss_start(axis, count):
        for k in range(1, count):
            loss_copy(axis, k).start()

    def loss_finish(axis, count, slots):
        for k in range(1, count):
            loss_copy(axis, k).wait()
        total = la[...]
        for k in range(1, count):
            total = total + slots[k - 1]
        la[...] = total

    for h in range(2):

        def finish_three(k, rows, dfeat):
            d3[h, rows] = (dfeat * sl3[h, rows]).astype(BF)

        local_terms(f3, h, cl3, 256.0, pixel_count // 256, finish_three)
    pack_ends(d3, se3, su3, sd3)
    start(5, plan3)
    loss_start("col", n_col)


    one = eye(128)
    for at in range(0, 1728, 128):
        size = min(128, 1728 - at)
        w3n[at : at + size, :] = flip(one[:size, :size], w3t[:, at : at + size])

    drain(0, plan0)
    for f in range(2):
        drain(1 + f, plan1[f])
        drain(3 + f, plan2[f])
    if n_chan > 1:
        shard_copy(0, None).wait_send()
        for part in range(6):
            shard_copy(1, part).wait_send()
            shard_copy(2, part).wait_send()
    arrive(5, plan3)
    loss_finish("col", n_col, lsa)
    loss_start("chan", n_chan)
    layer_three_operand(d3, ru3, rd3, hs3, x3d)
    acc = None
    for tap in range(9):
        part = dot(w3n[192 * (8 - tap) : 192 * (8 - tap) + 192, :], x3d[384 * tap : 384 * tap + 384, :])
        acc = part if acc is None else acc + part
    dp2[...] = acc

    for r in range(8):
        for k in range(3):
            rows = slice(64 * k, 64 * k + 64)
            t = dp2[rows, 128 * (r // 4) : 128 * (r // 4) + 128]
            low = lanes((64, 128)) < 64
            swap = roll(t, 64)
            wide = jnp.where(low, t, swap) if (r // 2) % 2 == 0 else jnp.where(low, swap, t)
            d2[2 + r, rows] = ((f2[0, r, rows] + 0.25 * wide) * sl2[r, rows]).astype(BF)
    pack_columns(lambda r, rows: d2[2 + r, rows], se4)
    start(6, plan4)

    zero = jnp.zeros((192, 128), BF)
    for rr in range(12):
        v = d2[rr] if 2 <= rr < 10 else zero
        if rr < 8:
            x4[192 * rr : 192 * rr + 192, :128] = v
        if rr >= 4:
            x4[192 * (rr - 4) : 192 * (rr - 4) + 192, 128:] = v
    lane = lanes((64, 128))

    def joined(pick):
        total = pick(0)
        for e, edge in ((1, lane == 127), (-1, lane == 0), (2, lane % 64 == 63), (-2, lane % 64 == 0)):
            total = total + jnp.where(edge, 0.0, shifted(pick(e), e))
        return total

    def taps(operand, pairs):
        acc = None
        for dy, block in pairs:
            part = dot(w2n[320 * (4 - dy) : 320 * (4 - dy) + 320, :], operand(block))
            acc = part if acc is None else acc + part
        return acc

    for i in range(4):
        yb[...] = taps(lambda n: x4[192 * n : 192 * n + 192, :], [(dy, i + dy) for dy in range(5)])
        for h in range(2):
            dp1[i + 4 * h] = joined(
                lambda e: yb[64 * (2 - e) : 64 * (2 - e) + 64, 128 * h : 128 * h + 128]
            )

    drain(5, plan3)
    arrive(6, plan4)
    loss_finish("chan", n_chan, lsb)
    loss_start("row", n_row)
    merged(hs4)
    for at in range(0, 192, 64):
        halo = hb[at : at + 64, :]
        for dy in range(5):
            xh[192 * dy + at : 192 * dy + at + 64, :] = roll(halo, -dy).astype(BF)
    yh[...] = taps(lambda n: xh[192 * n : 192 * n + 192, :], [(dy, dy) for dy in range(5)])
    for n, v in enumerate((d2[0], d2[1], d2[1], zero, d2[10], d2[11], zero, d2[10])):
        xe[192 * (n // 2) : 192 * (n // 2) + 192, 128 * (n % 2) : 128 * (n % 2) + 128] = v
    for first, pairs in ((0, ((0, 0), (1, 1))), (6, ((4, 2), (3, 3)))):
        yb[...] = taps(lambda n: xe[192 * n : 192 * n + 192, :], pairs)
        for h in range(2):
            dp1[first + h] = dp1[first + h] + joined(
                lambda e: yb[64 * (2 - e) : 64 * (2 - e) + 64, 128 * h : 128 * h + 128]
            )
    for r in range(8):

        def side(e):
            return yh[64 * (2 - e) : 64 * (2 - e) + 64, :]

        total = dp1[r]
        total = total + jnp.where(lane == 127, roll(side(1), 127 - r), 0.0)
        total = total + jnp.where(lane % 64 == 63, roll(side(2), 63 - r), 0.0)
        total = total + jnp.where(lane == 0, roll(side(-1), -80 - r), 0.0)
        total = total + jnp.where(lane % 64 == 0, roll(side(-2), -16 - r), 0.0)
        total = 0.25 * total
        for py in range(2):
            for px in range(2):
                n = 4 * r + 2 * py + px
                d1[2 * r + py, 64 * px : 64 * px + 64] = ((f1[0, n] + total) * sl1[n]).astype(BF)

    lane16 = lanes((16, 128))
    acc = jnp.zeros((16, 128), F32)
    for g in range(4):
        for cr in range(16):
            to = 32 * g + cr
            zero, one = d1[cr, 16 * g : 16 * g + 16], d1[cr, 64 + 16 * g : 80 + 16 * g]
            acc = jnp.where(lane16 == to, roll(zero.astype(F32), to), acc)
            acc = jnp.where(lane16 == to + 16, roll(one.astype(F32), to + 16 - 127), acc)
    se5[...] = acc.astype(BF)
    start(7, plan5)

    def beside(src):
        zero, one = src[:64], src[64:]
        before = jnp.where(lane == 0, 0.0, shifted(one.astype(F32), -1)).astype(BF)
        after = jnp.where(lane == 127, 0.0, shifted(zero.astype(F32), 1)).astype(BF)
        return before, zero, one, after

    for n in range(18):
        if n in (0, 17):
            cols = (jnp.zeros((64, 128), BF),) * 4
        else:
            cols = beside(d1.at[n - 1])
        for g, v in enumerate(cols):
            if n < 10:
                x5[256 * n + 64 * g : 256 * n + 64 * g + 64, :128] = v
            if n >= 8:
                x5[256 * (n - 8) + 64 * g : 256 * (n - 8) + 64 * g + 64, 128:] = v

    def spots(r):
        for px in range(8):
            for c in range(3):
                yield px * 24 + c * 8, 64 * c + 8 * r, 128 * px

    for i in range(4):
        out = dot(wb1b[...], x5[512 * i : 512 * i + 1024, :])
        for h in range(2):
            for at, row, col in spots(i + 4 * h):
                bf[row : row + 8, col : col + 128] = out[at : at + 8, 128 * h : 128 * h + 128]

    drain(6, plan4)
    arrive(7, plan5)
    slots = [hs5[n].astype(F32) for n in range(6)]
    for g in range(4):
        v = roll(slots[1], 1 - 32 * g)
        v = jnp.where(lane16 == 0, roll(slots[3], -15 - 32 * g), v)
        v = jnp.where(lane16 == 17, roll(slots[5], 17 - 32 * g), v)
        w = roll(slots[0], 17 - 32 * g)
        w = jnp.where(lane16 == 32, roll(slots[2], 1 - 32 * g), w)
        w = jnp.where(lane16 == 49, roll(slots[4], 33 - 32 * g), w)
        hb[16 * g : 16 * g + 16, :] = jnp.where(lane16 < 32, v, w)
    for r, src, at in ((0, ru5, 0), (7, rd5, 768)):
        out = dot(wb1b[:, at : at + 256], jnp.concatenate(beside(src), axis=0))
        for at, row, col in spots(r):
            bf[row : row + 8, col : col + 128] = bf[row : row + 8, col : col + 128] + out[at : at + 8]
    halo = hb[0:64, :]
    stack = jnp.concatenate([roll(halo, -w).astype(BF) for w in range(4)], axis=0)
    for side, (first, edge) in enumerate(((32, 0), (0, 127))):
        yh[0:96, :] = dot(wends[side], stack)
        for r in range(8):
            for at, row, col in spots(r):
                if at // 96 == side:
                    part = roll(yh[at - 96 * side : at - 96 * side + 8, :], edge - first - 2 * r)
                    bf[row : row + 8, col : col + 128] = bf[row : row + 8, col : col + 128] + jnp.where(
                        lane8 == edge, part, 0.0
                    )
    loss_finish("row", n_row, lsc)
    loss[...] = jnp.sum(la[0:1, :], axis=1, keepdims=True)
    planes[...] = bf[...].astype(BF)

    drain(7, plan5)


def to_pixels(planes, grad):
    at = lax.broadcasted_iota(jnp.int32, (128, 1024), 0)
    want = 8 * (2 * (at % 64) + at // 64) - lanes((128, 1024))
    out = None
    for k in range(4):
        spread = jnp.concatenate(
            [jnp.where(want == -(2 * k + j), 1.0, 0.0).astype(BF) for j in range(2)], axis=0
        )
        part = dot(planes[:, 256 * k : 256 * k + 256], spread)
        out = part if out is None else out + part
    for c in range(3):
        grad[c] = out[64 * c : 64 * c + 64] * (1.0 / SPREADS[c])


def local(
    image_gen, image_ref, kernel_one, bias_one, kernel_two, bias_two, kernel_three, bias_three,
    lin_first, lin_second, lin_third,
):
    n_row, n_col, n_chan = lax.axis_size("row"), lax.axis_size("col"), lax.axis_size("chan")
    rows = (bias_one, bias_two, bias_three, lin_first, lin_second, lin_third)
    V = pltpu.VMEM
    scratch = dict(
        img=V((2, 3, 64, 1024), F32), k1=V((432, 64), BF), w2n=V((1600, 192), BF), k3=V((1728, 96), BF),
        kpair=V((1024, 128), BF), sela=V((432, 768), BF), wb1=V((256, 768), BF), wb1b=V((192, 1024), BF),
        w2t=V((192, 1600), BF),
        sel=V((1024, 1024), BF), pf=V((6, 80, 1024), F32), ef=V((2, 6, 80, 128), F32),
        tmp=V((32, 1024), F32), lw=V((384, 1024), BF), ew=V((2, 384, 128), F32),
        x1=V((4, 768, 256), BF), f1=V((2, 32, 64, 128), F32), sl1=V((32, 64, 128), F32),
        pool1=V((2, 12, 64, 128), BF), x2=V((2560, 256), BF), f2=V((2, 8, 192, 128), F32),
        sl2=V((8, 192, 128), F32), keep=V((2, 192, 128), F32), pool2=V((2, 2, 192, 128), BF),
        x3=V((2, 1728, 256), BF), f3=V((2, 2, 384, 128), F32), sl3=V((2, 384, 128), F32),
        d3=V((2, 384, 128), BF), x3d=V((3456, 256), BF), w3t=V((384, 1728), BF), w3n=V((1728, 384), BF),
        dp2=V((192, 256), F32), d2=V((12, 192, 128), BF), x4=V((1536, 256), BF), yb=V((320, 256), F32),
        xh=V((960, 128), BF), yh=V((320, 128), F32), d1=V((16, 128, 128), BF), x5=V((2560, 256), BF),
        bf=V((192, 1024), F32), hb=V((384, 128), F32), wends=V((2, 96, 256), BF), dp1=V((8, 64, 128), F32),
        xe=V((768, 256), BF), cb1=V((64, 128), F32), cb2=V((192, 128), F32), cb3=V((384, 128), F32),
        cl1=V((64, 128), F32), cl2=V((192, 128), F32), cl3=V((384, 128), F32), la=V((8, 128), F32),
        lsa=V((max(n_col - 1, 1), 8, 128), F32), lsb=V((max(n_chan - 1, 1), 8, 128), F32),
        lsc=V((max(n_row - 1, 1), 8, 128), F32),
        su0=V((32, 1024), BF), sd0=V((32, 1024), BF), se0=V((24, 128), F32), seu=V((32, 128), BF),
        sed=V((32, 128), BF), ru0=V((32, 1024), BF), rd0=V((32, 1024), BF), rl0=V((24, 128), F32),
        rr0=V((24, 128), F32), rc0=V((4, 32, 128), BF),
        se1=V((2, 16, 128), BF), hs1=V((2, 6, 16, 128), BF), se2=V((2, 16, 128), BF),
        hs2=V((2, 6, 16, 128), BF), su2=V((2, 96, 128), BF), sd2=V((2, 96, 128), BF),
        ru2=V((2, 96, 128), BF), rd2=V((2, 96, 128), BF),
        se3=V((32, 128), BF), hs3=V((6, 32, 128), BF), su3=V((192, 128), BF), sd3=V((192, 128), BF),
        ru3=V((192, 128), BF), rd3=V((192, 128), BF),
        se4=V((48, 128), BF), hs4=V((6, 48, 128), BF), se5=V((16, 128), BF), hs5=V((6, 16, 128), BF),
        ru5=V((128, 128), BF), rd5=V((128, 128), BF),
        send_sem=pltpu.SemaphoreType.DMA((STAGES, 8)), recv_sem=pltpu.SemaphoreType.DMA((STAGES, 8)),
        wsend=pltpu.SemaphoreType.DMA((13,)), wrecv=pltpu.SemaphoreType.DMA((13,)),
        lsend=pltpu.SemaphoreType.DMA((3, 8)), lrecv=pltpu.SemaphoreType.DMA((3, 8)),
        in_sem=pltpu.SemaphoreType.DMA((5,)),
    )
    vmem = pl.BlockSpec(memory_space=pltpu.VMEM)
    planes, loss = pl.pallas_call(
        kernel,
        out_shape=(
            jax.ShapeDtypeStruct((192, 1024), BF),
            jax.ShapeDtypeStruct((1, 1), F32),
        ),
        in_specs=[pl.BlockSpec(memory_space=pl.ANY)] * 5 + [vmem] * 6,
        out_specs=(vmem, vmem),
        scratch_shapes=list(scratch.values()),
        compiler_params=pltpu.CompilerParams(
            collective_id=0, has_side_effects=True, vmem_limit_bytes=62 * 1024 * 1024
        ),
        name="whole",
    )(
        image_gen, image_ref, kernel_one.reshape(432, 64), kernel_two.reshape(1600, 192),
        kernel_three.reshape(1728, 96), *rows,
    )
    grad = pl.pallas_call(
        to_pixels,
        out_shape=jax.ShapeDtypeStruct(image_gen.shape, F32),
        in_specs=[vmem],
        out_specs=vmem,
        name="pixels",
    )(planes)
    return (grad, loss.reshape(()))


def solution(mesh):
    rows = ("row", "chan")
    in_specs = (
        P(None, rows, "col"), P(None, rows, "col"), P(), P(), P(), P(),
        P(None, None, None, "chan"), P(), P(), P(), P(),
    )
    out_specs = (P(None, rows, "col"), P())
    return jax.shard_map(local, mesh=mesh, in_specs=in_specs, out_specs=out_specs, check_vma=False)
```
